512 devices in a mesh: blk: 32 (over z, core), shard: 16 (over x, y).
Axes of the slice: x: 4, y: 4, z: 16, core: 2. Of those that a mesh axis runs over, the one named last changes fastest.
Arguments:
- seed_field: float32 [32, 2, 32, 32, 1024], P('blk', None, 'shard'), may hold values from -5 to 5
- segment_order: int32 [32], P('blk'), may hold values from 0 to 31, each once
- seg_disp: float32 [32], replicated, may hold values from -1 to 1
- seg_kerr: float32 [32], replicated, may hold values from 0.5 to 2
- seg_gain: float32 [32], replicated, may hold values from 1 to 4
- seg_sat: float32 [32], replicated, may hold values from 1 to 4
Outputs:
- out_field: float32 [32, 2, 32, 32, 1024], P('blk', None, 'shard')
The draws below stay inside these ranges and needn't reach their ends.
Inputs may be any that keep to these rules, and one draw needn't show every extreme that they name: segment_order[b] is the kind of the segment at cycle position b; each of the 32 kinds appears once.
All inputs are finite; a program needn't handle non-finite values.
Results may differ from the reference program's by a relative error of at most 0.0006.
Values sent between devices are 32-bit elements; how exact they have to be, the bound alone decides.
No kernel may reach another device: no remote copies, remote signals or barrier semaphores. Data moves between devices by JAX's collectives and lax.ppermute only.
A program may use at most 64 MiB of HBM per device.

```python
import math
import jax
import jax.numpy as jnp
from jax import lax

NX = 32
NY = 32
NT = 1024
KRYLOV = 8
TRAJ = 32


def draw_seed_field(key, part):
    shape_all = (TRAJ, 2, NX, NY, NT)
    ramp = jnp.arange(NX, dtype=jnp.float32) / (NX - 1)
    noise = jax.random.truncated_normal(key, -4.0, 4.0, shape_all, jnp.float32)
    profile = jnp.sqrt(0.5 + ramp)
    return noise * profile[None, None, :, None, None]


def setup_inputs(seed: int = 0) -> dict:
    key_of = jax.random.split(jax.random.key(seed), 7)
    seed_field = draw_seed_field(jax.random.fold_in(key_of[6], 71), 0)
    segment_order = jax.random.permutation(key_of[1], TRAJ).astype(jnp.int32)
    seg_disp = jnp.clip(jax.random.uniform(key_of[2], (TRAJ,), jnp.float32, -1.0, 1.0), -1.0, 1.0)
    seg_kerr = jnp.clip(jnp.exp(jax.random.uniform(key_of[3], (TRAJ,), jnp.float32, math.log(0.5), math.log(2.0))), 0.5, 2.0)
    seg_gain = jnp.clip(jnp.exp(jax.random.uniform(key_of[4], (TRAJ,), jnp.float32, math.log(1.0), math.log(4.0))), 1.0, 4.0)
    seg_sat = jnp.clip(jnp.exp(jax.random.uniform(key_of[5], (TRAJ,), jnp.float32, math.log(1.0), math.log(4.0))), 1.0, 4.0)
    return {"seed_field": seed_field, "segment_order": segment_order, "seg_disp": seg_disp, "seg_kerr": seg_kerr, "seg_gain": seg_gain, "seg_sat": seg_sat}


epsilon = 1e-06
step_length = 2.5
grin_depth = 1.5
squarings = 8
taylor_terms = 10
gain_width = 0.25
loss_rate = 0.5
disp_scale = 60.0
raman_share = 0.18
raman_freq = 0.05
raman_damp = 0.035

def potential_table(x_count, x_total, x_offset, y_count):
    x_cells = (x_offset + jnp.arange(x_count, dtype=jnp.int32)).astype(jnp.float32)
    y_cells = jnp.arange(y_count, dtype=jnp.int32).astype(jnp.float32)
    x_norm = (x_cells - (x_total - 1) / 2.0) / (x_total / 2.0)
    y_norm = (y_cells - (y_count - 1) / 2.0) / (y_count / 2.0)
    return grin_depth * (x_norm[:, None] * x_norm[:, None] + y_norm[None, :] * y_norm[None, :])

def stencil(padded, vector, potential):
    beside = padded[:, 2:, 1:-1] + padded[:, :-2, 1:-1] + padded[:, 1:-1, 2:] + padded[:, 1:-1, :-2]
    return 0.5 * beside - potential * vector

def krylov_exp(diagonals, couplings):
    basis_count = len(diagonals)
    coupled = jnp.stack(couplings)
    tridiag = jnp.diag(jnp.stack(diagonals)) + jnp.diag(coupled, 1) + jnp.diag(coupled, -1)
    scaled = tridiag * (step_length / 2.0 ** squarings)
    zero_block = jnp.zeros_like(scaled)
    generator = jnp.concatenate([jnp.concatenate([zero_block, -scaled], axis=1), jnp.concatenate([scaled, zero_block], axis=1)], axis=0)
    unit_matrix = jnp.eye(2 * basis_count, dtype=jnp.float32)
    power_term = unit_matrix
    running = unit_matrix
    for order_k in range(1, taylor_terms + 1):
        power_term = jnp.dot(power_term, generator, precision=lax.Precision.HIGHEST) / order_k
        running = running + power_term
    for repeat in range(squarings):
        running = jnp.dot(running, running, precision=lax.Precision.HIGHEST)
    return (running[:basis_count, 0], running[basis_count:, 0])

def assemble(vectors, real_coef, imag_coef):
    real_part = real_coef[0] * vectors[0][0] - imag_coef[0] * vectors[0][1]
    imag_part = real_coef[0] * vectors[0][1] + imag_coef[0] * vectors[0][0]
    for position in range(1, len(vectors)):
        real_part = real_part + real_coef[position] * vectors[position][0] - imag_coef[position] * vectors[position][1]
        imag_part = imag_part + real_coef[position] * vectors[position][1] + imag_coef[position] * vectors[position][0]
    return jnp.stack([real_part, imag_part])

def frequency_tables(freq_index, n_time, gain_now, dispersion):
    signed = jnp.where(freq_index >= n_time // 2, freq_index - n_time, freq_index)
    freq_norm = signed.astype(jnp.float32) / (n_time / 2.0)
    relative = freq_norm / gain_width
    amplitude = jnp.exp(0.5 * gain_now / (1.0 + relative * relative) - loss_rate)
    angle_k = disp_scale * dispersion * freq_norm * freq_norm
    resonance = raman_freq * raman_freq
    real_den = resonance - freq_norm * freq_norm
    imag_den = raman_damp * freq_norm
    magnitude = real_den * real_den + imag_den * imag_den
    return (amplitude * jnp.cos(angle_k), amplitude * jnp.sin(angle_k), resonance * real_den / magnitude, resonance * imag_den / magnitude)

def lanczos(incoming, energy, operate):
    scale_zero = jnp.sqrt(energy + epsilon)
    vectors = [incoming / scale_zero]
    diagonals = []
    couplings = []
    for lanczos_step in range(KRYLOV):
        current = vectors[lanczos_step]
        image = operate(current)
        if lanczos_step > 0:
            image = image - couplings[lanczos_step - 1] * vectors[lanczos_step - 1]
        diagonal_now = jnp.sum(current * image)
        diagonals.append(diagonal_now)
        if lanczos_step + 1 < KRYLOV:
            image = image - diagonal_now * current
            coupling = jnp.sqrt(jnp.sum(image * image) + epsilon)
            couplings.append(coupling)
            vectors.append(image / coupling)
    real_coef, imag_coef = krylov_exp(diagonals, couplings)
    return scale_zero * assemble(vectors, real_coef, imag_coef)

def propagate(trajectory, segment_kind, seg_disp, seg_kerr, seg_gain, seg_sat):
    n_x = trajectory.shape[1]
    n_y = trajectory.shape[2]
    n_time = trajectory.shape[3]
    dispersion = seg_disp[segment_kind]
    kerr_coef = seg_kerr[segment_kind]
    gain_peak = seg_gain[segment_kind]
    saturation = seg_sat[segment_kind]
    energy = jnp.sum(trajectory * trajectory)
    potential = potential_table(n_x, n_x, 0, n_y)[:, :, None]

    def operate(vector):
        padded = jnp.pad(vector, ((0, 0), (1, 1), (1, 1), (0, 0)))
        return stencil(padded, vector, potential)
    linear = lanczos(trajectory, energy, operate)
    gain_now = gain_peak / (1.0 + energy / (n_x * n_y * n_time) / saturation)
    freq_index = jnp.arange(n_time, dtype=jnp.int32)
    gain_real, gain_imag, raman_real, raman_imag = frequency_tables(freq_index, n_time, gain_now, dispersion)
    spectrum = jnp.fft.fft(lax.complex(linear[0], linear[1]), axis=-1)
    dispersed = jnp.fft.ifft(spectrum * lax.complex(gain_real, gain_imag), axis=-1)
    disp_real = jnp.real(dispersed)
    disp_imag = jnp.imag(dispersed)
    intensity = disp_real * disp_real + disp_imag * disp_imag
    delayed = jnp.real(jnp.fft.ifft(jnp.fft.fft(intensity, axis=-1) * lax.complex(raman_real, raman_imag), axis=-1))
    rotation = kerr_coef * ((1.0 - raman_share) * intensity + raman_share * delayed)
    cosine_r = jnp.cos(rotation)
    sine_r = jnp.sin(rotation)
    return jnp.stack([disp_real * cosine_r - disp_imag * sine_r, disp_real * sine_r + disp_imag * cosine_r])

def reference(seed_field, segment_order, seg_disp, seg_kerr, seg_gain, seg_sat):

    def per_trajectory(paired):
        return propagate(paired[0], paired[1], seg_disp, seg_kerr, seg_gain, seg_sat)
    processed = lax.map(per_trajectory, (seed_field, segment_order))
    return jnp.roll(processed, 1, axis=0)
```

```python
import functools

import jax
import jax.numpy as jnp
import numpy as np
from jax import lax
from jax.experimental import pallas as pl
from jax.experimental.pallas import tpu as pltpu
from jax.sharding import PartitionSpec as P

KRYLOV = 8
NS = 16
NG = 32
NT = 1024
NK = 8
NB = 128

epsilon = 1e-06
step_length = 2.5
grin_depth = 1.5
squarings = 8
taylor_terms = 10
gain_width = 0.25
loss_rate = 0.5
disp_scale = 60.0
raman_share = 0.18
raman_freq = 0.05
raman_damp = 0.035

F32 = jnp.float32
HIGHEST = lax.Precision.HIGHEST


@functools.cache
def tables():
    cell = (np.arange(NG) - (NG - 1) / 2.0) / (NG / 2.0)
    line = np.diag(-grin_depth * cell * cell)
    line = line + 0.5 * (np.eye(NG, k=1) + np.eye(NG, k=-1))
    values, q = np.linalg.eigh(line)

    to_ymode = np.zeros((NS, 2, 2, 2, 2, 2, NG))
    to_xmode = np.zeros((2, 2, NG, NS, 2, 2, 2))
    for part in range(2):
        for side in range(2):
            for jj in range(2):
                to_ymode[:, part, jj, side, part, side, :] = q[:, jj::2].T
                to_xmode[part, jj, :, :, part, jj, side] = q[side::2, :].T
    to_ymode = to_ymode.reshape(128, 128)
    to_xmode = to_xmode.reshape(128, 128)

    pair = values.reshape(NS, 2)
    lam = pair[:, None, :, None] + values[None, None, None, :] + np.zeros((1, 2, 1, 1))
    lam_all = lam.reshape(NS, 128)
    lam_own = np.broadcast_to(lam_all[:, :64, None], (NS, 64, 128))

    inner = np.arange(NB)
    angle = 2.0 * np.pi * ((inner[:, None] * inner[None, :]) % NB) / NB
    c, s = np.cos(angle), np.sin(angle)
    forward = np.block([[c, -s], [s, c]])
    backward = np.block([[c, s], [-s, c]])
    turn = 2.0 * np.pi * (np.arange(NK)[:, None] * inner[None, :]) / NT
    tw_cos, tw_sin = np.cos(turn), np.sin(turn)

    freq = np.arange(NK)[:, None] + NK * inner[None, :]
    signed = np.where(freq >= NT // 2, freq - NT, freq)
    w = signed / (NT / 2.0)
    resonance = raman_freq * raman_freq
    raman = resonance / (resonance - w * w - 1j * raman_damp * w)
    ram_re = raman.real / NT
    ram_im = np.where(signed == -(NT // 2), 0.0, raman.imag) / NT

    f32 = lambda a: np.ascontiguousarray(a, dtype=np.float32)
    return dict(
        to_ymode=f32(to_ymode),
        from_ymode=f32(to_ymode.T),
        to_xmode=f32(to_xmode),
        from_xmode=f32(to_xmode.T),
        lam_all=f32(lam_all),
        lam_own=f32(lam_own),
        forward=f32(forward),
        backward=f32(backward),
        twiddle=f32(np.stack([tw_cos, tw_sin])),
        w=f32(w),
        raman=f32(np.stack([ram_re, ram_im])),
    )


def mm(a, b):
    return jnp.dot(a, b, precision=HIGHEST, preferred_element_type=F32)


def fourier8(re, im, sign):
    def four(r, i):
        pr, pi = r[0] + r[2], i[0] + i[2]
        mr, mi = r[0] - r[2], i[0] - i[2]
        qr, qi = r[1] + r[3], i[1] + i[3]
        nr, ni = r[1] - r[3], i[1] - i[3]
        tr, ti = (-ni, nr) if sign > 0 else (ni, -nr)
        return (
            [pr + qr, mr + tr, pr - qr, mr - tr],
            [pi + qi, mi + ti, pi - qi, mi - ti],
        )

    er, ei = four(re[0::2], im[0::2])
    orr, oi = four(re[1::2], im[1::2])
    h = np.float32(np.sqrt(0.5))
    if sign > 0:
        w1 = ((orr[1] - oi[1]) * h, (orr[1] + oi[1]) * h)
        w2 = (-oi[2], orr[2])
        w3 = (-(orr[3] + oi[3]) * h, (orr[3] - oi[3]) * h)
    else:
        w1 = ((orr[1] + oi[1]) * h, (oi[1] - orr[1]) * h)
        w2 = (oi[2], -orr[2])
        w3 = ((oi[3] - orr[3]) * h, -(orr[3] + oi[3]) * h)
    tr = [orr[0], w1[0], w2[0], w3[0]]
    ti = [oi[0], w1[1], w2[1], w3[1]]
    out_r = [er[k] + tr[k] for k in range(4)] + [er[k] - tr[k] for k in range(4)]
    out_i = [ei[k] + ti[k] for k in range(4)] + [ei[k] - ti[k] for k in range(4)]
    return out_r, out_i


def outer_forward(load, rows, tw_ref, dest):
    for r0 in range(0, rows, 8):
        re = [load(0, r0, a) for a in range(NK)]
        im = [load(1, r0, a) for a in range(NK)]
        re, im = fourier8(re, im, -1)
        for k in range(NK):
            if k:
                c, s = tw_ref[0, k : k + 1, :], tw_ref[1, k : k + 1, :]
                re[k], im[k] = re[k] * c + im[k] * s, im[k] * c - re[k] * s
            dest[k * rows + r0 : k * rows + r0 + 8, 0:NB] = re[k]
            dest[k * rows + r0 : k * rows + r0 + 8, NB : 2 * NB] = im[k]


def outer_backward(src, rows, tw_ref, store):
    for r0 in range(0, rows, 8):
        re, im = [], []
        for k in range(NK):
            a = src[k * rows + r0 : k * rows + r0 + 8, 0:NB]
            b = src[k * rows + r0 : k * rows + r0 + 8, NB : 2 * NB]
            if k:
                c, s = tw_ref[0, k : k + 1, :], tw_ref[1, k : k + 1, :]
                a, b = a * c - b * s, a * s + b * c
            re.append(a)
            im.append(b)
        re, im = fourier8(re, im, 1)
        for a in range(NK):
            store(r0, a, re[a], im[a])


def filter_spectrum(spec, rows, factor_re, factor_im):
    for k in range(NK):
        fr, fi = factor_re[k : k + 1, :], factor_im[k : k + 1, :]
        lo, hi = k * rows, (k + 1) * rows
        a, b = spec[lo:hi, 0:NB], spec[lo:hi, NB : 2 * NB]
        spec[lo:hi, 0:NB] = a * fr - b * fi
        spec[lo:hi, NB : 2 * NB] = a * fi + b * fr


def ymode_kernel(seed_ref, mat_ref, out_ref):
    total = jnp.zeros((8, 128), F32)
    for c in range(NK):
        block = seed_ref[:, c * 128 : (c + 1) * 128]
        square = block * block
        for r in range(16):
            total = total + square[8 * r : 8 * r + 8, :]
        modes = mm(mat_ref[...], block)
        out_ref[:, 8 * c : 8 * c + 8, :] = modes.reshape(NS, 8, 128)
    for d in range(NS):
        out_ref[d, 64:72, :] = total


def xmode_kernel(in_ref, mat_ref, modes_ref, weight_ref, energy_ref):
    square = jnp.zeros((128, 128), F32)
    for c in range(NK):
        block = in_ref[:, 8 * c : 8 * c + 8, :].reshape(128, 128)
        modes = mm(mat_ref[...], block)
        modes_ref[:, c * 128 : (c + 1) * 128] = modes
        square = square + modes * modes
    weight = lax.dot_general(
        jnp.ones((8, 128), F32),
        square,
        (((1,), (1,)), ((), ())),
        precision=HIGHEST,
        preferred_element_type=F32,
    )
    for d in range(NS):
        weight_ref[d] = weight
    total = in_ref[0, 64:72, :]
    for d in range(1, NS):
        total = total + in_ref[d, 64:72, :]
    energy_ref[...] = total


def whole_sum(value):
    return jnp.sum(jnp.sum(value, axis=0, keepdims=True), axis=1, keepdims=True)


def disperse_kernel(
    kind_ref, disp_ref, gain_ref, sat_ref, modes_ref, energy_ref, w_ref, tw_ref, fwd_ref, bwd_ref,
    out_ref, one, two
):
    kind = kind_ref[0]

    def load(part, r0, a):
        return modes_ref[64 * part + r0 : 64 * part + r0 + 8, a * NB : (a + 1) * NB]

    outer_forward(load, 64, tw_ref, one)
    two[...] = mm(one[...], fwd_ref[...])

    energy = whole_sum(energy_ref[...])
    gain = gain_ref[kind] / (1.0 + energy / (NG * NG * NT) / sat_ref[kind])
    w = w_ref[...]
    relative = w / gain_width
    amplitude = jnp.exp(0.5 * gain / (1.0 + relative * relative) - loss_rate) * (1.0 / NT)
    angle = disp_scale * disp_ref[kind] * w * w
    filter_spectrum(two, 64, amplitude * jnp.cos(angle), amplitude * jnp.sin(angle))

    one[...] = mm(two[...], bwd_ref[...])

    def store(r0, a, re, im):
        out_ref[r0 : r0 + 8, a * NB : (a + 1) * NB] = re
        out_ref[64 + r0 : 64 + r0 + 8, a * NB : (a + 1) * NB] = im

    outer_backward(one, 64, tw_ref, store)


def small_product(a, b):
    total = a[:, 0:1] * b[0:1, :]
    for k in range(1, KRYLOV):
        total = total + a[:, k : k + 1] * b[k : k + 1, :]
    return total


def krylov_exp(diagonals, couplings):
    row = lax.broadcasted_iota(jnp.int32, (8, 128), 0)
    lane = lax.broadcasted_iota(jnp.int32, (8, 128), 1)
    zero = jnp.zeros((8, 128), F32)
    scale = step_length / 2.0**squarings
    mid, low, high = zero, zero, zero
    for j in range(KRYLOV):
        mid = jnp.where(row == j, diagonals[j] * scale, mid)
        if j + 1 < KRYLOV:
            high = jnp.where(row == j, couplings[j] * scale, high)
            low = jnp.where(row == j + 1, couplings[j] * scale, low)
    term = jnp.where(row == lane, 1.0, 0.0).astype(F32)
    real, imag = term, zero
    for order in range(1, taylor_terms + 1):
        term = mid * term + low * pltpu.roll(term, 1, 0) + high * pltpu.roll(term, 7, 0)
        term = term * (1.0 / order)
        signed = -term if order % 4 in (2, 3) else term
        if order % 2:
            imag = imag + signed
        else:
            real = real + signed
    for _ in range(squarings):
        real, imag = (
            small_product(real, real) - small_product(imag, imag),
            2.0 * small_product(real, imag),
        )
    return real, imag


def propagate_kernel(
    shard_ref, weight_ref, lam_ref, own_ref, modes_ref, mat_ref, out_ref, scaled
):
    weight = weight_ref[:, 0, :]
    lam = lam_ref[...]
    own = own_ref[0]
    scale_zero = jnp.sqrt(whole_sum(weight) + epsilon)
    vector = jnp.sqrt(weight) / scale_zero
    poly = jnp.ones((64, 128), F32) / scale_zero
    before_vector, before_poly, coupling = None, None, None
    diagonals, couplings, polys = [], [], [poly]
    for step in range(KRYLOV):
        image = lam * vector
        if step:
            image = image - coupling * before_vector
        diagonal = whole_sum(vector * image)
        diagonals.append(diagonal)
        if step + 1 < KRYLOV:
            image = image - diagonal * vector
            grown = own * poly
            if step:
                grown = grown - coupling * before_poly
            grown = grown - diagonal * poly
            coupling = jnp.sqrt(whole_sum(image * image) + epsilon)
            couplings.append(coupling)
            before_vector, vector = vector, image / coupling
            before_poly, poly = poly, grown / coupling
            polys.append(poly)
    real, imag = krylov_exp(diagonals, couplings)
    gain_re = real[0:1, 0:1] * polys[0]
    gain_im = imag[0:1, 0:1] * polys[0]
    for j in range(1, KRYLOV):
        gain_re = gain_re + real[j : j + 1, 0:1] * polys[j]
        gain_im = gain_im + imag[j : j + 1, 0:1] * polys[j]
    gain_re = gain_re * scale_zero
    gain_im = gain_im * scale_zero
    for c in range(NK):
        a = modes_ref[0:64, c * 128 : (c + 1) * 128]
        b = modes_ref[64:128, c * 128 : (c + 1) * 128]
        scaled[0:64, :] = gain_re * a - gain_im * b
        scaled[64:128, :] = gain_im * a + gain_re * b
        back = mm(mat_ref[...], scaled[...])
        out_ref[:, :, c * 128 : (c + 1) * 128] = back.reshape(NS, 8, 128)


def kerr_kernel(
    kind_ref, kerr_ref, in_ref, mat_ref, tw_ref, fwd_ref, bwd_ref, raman_ref,
    out_ref, field, delayed, one, two
):
    kerr = kerr_ref[kind_ref[0]]
    field[...] = mm(mat_ref[...], in_ref[...].reshape(128, NT))

    def load(side, r0, a):
        lanes = slice(a * NB, (a + 1) * NB)
        re = field[32 * side + r0 : 32 * side + r0 + 8, lanes]
        im = field[64 + 32 * side + r0 : 64 + 32 * side + r0 + 8, lanes]
        return re * re + im * im

    outer_forward(load, 32, tw_ref, one)
    two[...] = mm(one[...], fwd_ref[...])
    filter_spectrum(two, 32, raman_ref[0], raman_ref[1])
    one[...] = mm(two[...], bwd_ref[...])

    def store(r0, a, re, im):
        lanes = slice(a * NB, (a + 1) * NB)
        delayed[r0 : r0 + 8, lanes] = re
        delayed[32 + r0 : 32 + r0 + 8, lanes] = im

    outer_backward(one, 32, tw_ref, store)

    for r0 in range(0, 64, 8):
        re, im = field[r0 : r0 + 8, :], field[64 + r0 : 64 + r0 + 8, :]
        late = delayed[r0 : r0 + 8, :]
        rotation = kerr * ((1.0 - raman_share) * (re * re + im * im) + raman_share * late)
        c, s = jnp.cos(rotation), jnp.sin(rotation)
        out_ref[r0 : r0 + 8, :] = re * c - im * s
        out_ref[64 + r0 : 64 + r0 + 8, :] = re * s + im * c


def sds(*shape):
    return jax.ShapeDtypeStruct(shape, F32)


SMEM = pl.BlockSpec(memory_space=pltpu.SMEM)
VMEM = pl.BlockSpec(memory_space=pltpu.VMEM)


def cost(flops, moved):
    return pl.CostEstimate(flops=flops, bytes_accessed=moved, transcendentals=0)


def exchange(value):
    return lax.all_to_all(value, "shard", split_axis=0, concat_axis=0, tiled=True)


def per_device(seed_field, segment_order, seg_disp, seg_kerr, seg_gain, seg_sat):
    t = tables()
    shard = lax.axis_index("shard").astype(jnp.int32).reshape(1)
    seed = seed_field.reshape(128, NT)

    ymodes = pl.pallas_call(
        ymode_kernel, out_shape=sds(NS, 72, 128), in_specs=[VMEM] * 2, out_specs=VMEM,
        name="ymode",
    )(seed, t["to_ymode"])
    gathered = exchange(ymodes)
    modes, weight, energy = pl.pallas_call(
        xmode_kernel,
        out_shape=(sds(128, NT), sds(NS, 8, 128), sds(8, 128)),
        in_specs=[VMEM] * 2,
        out_specs=(VMEM,) * 3,
        name="xmode",
    )(gathered, t["to_xmode"])
    weights = exchange(weight)
    modes = pl.pallas_call(
        disperse_kernel,
        out_shape=sds(128, NT),
        in_specs=[SMEM] * 4 + [VMEM] * 6,
        out_specs=VMEM,
        scratch_shapes=[pltpu.VMEM((512, 256), F32)] * 2,
        cost_estimate=cost(6 * 4 * 512 * 256 * 256, 2**20),
        name="disperse",
    )(
        segment_order, seg_disp, seg_gain, seg_sat, modes, energy, t["w"], t["twiddle"],
        t["forward"], t["backward"],
    )
    xback = pl.pallas_call(
        propagate_kernel,
        out_shape=sds(NS, 8, NT),
        grid_spec=pltpu.PrefetchScalarGridSpec(
            num_scalar_prefetch=1,
            grid=(1,),
            in_specs=[
                pl.BlockSpec((NS, 8, 128), lambda i, s: (0, 0, 0)),
                pl.BlockSpec((NS, 128), lambda i, s: (0, 0)),
                pl.BlockSpec((1, 64, 128), lambda i, s: (s[0], 0, 0)),
                pl.BlockSpec((128, NT), lambda i, s: (0, 0)),
                pl.BlockSpec((128, 128), lambda i, s: (0, 0)),
            ],
            out_specs=pl.BlockSpec((NS, 8, NT), lambda i, s: (0, 0, 0)),
            scratch_shapes=[pltpu.VMEM((128, 128), F32)],
        ),
        name="propagate",
    )(shard, weights, t["lam_all"], t["lam_own"], modes, t["from_xmode"])
    rows = exchange(xback)
    result = pl.pallas_call(
        kerr_kernel,
        out_shape=sds(128, NT),
        in_specs=[SMEM] * 2 + [VMEM] * 6,
        out_specs=VMEM,
        scratch_shapes=[pltpu.VMEM((128, NT), F32), pltpu.VMEM((64, NT), F32)]
        + [pltpu.VMEM((256, 256), F32)] * 2,
        name="kerr",
    )(
        segment_order, seg_kerr, rows, t["from_ymode"], t["twiddle"], t["forward"],
        t["backward"], t["raman"],
    )
    count = lax.axis_size("blk")
    result = lax.ppermute(result, "blk", [(b, (b + 1) % count) for b in range(count)])
    return result.reshape(seed_field.shape)


def solution(mesh):
    in_specs = (P("blk", None, "shard", None, None), P("blk"), P(), P(), P(), P())
    out_specs = P("blk", None, "shard", None, None)
    return jax.shard_map(
        per_device, mesh=mesh, in_specs=in_specs, out_specs=out_specs, check_vma=False
    )
```

```python
import functools

import jax
import jax.numpy as jnp
import numpy as np
from jax import lax
from jax.experimental import pallas as pl
from jax.experimental.pallas import tpu as pltpu
from jax.sharding import PartitionSpec as P

KRYLOV = 8
NS = 16
NG = 32
NT = 1024
NK = 8
NB = 128

epsilon = 1e-06
step_length = 2.5
grin_depth = 1.5
squarings = 8
taylor_terms = 10
gain_width = 0.25
loss_rate = 0.5
disp_scale = 60.0
raman_share = 0.18
raman_freq = 0.05
raman_damp = 0.035

F32 = jnp.float32
HIGHEST = lax.Precision.HIGHEST


@functools.cache
def tables():
    cell = (np.arange(NG) - (NG - 1) / 2.0) / (NG / 2.0)
    line = np.diag(-grin_depth * cell * cell)
    line = line + 0.5 * (np.eye(NG, k=1) + np.eye(NG, k=-1))
    values, q = np.linalg.eigh(line)

    to_ymode = np.zeros((NS, 2, 2, 2, 2, 2, NG))
    to_xmode = np.zeros((2, 2, NG, NS, 2, 2, 2))
    for part in range(2):
        for side in range(2):
            for jj in range(2):
                to_ymode[:, part, jj, side, part, side, :] = q[:, jj::2].T
                to_xmode[part, jj, :, :, part, jj, side] = q[side::2, :].T
    to_ymode = to_ymode.reshape(128, 128)
    to_xmode = to_xmode.reshape(128, 128)

    pair = values.reshape(NS, 2)
    lam = pair[:, None, :, None] + values[None, None, None, :] + np.zeros((1, 2, 1, 1))
    lam_all = lam.reshape(NS, 128)
    lam_own = np.broadcast_to(lam_all[:, :64, None], (NS, 64, 128))

    inner = np.arange(NB)
    angle = 2.0 * np.pi * ((inner[:, None] * inner[None, :]) % NB) / NB
    c, s = np.cos(angle), np.sin(angle)
    forward = np.block([[c, -s], [s, c]])
    backward = np.block([[c, s], [-s, c]])
    turn = 2.0 * np.pi * (np.arange(NK)[:, None] * inner[None, :]) / NT
    tw_cos, tw_sin = np.cos(turn), np.sin(turn)

    freq = np.arange(NK)[:, None] + NK * inner[None, :]
    signed = np.where(freq >= NT // 2, freq - NT, freq)
    w = signed / (NT / 2.0)
    resonance = raman_freq * raman_freq
    raman = resonance / (resonance - w * w - 1j * raman_damp * w)
    ram_re = raman.real / NT
    ram_im = np.where(signed == -(NT // 2), 0.0, raman.imag) / NT

    f32 = lambda a: np.ascontiguousarray(a, dtype=np.float32)
    return dict(
        to_ymode=f32(to_ymode),
        from_ymode=f32(to_ymode.T),
        to_xmode=f32(to_xmode),
        from_xmode=f32(to_xmode.T),
        lam_all=f32(lam_all),
        lam_own=f32(lam_own),
        forward=f32(forward),
        backward=f32(backward),
        twiddle=f32(np.stack([tw_cos, tw_sin])),
        w=f32(w),
        raman=f32(np.stack([ram_re, ram_im])),
    )


def mm(a, b):
    return jnp.dot(a, b, precision=HIGHEST, preferred_element_type=F32)


def fourier8(re, im, sign):
    def four(r, i):
        pr, pi = r[0] + r[2], i[0] + i[2]
        mr, mi = r[0] - r[2], i[0] - i[2]
        qr, qi = r[1] + r[3], i[1] + i[3]
        nr, ni = r[1] - r[3], i[1] - i[3]
        tr, ti = (-ni, nr) if sign > 0 else (ni, -nr)
        return (
            [pr + qr, mr + tr, pr - qr, mr - tr],
            [pi + qi, mi + ti, pi - qi, mi - ti],
        )

    er, ei = four(re[0::2], im[0::2])
    orr, oi = four(re[1::2], im[1::2])
    h = np.float32(np.sqrt(0.5))
    if sign > 0:
        w1 = ((orr[1] - oi[1]) * h, (orr[1] + oi[1]) * h)
        w2 = (-oi[2], orr[2])
        w3 = (-(orr[3] + oi[3]) * h, (orr[3] - oi[3]) * h)
    else:
        w1 = ((orr[1] + oi[1]) * h, (oi[1] - orr[1]) * h)
        w2 = (oi[2], -orr[2])
        w3 = ((oi[3] - orr[3]) * h, -(orr[3] + oi[3]) * h)
    tr = [orr[0], w1[0], w2[0], w3[0]]
    ti = [oi[0], w1[1], w2[1], w3[1]]
    out_r = [er[k] + tr[k] for k in range(4)] + [er[k] - tr[k] for k in range(4)]
    out_i = [ei[k] + ti[k] for k in range(4)] + [ei[k] - ti[k] for k in range(4)]
    return out_r, out_i


def outer_forward(load, rows, tw_ref, dest):
    for r0 in range(0, rows, 8):
        re = [load(0, r0, a) for a in range(NK)]
        im = [load(1, r0, a) for a in range(NK)]
        re, im = fourier8(re, im, -1)
        for k in range(NK):
            if k:
                c, s = tw_ref[0, k : k + 1, :], tw_ref[1, k : k + 1, :]
                re[k], im[k] = re[k] * c + im[k] * s, im[k] * c - re[k] * s
            dest[k * rows + r0 : k * rows + r0 + 8, 0:NB] = re[k]
            dest[k * rows + r0 : k * rows + r0 + 8, NB : 2 * NB] = im[k]


def outer_backward(src, rows, tw_ref, store):
    for r0 in range(0, rows, 8):
        re, im = [], []
        for k in range(NK):
            a = src[k * rows + r0 : k * rows + r0 + 8, 0:NB]
            b = src[k * rows + r0 : k * rows + r0 + 8, NB : 2 * NB]
            if k:
                c, s = tw_ref[0, k : k + 1, :], tw_ref[1, k : k + 1, :]
                a, b = a * c - b * s, a * s + b * c
            re.append(a)
            im.append(b)
        re, im = fourier8(re, im, 1)
        for a in range(NK):
            store(r0, a, re[a], im[a])


def filter_spectrum(spec, rows, factor_re, factor_im):
    for k in range(NK):
        fr, fi = factor_re[k : k + 1, :], factor_im[k : k + 1, :]
        lo, hi = k * rows, (k + 1) * rows
        a, b = spec[lo:hi, 0:NB], spec[lo:hi, NB : 2 * NB]
        spec[lo:hi, 0:NB] = a * fr - b * fi
        spec[lo:hi, NB : 2 * NB] = a * fi + b * fr


def ymode_kernel(seed_ref, mat_ref, out_ref):
    total = jnp.zeros((8, 128), F32)
    for c in range(NK):
        block = seed_ref[:, c * 128 : (c + 1) * 128]
        square = block * block
        for r in range(16):
            total = total + square[8 * r : 8 * r + 8, :]
        modes = mm(mat_ref[...], block)
        out_ref[:, 8 * c : 8 * c + 8, :] = modes.reshape(NS, 8, 128)
    for d in range(NS):
        out_ref[d, 64:72, :] = total


def xmode_kernel(
    kind_ref, disp_ref, gain_ref, sat_ref, kerr_ref, in_ref, mat_ref, modes_ref, tile_ref
):
    square = jnp.zeros((128, 128), F32)
    for c in range(NK):
        block = in_ref[:, 8 * c : 8 * c + 8, :].reshape(128, 128)
        modes = mm(mat_ref[...], block)
        modes_ref[:, c * 128 : (c + 1) * 128] = modes
        square = square + modes * modes
    weight = lax.dot_general(
        jnp.ones((8, 128), F32),
        square,
        (((1,), (1,)), ((), ())),
        precision=HIGHEST,
        preferred_element_type=F32,
    )
    total = in_ref[0, 64:72, :]
    for d in range(1, NS):
        total = total + in_ref[d, 64:72, :]
    total = jnp.sum(total, axis=0, keepdims=True)
    kind = kind_ref[0]
    row = lax.broadcasted_iota(jnp.int32, (8, 128), 0)
    tile = jnp.where(row == 1, total, weight)
    for place, ref in ((2, disp_ref), (3, gain_ref), (4, sat_ref), (5, kerr_ref)):
        tile = jnp.where(row == place, ref[kind], tile)
    for d in range(NS):
        tile_ref[d] = tile


def whole_sum(value):
    return jnp.sum(jnp.sum(value, axis=0, keepdims=True), axis=1, keepdims=True)


def disperse_kernel(
    modes_ref, tile_ref, w_ref, tw_ref, fwd_ref, bwd_ref, out_ref, one, two
):

    def load(part, r0, a):
        return modes_ref[64 * part + r0 : 64 * part + r0 + 8, a * NB : (a + 1) * NB]

    outer_forward(load, 64, tw_ref, one)
    two[...] = mm(one[...], fwd_ref[...])

    energy = whole_sum(tile_ref[0, 1:2, :])
    dispersion, gain_peak = tile_ref[0, 2:3, :], tile_ref[0, 3:4, :]
    gain = gain_peak / (1.0 + energy / (NG * NG * NT) / tile_ref[0, 4:5, :])
    w = w_ref[...]
    relative = w / gain_width
    amplitude = jnp.exp(0.5 * gain / (1.0 + relative * relative) - loss_rate) * (1.0 / NT)
    angle = disp_scale * dispersion * w * w
    filter_spectrum(two, 64, amplitude * jnp.cos(angle), amplitude * jnp.sin(angle))

    one[...] = mm(two[...], bwd_ref[...])

    def store(r0, a, re, im):
        out_ref[r0 : r0 + 8, a * NB : (a + 1) * NB] = re
        out_ref[64 + r0 : 64 + r0 + 8, a * NB : (a + 1) * NB] = im

    outer_backward(one, 64, tw_ref, store)


def small_product(a, b):
    total = a[:, 0:1] * b[0:1, :]
    for k in range(1, KRYLOV):
        total = total + a[:, k : k + 1] * b[k : k + 1, :]
    return total


def krylov_exp(diagonals, couplings):
    row = lax.broadcasted_iota(jnp.int32, (8, 128), 0)
    lane = lax.broadcasted_iota(jnp.int32, (8, 128), 1)
    zero = jnp.zeros((8, 128), F32)
    scale = step_length / 2.0**squarings
    mid, low, high = zero, zero, zero
    for j in range(KRYLOV):
        mid = jnp.where(row == j, diagonals[j] * scale, mid)
        if j + 1 < KRYLOV:
            high = jnp.where(row == j, couplings[j] * scale, high)
            low = jnp.where(row == j + 1, couplings[j] * scale, low)
    term = jnp.where(row == lane, 1.0, 0.0).astype(F32)
    real, imag = term, zero
    for order in range(1, taylor_terms + 1):
        term = mid * term + low * pltpu.roll(term, 1, 0) + high * pltpu.roll(term, 7, 0)
        term = term * (1.0 / order)
        signed = -term if order % 4 in (2, 3) else term
        if order % 2:
            imag = imag + signed
        else:
            real = real + signed
    for _ in range(squarings):
        real, imag = (
            small_product(real, real) - small_product(imag, imag),
            2.0 * small_product(real, imag),
        )
    return real, imag


def propagate_kernel(
    shard_ref, weight_ref, lam_ref, own_ref, modes_ref, mat_ref, out_ref, scaled
):
    weight = weight_ref[:, 0, :]
    lam = lam_ref[...]
    own = own_ref[0]
    scale_zero = jnp.sqrt(whole_sum(weight) + epsilon)
    vector = jnp.sqrt(weight) / scale_zero
    poly = jnp.ones((64, 128), F32) / scale_zero
    before_vector, before_poly, coupling = None, None, None
    diagonals, couplings, polys = [], [], [poly]
    for step in range(KRYLOV):
        image = lam * vector
        if step:
            image = image - coupling * before_vector
        diagonal = whole_sum(vector * image)
        diagonals.append(diagonal)
        if step + 1 < KRYLOV:
            image = image - diagonal * vector
            grown = own * poly
            if step:
                grown = grown - coupling * before_poly
            grown = grown - diagonal * poly
            coupling = jnp.sqrt(whole_sum(image * image) + epsilon)
            couplings.append(coupling)
            before_vector, vector = vector, image / coupling
            before_poly, poly = poly, grown / coupling
            polys.append(poly)
    real, imag = krylov_exp(diagonals, couplings)
    gain_re = real[0:1, 0:1] * polys[0]
    gain_im = imag[0:1, 0:1] * polys[0]
    for j in range(1, KRYLOV):
        gain_re = gain_re + real[j : j + 1, 0:1] * polys[j]
        gain_im = gain_im + imag[j : j + 1, 0:1] * polys[j]
    gain_re = gain_re * scale_zero
    gain_im = gain_im * scale_zero
    for c in range(NK):
        a = modes_ref[0:64, c * 128 : (c + 1) * 128]
        b = modes_ref[64:128, c * 128 : (c + 1) * 128]
        scaled[0:64, :] = gain_re * a - gain_im * b
        scaled[64:128, :] = gain_im * a + gain_re * b
        back = mm(mat_ref[...], scaled[...])
        out_ref[:, :, c * 128 : (c + 1) * 128] = back.reshape(NS, 8, 128)


def kerr_kernel(
    tile_ref, in_ref, mat_ref, tw_ref, fwd_ref, bwd_ref, raman_ref,
    out_ref, field, delayed, one, two
):
    kerr = tile_ref[0, 5:6, 0:1]
    field[...] = mm(mat_ref[...], in_ref[...].reshape(128, NT))

    def load(side, r0, a):
        lanes = slice(a * NB, (a + 1) * NB)
        re = field[32 * side + r0 : 32 * side + r0 + 8, lanes]
        im = field[64 + 32 * side + r0 : 64 + 32 * side + r0 + 8, lanes]
        return re * re + im * im

    outer_forward(load, 32, tw_ref, one)
    two[...] = mm(one[...], fwd_ref[...])
    filter_spectrum(two, 32, raman_ref[0], raman_ref[1])
    one[...] = mm(two[...], bwd_ref[...])

    def store(r0, a, re, im):
        lanes = slice(a * NB, (a + 1) * NB)
        delayed[r0 : r0 + 8, lanes] = re
        delayed[32 + r0 : 32 + r0 + 8, lanes] = im

    outer_backward(one, 32, tw_ref, store)

    for r0 in range(0, 64, 8):
        re, im = field[r0 : r0 + 8, :], field[64 + r0 : 64 + r0 + 8, :]
        late = delayed[r0 : r0 + 8, :]
        rotation = kerr * ((1.0 - raman_share) * (re * re + im * im) + raman_share * late)
        c, s = jnp.cos(rotation), jnp.sin(rotation)
        out_ref[r0 : r0 + 8, :] = re * c - im * s
        out_ref[64 + r0 : 64 + r0 + 8, :] = re * s + im * c


SMEM = pl.BlockSpec(memory_space=pltpu.SMEM)
VMEM = pl.BlockSpec(memory_space=pltpu.VMEM)


def near(*shape):
    return pltpu.VMEM(shape, F32)


def hold(value):
    return pltpu.with_memory_space_constraint(value, pltpu.VMEM)


def cost(flops, moved):
    return pl.CostEstimate(flops=flops, bytes_accessed=moved, transcendentals=0)


def exchange(value):
    return lax.all_to_all(value, "shard", split_axis=0, concat_axis=0, tiled=True)


def pass_on(value):
    count = lax.axis_size("blk")
    return lax.ppermute(value, "blk", [(b, (b + 1) % count) for b in range(count)])


def per_device(seed_field, segment_order, seg_disp, seg_kerr, seg_gain, seg_sat):
    t = tables()
    shard = lax.axis_index("shard").astype(jnp.int32).reshape(1)
    seed = seed_field.reshape(128, NT)

    ymodes = pl.pallas_call(
        ymode_kernel, out_shape=near(NS, 72, 128), in_specs=[VMEM] * 2, out_specs=VMEM,
        name="ymode",
    )(seed, t["to_ymode"])
    gathered = exchange(ymodes)
    modes, tile = pl.pallas_call(
        xmode_kernel,
        out_shape=(near(128, NT), near(NS, 8, 128)),
        in_specs=[SMEM] * 5 + [VMEM] * 2,
        out_specs=(VMEM,) * 2,
        name="xmode",
    )(segment_order, seg_disp, seg_gain, seg_sat, seg_kerr, hold(gathered), t["to_xmode"])
    modes = pass_on(modes)
    tile = pass_on(tile)
    weights = exchange(tile)
    modes = pl.pallas_call(
        disperse_kernel,
        out_shape=near(128, NT),
        in_specs=[VMEM] * 6,
        out_specs=VMEM,
        scratch_shapes=[pltpu.VMEM((512, 256), F32)] * 2,
        cost_estimate=cost(6 * 4 * 512 * 256 * 256, 2**20),
        name="disperse",
    )(hold(modes), hold(tile), t["w"], t["twiddle"], t["forward"], t["backward"])
    xback = pl.pallas_call(
        propagate_kernel,
        out_shape=near(NS, 8, NT),
        grid_spec=pltpu.PrefetchScalarGridSpec(
            num_scalar_prefetch=1,
            grid=(1,),
            in_specs=[
                VMEM,
                VMEM,
                pl.BlockSpec((1, 64, 128), lambda i, s: (s[0], 0, 0)),
                VMEM,
                VMEM,
            ],
            out_specs=VMEM,
            scratch_shapes=[pltpu.VMEM((128, 128), F32)],
        ),
        name="propagate",
    )(shard, hold(weights), t["lam_all"], t["lam_own"], hold(modes), t["from_xmode"])
    rows = exchange(xback)
    result = pl.pallas_call(
        kerr_kernel,
        out_shape=jax.ShapeDtypeStruct((128, NT), F32),
        in_specs=[VMEM] * 7,
        out_specs=VMEM,
        scratch_shapes=[pltpu.VMEM((128, NT), F32), pltpu.VMEM((64, NT), F32)]
        + [pltpu.VMEM((256, 256), F32)] * 2,
        name="kerr",
    )(
        hold(tile), hold(rows), t["from_ymode"], t["twiddle"], t["forward"], t["backward"],
        t["raman"],
    )
    return result.reshape(seed_field.shape)


def solution(mesh):
    in_specs = (P("blk", None, "shard", None, None), P("blk"), P(), P(), P(), P())
    out_specs = P("blk", None, "shard", None, None)
    return jax.shard_map(
        per_device, mesh=mesh, in_specs=in_specs, out_specs=out_specs, check_vma=False
    )
```

```python
import functools

import jax
import jax.numpy as jnp
import numpy as np
from jax import lax
from jax.experimental import pallas as pl
from jax.experimental.pallas import tpu as pltpu
from jax.sharding import PartitionSpec as P

KRYLOV = 8
NS = 16
NG = 32
NT = 1024
NK = 8
NB = 128

epsilon = 1e-06
step_length = 2.5
grin_depth = 1.5
squarings = 8
taylor_terms = 10
gain_width = 0.25
loss_rate = 0.5
disp_scale = 60.0
raman_share = 0.18
raman_freq = 0.05
raman_damp = 0.035

F32 = jnp.float32
HIGHEST = lax.Precision.HIGHEST


@functools.cache
def tables():
    cell = (np.arange(NG) - (NG - 1) / 2.0) / (NG / 2.0)
    line = np.diag(-grin_depth * cell * cell)
    line = line + 0.5 * (np.eye(NG, k=1) + np.eye(NG, k=-1))
    values, q = np.linalg.eigh(line)

    to_ymode = np.zeros((NS, 2, 2, 2, 2, 2, NG))
    to_xmode = np.zeros((2, 2, NG, NS, 2, 2, 2))
    for part in range(2):
        for side in range(2):
            for jj in range(2):
                to_ymode[:, part, jj, side, part, side, :] = q[:, jj::2].T
                to_xmode[part, jj, :, :, part, jj, side] = q[side::2, :].T
    to_ymode = to_ymode.reshape(128, 128)
    to_xmode = to_xmode.reshape(128, 128)

    pair = values.reshape(NS, 2)
    lam = pair[:, None, :, None] + values[None, None, None, :] + np.zeros((1, 2, 1, 1))
    lam_all = lam.reshape(NS, 128)
    lam_own = np.broadcast_to(lam_all[:, :64, None], (NS, 64, 128))

    inner = np.arange(NB)
    angle = 2.0 * np.pi * ((inner[:, None] * inner[None, :]) % NB) / NB
    c, s = np.cos(angle), np.sin(angle)
    forward = np.block([[c, -s], [s, c]])
    backward = np.block([[c, s], [-s, c]])
    turn = 2.0 * np.pi * (np.arange(NK)[:, None] * inner[None, :]) / NT
    tw_cos, tw_sin = np.cos(turn), np.sin(turn)

    freq = np.arange(NK)[:, None] + NK * inner[None, :]
    signed = np.where(freq >= NT // 2, freq - NT, freq)
    w = signed / (NT / 2.0)
    resonance = raman_freq * raman_freq
    raman = resonance / (resonance - w * w - 1j * raman_damp * w)
    ram_re = raman.real / NT
    ram_im = np.where(signed == -(NT // 2), 0.0, raman.imag) / NT

    f32 = lambda a: np.ascontiguousarray(a, dtype=np.float32)
    return dict(
        to_ymode=f32(to_ymode),
        from_ymode=f32(to_ymode.T),
        to_xmode=f32(to_xmode),
        from_xmode=f32(to_xmode.T),
        lam_all=f32(lam_all),
        lam_own=f32(lam_own),
        forward=f32(forward),
        backward=f32(backward),
        twiddle=f32(np.stack([tw_cos, tw_sin])),
        w=f32(w),
        raman=f32(np.stack([ram_re, ram_im])),
    )


def mm(a, b):
    return jnp.dot(a, b, precision=HIGHEST, preferred_element_type=F32)


def fourier8(re, im, sign):
    def four(r, i):
        pr, pi = r[0] + r[2], i[0] + i[2]
        mr, mi = r[0] - r[2], i[0] - i[2]
        qr, qi = r[1] + r[3], i[1] + i[3]
        nr, ni = r[1] - r[3], i[1] - i[3]
        tr, ti = (-ni, nr) if sign > 0 else (ni, -nr)
        return (
            [pr + qr, mr + tr, pr - qr, mr - tr],
            [pi + qi, mi + ti, pi - qi, mi - ti],
        )

    er, ei = four(re[0::2], im[0::2])
    orr, oi = four(re[1::2], im[1::2])
    h = np.float32(np.sqrt(0.5))
    if sign > 0:
        w1 = ((orr[1] - oi[1]) * h, (orr[1] + oi[1]) * h)
        w2 = (-oi[2], orr[2])
        w3 = (-(orr[3] + oi[3]) * h, (orr[3] - oi[3]) * h)
    else:
        w1 = ((orr[1] + oi[1]) * h, (oi[1] - orr[1]) * h)
        w2 = (oi[2], -orr[2])
        w3 = ((oi[3] - orr[3]) * h, -(orr[3] + oi[3]) * h)
    tr = [orr[0], w1[0], w2[0], w3[0]]
    ti = [oi[0], w1[1], w2[1], w3[1]]
    out_r = [er[k] + tr[k] for k in range(4)] + [er[k] - tr[k] for k in range(4)]
    out_i = [ei[k] + ti[k] for k in range(4)] + [ei[k] - ti[k] for k in range(4)]
    return out_r, out_i


def outer_forward(load, rows, tw_ref, dest):
    for r0 in range(0, rows, 8):
        re = [load(0, r0, a) for a in range(NK)]
        im = [load(1, r0, a) for a in range(NK)]
        re, im = fourier8(re, im, -1)
        for k in range(NK):
            if k:
                c, s = tw_ref[0, k : k + 1, :], tw_ref[1, k : k + 1, :]
                re[k], im[k] = re[k] * c + im[k] * s, im[k] * c - re[k] * s
            dest[k * rows + r0 : k * rows + r0 + 8, 0:NB] = re[k]
            dest[k * rows + r0 : k * rows + r0 + 8, NB : 2 * NB] = im[k]


def outer_backward(src, rows, tw_ref, store):
    for r0 in range(0, rows, 8):
        re, im = [], []
        for k in range(NK):
            a = src[k * rows + r0 : k * rows + r0 + 8, 0:NB]
            b = src[k * rows + r0 : k * rows + r0 + 8, NB : 2 * NB]
            if k:
                c, s = tw_ref[0, k : k + 1, :], tw_ref[1, k : k + 1, :]
                a, b = a * c - b * s, a * s + b * c
            re.append(a)
            im.append(b)
        re, im = fourier8(re, im, 1)
        for a in range(NK):
            store(r0, a, re[a], im[a])


def filter_spectrum(spec, rows, factor_re, factor_im):
    for k in range(NK):
        fr, fi = factor_re[k : k + 1, :], factor_im[k : k + 1, :]
        lo, hi = k * rows, (k + 1) * rows
        a, b = spec[lo:hi, 0:NB], spec[lo:hi, NB : 2 * NB]
        spec[lo:hi, 0:NB] = a * fr - b * fi
        spec[lo:hi, NB : 2 * NB] = a * fi + b * fr


def ymode_kernel(seed_ref, mat_ref, out_ref):
    total = jnp.zeros((8, 128), F32)
    for c in range(NK):
        block = seed_ref[:, c * 128 : (c + 1) * 128]
        square = block * block
        for r in range(16):
            total = total + square[8 * r : 8 * r + 8, :]
        modes = mm(mat_ref[...], block)
        out_ref[:, 8 * c : 8 * c + 8, :] = modes.reshape(NS, 8, 128)
    for d in range(NS):
        out_ref[d, 64:72, :] = total


def xmode_kernel(
    kind_ref, disp_ref, gain_ref, sat_ref, kerr_ref, in_ref, mat_ref, modes_ref, tile_ref
):
    square = jnp.zeros((128, 128), F32)
    for c in range(NK):
        block = in_ref[:, 8 * c : 8 * c + 8, :].reshape(128, 128)
        modes = mm(mat_ref[...], block)
        modes_ref[:, c * 128 : (c + 1) * 128] = modes
        square = square + modes * modes
    weight = lax.dot_general(
        jnp.ones((8, 128), F32),
        square,
        (((1,), (1,)), ((), ())),
        precision=HIGHEST,
        preferred_element_type=F32,
    )
    total = in_ref[0, 64:72, :]
    for d in range(1, NS):
        total = total + in_ref[d, 64:72, :]
    total = jnp.sum(total, axis=0, keepdims=True)
    kind = kind_ref[0]
    row = lax.broadcasted_iota(jnp.int32, (8, 128), 0)
    tile = jnp.where(row == 1, total, weight)
    for place, ref in ((2, disp_ref), (3, gain_ref), (4, sat_ref), (5, kerr_ref)):
        tile = jnp.where(row == place, ref[kind], tile)
    for d in range(NS):
        tile_ref[d] = tile


def whole_sum(value):
    return jnp.sum(jnp.sum(value, axis=0, keepdims=True), axis=1, keepdims=True)


def disperse_kernel(
    modes_ref, tile_ref, w_ref, tw_ref, fwd_ref, bwd_ref, out_ref, one, two
):

    def load(part, r0, a):
        return modes_ref[64 * part + r0 : 64 * part + r0 + 8, a * NB : (a + 1) * NB]

    outer_forward(load, 64, tw_ref, one)
    two[...] = mm(one[...], fwd_ref[...])

    energy = whole_sum(tile_ref[0, 1:2, :])
    dispersion, gain_peak = tile_ref[0, 2:3, :], tile_ref[0, 3:4, :]
    gain = gain_peak / (1.0 + energy / (NG * NG * NT) / tile_ref[0, 4:5, :])
    w = w_ref[...]
    relative = w / gain_width
    amplitude = jnp.exp(0.5 * gain / (1.0 + relative * relative) - loss_rate) * (1.0 / NT)
    angle = disp_scale * dispersion * w * w
    filter_spectrum(two, 64, amplitude * jnp.cos(angle), amplitude * jnp.sin(angle))

    one[...] = mm(two[...], bwd_ref[...])

    def store(r0, a, re, im):
        out_ref[r0 : r0 + 8, a * NB : (a + 1) * NB] = re
        out_ref[64 + r0 : 64 + r0 + 8, a * NB : (a + 1) * NB] = im

    outer_backward(one, 64, tw_ref, store)


def small_product(a, b):
    total = a[:, 0:1] * b[0:1, :]
    for k in range(1, KRYLOV):
        total = total + a[:, k : k + 1] * b[k : k + 1, :]
    return total


def krylov_exp(diagonals, couplings):
    row = lax.broadcasted_iota(jnp.int32, (8, 128), 0)
    lane = lax.broadcasted_iota(jnp.int32, (8, 128), 1)
    zero = jnp.zeros((8, 128), F32)
    scale = step_length / 2.0**squarings
    mid, low, high = zero, zero, zero
    for j in range(KRYLOV):
        mid = jnp.where(row == j, diagonals[j] * scale, mid)
        if j + 1 < KRYLOV:
            high = jnp.where(row == j, couplings[j] * scale, high)
            low = jnp.where(row == j + 1, couplings[j] * scale, low)
    term = jnp.where(row == lane, 1.0, 0.0).astype(F32)
    real, imag = term, zero
    for order in range(1, taylor_terms + 1):
        term = mid * term + low * pltpu.roll(term, 1, 0) + high * pltpu.roll(term, 7, 0)
        term = term * (1.0 / order)
        signed = -term if order % 4 in (2, 3) else term
        if order % 2:
            imag = imag + signed
        else:
            real = real + signed
    for _ in range(squarings):
        real, imag = (
            small_product(real, real) - small_product(imag, imag),
            2.0 * small_product(real, imag),
        )
    return real, imag


def lanczos_kernel(shard_ref, weight_ref, lam_ref, own_ref, factor_ref):
    weight = weight_ref[:, 0, :]
    lam = lam_ref[...]
    own = own_ref[0]
    scale_zero = jnp.sqrt(whole_sum(weight) + epsilon)
    vector = jnp.sqrt(weight) / scale_zero
    poly = jnp.ones((64, 128), F32) / scale_zero
    before_vector, before_poly, coupling = None, None, None
    diagonals, couplings, polys = [], [], [poly]
    for step in range(KRYLOV):
        image = lam * vector
        if step:
            image = image - coupling * before_vector
        diagonal = whole_sum(vector * image)
        diagonals.append(diagonal)
        if step + 1 < KRYLOV:
            image = image - diagonal * vector
            grown = own * poly
            if step:
                grown = grown - coupling * before_poly
            grown = grown - diagonal * poly
            coupling = jnp.sqrt(whole_sum(image * image) + epsilon)
            couplings.append(coupling)
            before_vector, vector = vector, image / coupling
            before_poly, poly = poly, grown / coupling
            polys.append(poly)
    real, imag = krylov_exp(diagonals, couplings)
    gain_re = real[0:1, 0:1] * polys[0]
    gain_im = imag[0:1, 0:1] * polys[0]
    for j in range(1, KRYLOV):
        gain_re = gain_re + real[j : j + 1, 0:1] * polys[j]
        gain_im = gain_im + imag[j : j + 1, 0:1] * polys[j]
    factor_ref[0] = gain_re * scale_zero
    factor_ref[1] = gain_im * scale_zero


def propagate_kernel(factor_ref, modes_ref, mat_ref, out_ref, scaled):
    gain_re, gain_im = factor_ref[0], factor_ref[1]
    for c in range(NK):
        a = modes_ref[0:64, c * 128 : (c + 1) * 128]
        b = modes_ref[64:128, c * 128 : (c + 1) * 128]
        scaled[0:64, :] = gain_re * a - gain_im * b
        scaled[64:128, :] = gain_im * a + gain_re * b
        back = mm(mat_ref[...], scaled[...])
        out_ref[:, :, c * 128 : (c + 1) * 128] = back.reshape(NS, 8, 128)


def kerr_kernel(
    tile_ref, in_ref, mat_ref, tw_ref, fwd_ref, bwd_ref, raman_ref,
    out_ref, field, delayed, one, two
):
    kerr = tile_ref[0, 5:6, 0:1]
    field[...] = mm(mat_ref[...], in_ref[...].reshape(128, NT))

    def load(side, r0, a):
        lanes = slice(a * NB, (a + 1) * NB)
        re = field[32 * side + r0 : 32 * side + r0 + 8, lanes]
        im = field[64 + 32 * side + r0 : 64 + 32 * side + r0 + 8, lanes]
        return re * re + im * im

    outer_forward(load, 32, tw_ref, one)
    two[...] = mm(one[...], fwd_ref[...])
    filter_spectrum(two, 32, raman_ref[0], raman_ref[1])
    one[...] = mm(two[...], bwd_ref[...])

    def store(r0, a, re, im):
        lanes = slice(a * NB, (a + 1) * NB)
        delayed[r0 : r0 + 8, lanes] = re
        delayed[32 + r0 : 32 + r0 + 8, lanes] = im

    outer_backward(one, 32, tw_ref, store)

    for r0 in range(0, 64, 8):
        re, im = field[r0 : r0 + 8, :], field[64 + r0 : 64 + r0 + 8, :]
        late = delayed[r0 : r0 + 8, :]
        rotation = kerr * ((1.0 - raman_share) * (re * re + im * im) + raman_share * late)
        c, s = jnp.cos(rotation), jnp.sin(rotation)
        out_ref[r0 : r0 + 8, :] = re * c - im * s
        out_ref[64 + r0 : 64 + r0 + 8, :] = re * s + im * c


SMEM = pl.BlockSpec(memory_space=pltpu.SMEM)
VMEM = pl.BlockSpec(memory_space=pltpu.VMEM)


def near(*shape):
    return pltpu.VMEM(shape, F32)


def hold(value):
    return pltpu.with_memory_space_constraint(value, pltpu.VMEM)


def cost(flops, moved):
    return pl.CostEstimate(flops=flops, bytes_accessed=moved, transcendentals=0)


def exchange(value):
    return lax.all_to_all(value, "shard", split_axis=0, concat_axis=0, tiled=True)


def pass_on(value):
    count = lax.axis_size("blk")
    return lax.ppermute(value, "blk", [(b, (b + 1) % count) for b in range(count)])


def per_device(seed_field, segment_order, seg_disp, seg_kerr, seg_gain, seg_sat):
    t = tables()
    shard = lax.axis_index("shard").astype(jnp.int32).reshape(1)
    seed = seed_field.reshape(128, NT)

    ymodes = pl.pallas_call(
        ymode_kernel, out_shape=near(NS, 72, 128), in_specs=[VMEM] * 2, out_specs=VMEM,
        name="ymode",
    )(seed, t["to_ymode"])
    gathered = exchange(ymodes)
    modes, tile = pl.pallas_call(
        xmode_kernel,
        out_shape=(near(128, NT), near(NS, 8, 128)),
        in_specs=[SMEM] * 5 + [VMEM] * 2,
        out_specs=(VMEM,) * 2,
        name="xmode",
    )(segment_order, seg_disp, seg_gain, seg_sat, seg_kerr, hold(gathered), t["to_xmode"])
    shifted = pass_on(tile)
    modes = pl.pallas_call(
        disperse_kernel,
        out_shape=near(128, NT),
        in_specs=[VMEM] * 6,
        out_specs=VMEM,
        scratch_shapes=[pltpu.VMEM((512, 256), F32)] * 2,
        cost_estimate=cost(6 * 4 * 512 * 256 * 256, 2**20),
        name="disperse",
    )(hold(modes), hold(tile), t["w"], t["twiddle"], t["forward"], t["backward"])
    modes, shifted = lax.optimization_barrier((modes, shifted))
    modes = pass_on(modes)
    weights = exchange(shifted)
    factor = pl.pallas_call(
        lanczos_kernel,
        out_shape=near(2, 64, 128),
        grid_spec=pltpu.PrefetchScalarGridSpec(
            num_scalar_prefetch=1,
            grid=(1,),
            in_specs=[VMEM, VMEM, pl.BlockSpec((1, 64, 128), lambda i, s: (s[0], 0, 0))],
            out_specs=VMEM,
        ),
        cost_estimate=cost(6 * 2 * 512 * 256 * 256, 2**20),
        name="lanczos",
    )(shard, hold(weights), t["lam_all"], t["lam_own"])
    xback = pl.pallas_call(
        propagate_kernel,
        out_shape=near(NS, 8, NT),
        in_specs=[VMEM] * 3,
        out_specs=VMEM,
        scratch_shapes=[pltpu.VMEM((128, 128), F32)],
        name="propagate",
    )(hold(factor), hold(modes), t["from_xmode"])
    rows = exchange(xback)
    result = pl.pallas_call(
        kerr_kernel,
        out_shape=jax.ShapeDtypeStruct((128, NT), F32),
        in_specs=[VMEM] * 7,
        out_specs=VMEM,
        scratch_shapes=[pltpu.VMEM((128, NT), F32), pltpu.VMEM((64, NT), F32)]
        + [pltpu.VMEM((256, 256), F32)] * 2,
        name="kerr",
    )(
        hold(shifted), hold(rows), t["from_ymode"], t["twiddle"], t["forward"], t["backward"],
        t["raman"],
    )
    return result.reshape(seed_field.shape)


def solution(mesh):
    in_specs = (P("blk", None, "shard", None, None), P("blk"), P(), P(), P(), P())
    out_specs = P("blk", None, "shard", None, None)
    return jax.shard_map(
        per_device, mesh=mesh, in_specs=in_specs, out_specs=out_specs, check_vma=False
    )
```

```python
import functools

import jax
import jax.numpy as jnp
import numpy as np
from jax import lax
from jax.experimental import pallas as pl
from jax.experimental.pallas import tpu as pltpu
from jax.sharding import PartitionSpec as P

KRYLOV = 8
NS = 16
NG = 32
NT = 1024
NK = 8
NB = 128

epsilon = 1e-06
step_length = 2.5
grin_depth = 1.5
squarings = 8
taylor_terms = 10
gain_width = 0.25
loss_rate = 0.5
disp_scale = 60.0
raman_share = 0.18
raman_freq = 0.05
raman_damp = 0.035

F32 = jnp.float32
HIGHEST = lax.Precision.HIGHEST


@functools.cache
def tables():
    cell = (np.arange(NG) - (NG - 1) / 2.0) / (NG / 2.0)
    line = np.diag(-grin_depth * cell * cell)
    line = line + 0.5 * (np.eye(NG, k=1) + np.eye(NG, k=-1))
    values, q = np.linalg.eigh(line)

    to_ymode = np.zeros((NS, 2, 2, 2, 2, 2, NG))
    to_xmode = np.zeros((2, 2, NG, NS, 2, 2, 2))
    for part in range(2):
        for side in range(2):
            for jj in range(2):
                to_ymode[:, part, jj, side, part, side, :] = q[:, jj::2].T
                to_xmode[part, jj, :, :, part, jj, side] = q[side::2, :].T
    to_ymode = to_ymode.reshape(128, 128)
    to_xmode = to_xmode.reshape(128, 128)

    pair = values.reshape(NS, 2)
    lam = pair[:, None, :, None] + values[None, None, None, :] + np.zeros((1, 2, 1, 1))
    lam_all = lam.reshape(NS, 128)

    inner = np.arange(NB)
    angle = 2.0 * np.pi * ((inner[:, None] * inner[None, :]) % NB) / NB
    c, s = np.cos(angle), np.sin(angle)
    forward = np.block([[c, -s], [s, c]])
    backward = np.block([[c, s], [-s, c]])
    turn = 2.0 * np.pi * (np.arange(NK)[:, None] * inner[None, :]) / NT
    tw_cos, tw_sin = np.cos(turn), np.sin(turn)

    freq = np.arange(NK)[:, None] + NK * inner[None, :]
    signed = np.where(freq >= NT // 2, freq - NT, freq)
    w = signed / (NT / 2.0)
    resonance = raman_freq * raman_freq
    raman = resonance / (resonance - w * w - 1j * raman_damp * w)
    ram_re = raman.real / NT
    ram_im = np.where(signed == -(NT // 2), 0.0, raman.imag) / NT

    f32 = lambda a: np.ascontiguousarray(a, dtype=np.float32)
    return dict(
        to_ymode=f32(to_ymode),
        from_ymode=f32(to_ymode.T),
        to_xmode=f32(to_xmode),
        from_xmode=f32(to_xmode.T),
        lam_all=f32(lam_all),
        forward=f32(forward),
        backward=f32(backward),
        twiddle=f32(np.stack([tw_cos, tw_sin])),
        w=f32(w),
        raman=f32(np.stack([ram_re, ram_im])),
    )


def mm(a, b):
    return jnp.dot(a, b, precision=HIGHEST, preferred_element_type=F32)


def fourier8(re, im, sign):
    def four(r, i):
        pr, pi = r[0] + r[2], i[0] + i[2]
        mr, mi = r[0] - r[2], i[0] - i[2]
        qr, qi = r[1] + r[3], i[1] + i[3]
        nr, ni = r[1] - r[3], i[1] - i[3]
        tr, ti = (-ni, nr) if sign > 0 else (ni, -nr)
        return (
            [pr + qr, mr + tr, pr - qr, mr - tr],
            [pi + qi, mi + ti, pi - qi, mi - ti],
        )

    er, ei = four(re[0::2], im[0::2])
    orr, oi = four(re[1::2], im[1::2])
    h = np.float32(np.sqrt(0.5))
    if sign > 0:
        w1 = ((orr[1] - oi[1]) * h, (orr[1] + oi[1]) * h)
        w2 = (-oi[2], orr[2])
        w3 = (-(orr[3] + oi[3]) * h, (orr[3] - oi[3]) * h)
    else:
        w1 = ((orr[1] + oi[1]) * h, (oi[1] - orr[1]) * h)
        w2 = (oi[2], -orr[2])
        w3 = ((oi[3] - orr[3]) * h, -(orr[3] + oi[3]) * h)
    tr = [orr[0], w1[0], w2[0], w3[0]]
    ti = [oi[0], w1[1], w2[1], w3[1]]
    out_r = [er[k] + tr[k] for k in range(4)] + [er[k] - tr[k] for k in range(4)]
    out_i = [ei[k] + ti[k] for k in range(4)] + [ei[k] - ti[k] for k in range(4)]
    return out_r, out_i


def outer_forward(load, rows, tw_ref, dest):
    for r0 in range(0, rows, 8):
        re = [load(0, r0, a) for a in range(NK)]
        im = [load(1, r0, a) for a in range(NK)]
        re, im = fourier8(re, im, -1)
        for k in range(NK):
            if k:
                c, s = tw_ref[0, k : k + 1, :], tw_ref[1, k : k + 1, :]
                re[k], im[k] = re[k] * c + im[k] * s, im[k] * c - re[k] * s
            dest[k * rows + r0 : k * rows + r0 + 8, 0:NB] = re[k]
            dest[k * rows + r0 : k * rows + r0 + 8, NB : 2 * NB] = im[k]


def outer_backward(src, rows, tw_ref, store):
    for r0 in range(0, rows, 8):
        re, im = [], []
        for k in range(NK):
            a = src[k * rows + r0 : k * rows + r0 + 8, 0:NB]
            b = src[k * rows + r0 : k * rows + r0 + 8, NB : 2 * NB]
            if k:
                c, s = tw_ref[0, k : k + 1, :], tw_ref[1, k : k + 1, :]
                a, b = a * c - b * s, a * s + b * c
            re.append(a)
            im.append(b)
        re, im = fourier8(re, im, 1)
        for a in range(NK):
            store(r0, a, re[a], im[a])


def filter_spectrum(spec, rows, factor_re, factor_im):
    for k in range(NK):
        fr, fi = factor_re[k : k + 1, :], factor_im[k : k + 1, :]
        lo, hi = k * rows, (k + 1) * rows
        a, b = spec[lo:hi, 0:NB], spec[lo:hi, NB : 2 * NB]
        spec[lo:hi, 0:NB] = a * fr - b * fi
        spec[lo:hi, NB : 2 * NB] = a * fi + b * fr


def ymode_kernel(
    seed_ref, mat_ref, lam_ref, kind_ref, disp_ref, gain_ref, sat_ref, kerr_ref, out_ref
):
    total = jnp.zeros((8, 128), F32)
    for c in range(NK):
        block = seed_ref[:, c * 128 : (c + 1) * 128]
        square = block * block
        for r in range(16):
            total = total + square[8 * r : 8 * r + 8, :]
        modes = mm(mat_ref[...], block)
        out_ref[:, 8 * c : 8 * c + 8, :] = modes.reshape(NS, 8, 128)
    row = lax.broadcasted_iota(jnp.int32, (8, 128), 0)
    chosen = lax.broadcasted_iota(jnp.int32, (1, 32), 1) == kind_ref[...]
    side = jnp.broadcast_to(jnp.sum(total, axis=0, keepdims=True), (8, 128))
    for place, ref in ((2, disp_ref), (3, gain_ref), (4, sat_ref), (5, kerr_ref)):
        value = jnp.sum(jnp.where(chosen, ref[...], 0.0), axis=1, keepdims=True)
        side = jnp.where(row == place, value, side)
    for d in range(NS):
        out_ref[d, 64:72, :] = jnp.where(row == 6, lam_ref[d : d + 1, :], side)


def xmode_kernel(in_ref, mat_ref, modes_ref, tile_ref):
    square = jnp.zeros((128, 128), F32)
    for c in range(NK):
        block = in_ref[:, 8 * c : 8 * c + 8, :].reshape(128, 128)
        modes = mm(mat_ref[...], block)
        modes_ref[:, c * 128 : (c + 1) * 128] = modes
        square = square + modes * modes
    weight = lax.dot_general(
        jnp.ones((8, 128), F32),
        square,
        (((1,), (1,)), ((), ())),
        precision=HIGHEST,
        preferred_element_type=F32,
    )
    side = in_ref[0, 64:72, :]
    energy = side
    for d in range(1, NS):
        energy = energy + in_ref[d, 64:72, :]
    row = lax.broadcasted_iota(jnp.int32, (8, 128), 0)
    tile = jnp.where(row == 0, weight, jnp.where(row == 1, energy, side))
    for d in range(NS):
        tile_ref[d] = tile


def whole_sum(value):
    return jnp.sum(jnp.sum(value, axis=0, keepdims=True), axis=1, keepdims=True)


def disperse_kernel(
    modes_ref, tile_ref, w_ref, tw_ref, fwd_ref, bwd_ref, out_ref, one, two
):

    def load(part, r0, a):
        return modes_ref[64 * part + r0 : 64 * part + r0 + 8, a * NB : (a + 1) * NB]

    outer_forward(load, 64, tw_ref, one)
    two[...] = mm(one[...], fwd_ref[...])

    energy = whole_sum(tile_ref[0, 1:2, :])
    dispersion, gain_peak = tile_ref[0, 2:3, :], tile_ref[0, 3:4, :]
    gain = gain_peak / (1.0 + energy / (NG * NG * NT) / tile_ref[0, 4:5, :])
    w = w_ref[...]
    relative = w / gain_width
    amplitude = jnp.exp(0.5 * gain / (1.0 + relative * relative) - loss_rate) * (1.0 / NT)
    angle = disp_scale * dispersion * w * w
    filter_spectrum(two, 64, amplitude * jnp.cos(angle), amplitude * jnp.sin(angle))

    one[...] = mm(two[...], bwd_ref[...])

    def store(r0, a, re, im):
        out_ref[r0 : r0 + 8, a * NB : (a + 1) * NB] = re
        out_ref[64 + r0 : 64 + r0 + 8, a * NB : (a + 1) * NB] = im

    outer_backward(one, 64, tw_ref, store)


def small_product(a, b):
    total = a[:, 0:1] * b[0:1, :]
    for k in range(1, KRYLOV):
        total = total + a[:, k : k + 1] * b[k : k + 1, :]
    return total


def krylov_exp(diagonals, couplings):
    row = lax.broadcasted_iota(jnp.int32, (8, 128), 0)
    lane = lax.broadcasted_iota(jnp.int32, (8, 128), 1)
    zero = jnp.zeros((8, 128), F32)
    scale = step_length / 2.0**squarings
    mid, low, high = zero, zero, zero
    for j in range(KRYLOV):
        mid = jnp.where(row == j, diagonals[j] * scale, mid)
        if j + 1 < KRYLOV:
            high = jnp.where(row == j, couplings[j] * scale, high)
            low = jnp.where(row == j + 1, couplings[j] * scale, low)
    term = jnp.where(row == lane, 1.0, 0.0).astype(F32)
    real, imag = term, zero
    for order in range(1, taylor_terms + 1):
        term = mid * term + low * pltpu.roll(term, 1, 0) + high * pltpu.roll(term, 7, 0)
        term = term * (1.0 / order)
        signed = -term if order % 4 in (2, 3) else term
        if order % 2:
            imag = imag + signed
        else:
            real = real + signed
    for _ in range(squarings):
        real, imag = (
            small_product(real, real) - small_product(imag, imag),
            2.0 * small_product(real, imag),
        )
    return real, imag


def lanczos_kernel(own_ref, weight_ref, factor_ref):
    weight = weight_ref[:, 0, :]
    lam = weight_ref[:, 6, :]
    own = jnp.broadcast_to(own_ref[0, 6:7, :], (8, 128))
    scale_zero = jnp.sqrt(whole_sum(weight) + epsilon)
    vector = jnp.sqrt(weight) / scale_zero
    poly = jnp.ones((8, 128), F32) / scale_zero
    before_vector, before_poly, coupling = None, None, None
    diagonals, couplings, polys = [], [], [poly]
    for step in range(KRYLOV):
        image = lam * vector
        if step:
            image = image - coupling * before_vector
        diagonal = whole_sum(vector * image)
        diagonals.append(diagonal)
        if step + 1 < KRYLOV:
            image = image - diagonal * vector
            grown = own * poly
            if step:
                grown = grown - coupling * before_poly
            grown = grown - diagonal * poly
            coupling = jnp.sqrt(whole_sum(image * image) + epsilon)
            couplings.append(coupling)
            before_vector, vector = vector, image / coupling
            before_poly, poly = poly, grown / coupling
            polys.append(poly)
    real, imag = krylov_exp(diagonals, couplings)
    for place, part in ((0, real), (1, imag)):
        gain = part[0:1, 0:1] * polys[0]
        for j in range(1, KRYLOV):
            gain = gain + part[j : j + 1, 0:1] * polys[j]
        gain = gain * scale_zero
        factor_ref[place] = jnp.broadcast_to(gain[0:1, :], (128, 128)).T[0:64, :]


def propagate_kernel(factor_ref, modes_ref, mat_ref, out_ref, scaled):
    gain_re, gain_im = factor_ref[0], factor_ref[1]
    for c in range(NK):
        a = modes_ref[0:64, c * 128 : (c + 1) * 128]
        b = modes_ref[64:128, c * 128 : (c + 1) * 128]
        scaled[0:64, :] = gain_re * a - gain_im * b
        scaled[64:128, :] = gain_im * a + gain_re * b
        back = mm(mat_ref[...], scaled[...])
        out_ref[:, :, c * 128 : (c + 1) * 128] = back.reshape(NS, 8, 128)


def kerr_kernel(
    tile_ref, in_ref, mat_ref, tw_ref, fwd_ref, bwd_ref, raman_ref,
    out_ref, field, delayed, one, two
):
    kerr = tile_ref[0, 5:6, 0:1]
    field[...] = mm(mat_ref[...], in_ref[...].reshape(128, NT))

    def load(side, r0, a):
        lanes = slice(a * NB, (a + 1) * NB)
        re = field[32 * side + r0 : 32 * side + r0 + 8, lanes]
        im = field[64 + 32 * side + r0 : 64 + 32 * side + r0 + 8, lanes]
        return re * re + im * im

    outer_forward(load, 32, tw_ref, one)
    two[...] = mm(one[...], fwd_ref[...])
    filter_spectrum(two, 32, raman_ref[0], raman_ref[1])
    one[...] = mm(two[...], bwd_ref[...])

    def store(r0, a, re, im):
        lanes = slice(a * NB, (a + 1) * NB)
        delayed[r0 : r0 + 8, lanes] = re
        delayed[32 + r0 : 32 + r0 + 8, lanes] = im

    outer_backward(one, 32, tw_ref, store)

    for r0 in range(0, 64, 8):
        re, im = field[r0 : r0 + 8, :], field[64 + r0 : 64 + r0 + 8, :]
        late = delayed[r0 : r0 + 8, :]
        rotation = kerr * ((1.0 - raman_share) * (re * re + im * im) + raman_share * late)
        c, s = jnp.cos(rotation), jnp.sin(rotation)
        out_ref[r0 : r0 + 8, :] = re * c - im * s
        out_ref[64 + r0 : 64 + r0 + 8, :] = re * s + im * c


VMEM = pl.BlockSpec(memory_space=pltpu.VMEM)


def near(*shape):
    return pltpu.VMEM(shape, F32)


def hold(value):
    return pltpu.with_memory_space_constraint(value, pltpu.VMEM)


def cost(flops, moved):
    return pl.CostEstimate(flops=flops, bytes_accessed=moved, transcendentals=0)


def exchange(value):
    return lax.all_to_all(value, "shard", split_axis=0, concat_axis=0, tiled=True)


def pass_on(value):
    count = lax.axis_size("blk")
    return lax.ppermute(value, "blk", [(b, (b + 1) % count) for b in range(count)])


def per_device(seed_field, segment_order, seg_disp, seg_kerr, seg_gain, seg_sat):
    t = tables()
    near_tables = {name: hold(jnp.asarray(value)) for name, value in t.items()}
    seed = seed_field.reshape(128, NT)

    ymodes = pl.pallas_call(
        ymode_kernel,
        out_shape=near(NS, 72, 128),
        in_specs=[VMEM] * 8,
        out_specs=VMEM,
        name="ymode",
    )(
        seed, t["to_ymode"], t["lam_all"], segment_order.reshape(1, 1),
        *(each.reshape(1, 32) for each in (seg_disp, seg_gain, seg_sat, seg_kerr)),
    )
    gathered = exchange(ymodes)
    modes, tile = pl.pallas_call(
        xmode_kernel,
        out_shape=(near(128, NT), near(NS, 8, 128)),
        in_specs=[VMEM] * 2,
        out_specs=(VMEM,) * 2,
        name="xmode",
    )(hold(gathered), near_tables["to_xmode"])
    shifted = pass_on(tile)
    modes = pl.pallas_call(
        disperse_kernel,
        out_shape=near(128, NT),
        in_specs=[VMEM] * 6,
        out_specs=VMEM,
        scratch_shapes=[pltpu.VMEM((512, 256), F32)] * 2,
        cost_estimate=cost(6 * 4 * 512 * 256 * 256, 2**20),
        name="disperse",
    )(
        hold(modes), hold(tile),
        *(near_tables[name] for name in ("w", "twiddle", "forward", "backward")),
    )
    modes, shifted = lax.optimization_barrier((modes, shifted))
    modes = pass_on(modes)
    weights = exchange(shifted)
    factor = pl.pallas_call(
        lanczos_kernel,
        out_shape=near(2, 64, 128),
        in_specs=[VMEM] * 2,
        out_specs=VMEM,
        cost_estimate=cost(6 * 2 * 512 * 256 * 256, 2**20),
        name="lanczos",
    )(hold(shifted), hold(weights))
    xback = pl.pallas_call(
        propagate_kernel,
        out_shape=near(NS, 8, NT),
        in_specs=[VMEM] * 3,
        out_specs=VMEM,
        scratch_shapes=[pltpu.VMEM((128, 128), F32)],
        name="propagate",
    )(hold(factor), hold(modes), near_tables["from_xmode"])
    rows = exchange(xback)
    result = pl.pallas_call(
        kerr_kernel,
        out_shape=jax.ShapeDtypeStruct((128, NT), F32),
        in_specs=[VMEM] * 7,
        out_specs=VMEM,
        scratch_shapes=[pltpu.VMEM((128, NT), F32), pltpu.VMEM((64, NT), F32)]
        + [pltpu.VMEM((256, 256), F32)] * 2,
        name="kerr",
    )(
        hold(shifted), hold(rows),
        *(
            near_tables[name]
            for name in ("from_ymode", "twiddle", "forward", "backward", "raman")
        ),
    )
    return result.reshape(seed_field.shape)


def solution(mesh):
    in_specs = (P("blk", None, "shard", None, None), P("blk"), P(), P(), P(), P())
    out_specs = P("blk", None, "shard", None, None)
    return jax.shard_map(
        per_device, mesh=mesh, in_specs=in_specs, out_specs=out_specs, check_vma=False
    )
```

```python
import functools

import jax
import jax.numpy as jnp
import numpy as np
from jax import lax
from jax.experimental import pallas as pl
from jax.experimental.pallas import tpu as pltpu
from jax.sharding import PartitionSpec as P

KRYLOV = 8
NS = 16
NG = 32
NT = 1024
NK = 8
NB = 128

epsilon = 1e-06
step_length = 2.5
grin_depth = 1.5
squarings = 8
taylor_terms = 10
gain_width = 0.25
loss_rate = 0.5
disp_scale = 60.0
raman_share = 0.18
raman_freq = 0.05
raman_damp = 0.035

F32 = jnp.float32
HIGHEST = lax.Precision.HIGHEST


@functools.cache
def tables():
    cell = (np.arange(NG) - (NG - 1) / 2.0) / (NG / 2.0)
    line = np.diag(-grin_depth * cell * cell)
    line = line + 0.5 * (np.eye(NG, k=1) + np.eye(NG, k=-1))
    values, q = np.linalg.eigh(line)

    to_ymode = np.zeros((NS, 2, 2, 2, 2, 2, NG))
    to_xmode = np.zeros((2, 2, NG, NS, 2, 2, 2))
    for part in range(2):
        for side in range(2):
            for jj in range(2):
                to_ymode[:, part, jj, side, part, side, :] = q[:, jj::2].T
                to_xmode[part, jj, :, :, part, jj, side] = q[side::2, :].T
    to_ymode = to_ymode.reshape(128, 128)
    to_xmode = to_xmode.reshape(128, 128)

    pair = values.reshape(NS, 2)
    lam = pair[:, None, :, None] + values[None, None, None, :] + np.zeros((1, 2, 1, 1))
    lam_all = lam.reshape(NS, 128)

    inner = np.arange(NB)
    angle = 2.0 * np.pi * ((inner[:, None] * inner[None, :]) % NB) / NB
    c, s = np.cos(angle), np.sin(angle)
    forward = np.block([[c, -s], [s, c]])
    backward = np.block([[c, s], [-s, c]])
    turn = 2.0 * np.pi * (np.arange(NK)[:, None] * inner[None, :]) / NT
    tw_cos, tw_sin = np.cos(turn), np.sin(turn)

    freq = np.arange(NK)[:, None] + NK * inner[None, :]
    signed = np.where(freq >= NT // 2, freq - NT, freq)
    w = signed / (NT / 2.0)
    resonance = raman_freq * raman_freq
    raman = resonance / (resonance - w * w - 1j * raman_damp * w)
    ram_re = raman.real / NT
    ram_im = np.where(signed == -(NT // 2), 0.0, raman.imag) / NT

    f32 = lambda a: np.ascontiguousarray(a, dtype=np.float32)
    return dict(
        to_ymode=f32(to_ymode),
        from_ymode=f32(to_ymode.T),
        to_xmode=f32(to_xmode),
        from_xmode=f32(to_xmode.T),
        lam_all=f32(lam_all),
        forward_split=split(f32(forward)),
        backward_split=split(f32(backward)),
        forward=f32(forward),
        backward=f32(backward),
        twiddle=f32(np.stack([tw_cos, tw_sin])),
        w=f32(w),
        raman=f32(np.stack([ram_re, ram_im])),
    )


def split(table):
    high = table.astype(jnp.bfloat16)
    return np.stack([high, (table - high.astype(np.float32)).astype(jnp.bfloat16)])


def mm_split(a, b_ref):
    high = a.astype(jnp.bfloat16)
    low = (a - high.astype(F32)).astype(jnp.bfloat16)
    dot = functools.partial(jnp.dot, preferred_element_type=F32)
    return dot(high, b_ref[0]) + (dot(high, b_ref[1]) + dot(low, b_ref[0]))


def mm(a, b):
    return jnp.dot(a, b, precision=HIGHEST, preferred_element_type=F32)


def fourier8(re, im, sign):
    def four(r, i):
        pr, pi = r[0] + r[2], i[0] + i[2]
        mr, mi = r[0] - r[2], i[0] - i[2]
        qr, qi = r[1] + r[3], i[1] + i[3]
        nr, ni = r[1] - r[3], i[1] - i[3]
        tr, ti = (-ni, nr) if sign > 0 else (ni, -nr)
        return (
            [pr + qr, mr + tr, pr - qr, mr - tr],
            [pi + qi, mi + ti, pi - qi, mi - ti],
        )

    er, ei = four(re[0::2], im[0::2])
    orr, oi = four(re[1::2], im[1::2])
    h = np.float32(np.sqrt(0.5))
    if sign > 0:
        w1 = ((orr[1] - oi[1]) * h, (orr[1] + oi[1]) * h)
        w2 = (-oi[2], orr[2])
        w3 = (-(orr[3] + oi[3]) * h, (orr[3] - oi[3]) * h)
    else:
        w1 = ((orr[1] + oi[1]) * h, (oi[1] - orr[1]) * h)
        w2 = (oi[2], -orr[2])
        w3 = ((oi[3] - orr[3]) * h, -(orr[3] + oi[3]) * h)
    tr = [orr[0], w1[0], w2[0], w3[0]]
    ti = [oi[0], w1[1], w2[1], w3[1]]
    out_r = [er[k] + tr[k] for k in range(4)] + [er[k] - tr[k] for k in range(4)]
    out_i = [ei[k] + ti[k] for k in range(4)] + [ei[k] - ti[k] for k in range(4)]
    return out_r, out_i


def outer_forward(load, rows, tw_ref, dest):
    for r0 in range(0, rows, 8):
        re = [load(0, r0, a) for a in range(NK)]
        im = [load(1, r0, a) for a in range(NK)]
        re, im = fourier8(re, im, -1)
        for k in range(NK):
            if k:
                c, s = tw_ref[0, k : k + 1, :], tw_ref[1, k : k + 1, :]
                re[k], im[k] = re[k] * c + im[k] * s, im[k] * c - re[k] * s
            dest[k * rows + r0 : k * rows + r0 + 8, 0:NB] = re[k]
            dest[k * rows + r0 : k * rows + r0 + 8, NB : 2 * NB] = im[k]


def outer_backward(src, rows, tw_ref, store):
    for r0 in range(0, rows, 8):
        re, im = [], []
        for k in range(NK):
            a = src[k * rows + r0 : k * rows + r0 + 8, 0:NB]
            b = src[k * rows + r0 : k * rows + r0 + 8, NB : 2 * NB]
            if k:
                c, s = tw_ref[0, k : k + 1, :], tw_ref[1, k : k + 1, :]
                a, b = a * c - b * s, a * s + b * c
            re.append(a)
            im.append(b)
        re, im = fourier8(re, im, 1)
        for a in range(NK):
            store(r0, a, re[a], im[a])


def filter_spectrum(spec, rows, factor_re, factor_im):
    for k in range(NK):
        fr, fi = factor_re[k : k + 1, :], factor_im[k : k + 1, :]
        lo, hi = k * rows, (k + 1) * rows
        a, b = spec[lo:hi, 0:NB], spec[lo:hi, NB : 2 * NB]
        spec[lo:hi, 0:NB] = a * fr - b * fi
        spec[lo:hi, NB : 2 * NB] = a * fi + b * fr


def ymode_kernel(
    seed_ref, mat_ref, lam_ref, kind_ref, disp_ref, gain_ref, sat_ref, kerr_ref, out_ref
):
    total = jnp.zeros((8, 128), F32)
    for c in range(NK):
        block = seed_ref[:, c * 128 : (c + 1) * 128]
        square = block * block
        for r in range(16):
            total = total + square[8 * r : 8 * r + 8, :]
        modes = mm(mat_ref[...], block)
        out_ref[:, 8 * c : 8 * c + 8, :] = modes.reshape(NS, 8, 128)
    row = lax.broadcasted_iota(jnp.int32, (8, 128), 0)
    chosen = lax.broadcasted_iota(jnp.int32, (1, 32), 1) == kind_ref[...]
    side = jnp.broadcast_to(jnp.sum(total, axis=0, keepdims=True), (8, 128))
    for place, ref in ((2, disp_ref), (3, gain_ref), (4, sat_ref), (5, kerr_ref)):
        value = jnp.sum(jnp.where(chosen, ref[...], 0.0), axis=1, keepdims=True)
        side = jnp.where(row == place, value, side)
    for d in range(NS):
        out_ref[d, 64:72, :] = jnp.where(row == 6, lam_ref[d : d + 1, :], side)


def xmode_kernel(in_ref, mat_ref, modes_ref, side_ref, tile_ref):
    square = jnp.zeros((128, 128), F32)
    for c in range(NK):
        block = in_ref[:, 8 * c : 8 * c + 8, :].reshape(128, 128)
        modes = mm(mat_ref[...], block)
        modes_ref[:, c * 128 : (c + 1) * 128] = modes
        square = square + modes * modes
    weight = lax.dot_general(
        jnp.ones((8, 128), F32),
        square,
        (((1,), (1,)), ((), ())),
        precision=HIGHEST,
        preferred_element_type=F32,
    )
    side = in_ref[0, 64:72, :]
    energy = side
    for d in range(1, NS):
        energy = energy + in_ref[d, 64:72, :]
    row = lax.broadcasted_iota(jnp.int32, (8, 128), 0)
    side_ref[...] = jnp.where(row == 1, energy, side)
    lane = lax.broadcasted_iota(jnp.int32, (8, 128), 1)
    tile = jnp.where(lane < 64, weight + pltpu.roll(weight, 64, 1), side[5:6, :])
    for d in range(NS):
        tile_ref[d] = tile[0:1, :]


def turn(angle):
    count = jnp.floor(angle * np.float32(2.0 / np.pi) + 0.5)
    x = angle - count * 1.5703125
    x = x - count * 4.837512969970703e-4
    x = x - count * 7.549789948768648e-8
    x = jnp.clip(x, -0.8, 0.8)
    z = x * x
    sine = ((-1.9515295891e-4 * z + 8.3321608736e-3) * z - 1.6666654611e-1) * z * x + x
    cosine = ((2.443315711809948e-5 * z - 1.388731625493765e-3) * z + 4.166664568298827e-2) * z
    cosine = cosine * z - 0.5 * z + 1.0
    quarter = count.astype(jnp.int32)
    odd = (quarter & 1) == 1
    c, s = jnp.where(odd, sine, cosine), jnp.where(odd, cosine, sine)
    c = jnp.where(((quarter + 1) & 2) == 2, -c, c)
    s = jnp.where((quarter & 2) == 2, -s, s)
    return c, s


def whole_sum(value):
    return jnp.sum(jnp.sum(value, axis=0, keepdims=True), axis=1, keepdims=True)


def disperse_kernel(
    modes_ref, side_ref, w_ref, tw_ref, fwd_ref, bwd_ref, out_ref, one, two
):

    def load(part, r0, a):
        return modes_ref[64 * part + r0 : 64 * part + r0 + 8, a * NB : (a + 1) * NB]

    outer_forward(load, 64, tw_ref, one)
    two[...] = mm(one[...], fwd_ref[...])

    energy = whole_sum(side_ref[1:2, :])
    dispersion, gain_peak = side_ref[2:3, :], side_ref[3:4, :]
    gain = gain_peak / (1.0 + energy / (NG * NG * NT) / side_ref[4:5, :])
    w = w_ref[...]
    relative = w / gain_width
    amplitude = jnp.exp(0.5 * gain / (1.0 + relative * relative) - loss_rate) * (1.0 / NT)
    angle = disp_scale * dispersion * w * w
    filter_spectrum(two, 64, amplitude * jnp.cos(angle), amplitude * jnp.sin(angle))

    one[...] = mm(two[...], bwd_ref[...])

    def store(r0, a, re, im):
        out_ref[r0 : r0 + 8, a * NB : (a + 1) * NB] = re
        out_ref[64 + r0 : 64 + r0 + 8, a * NB : (a + 1) * NB] = im

    outer_backward(one, 64, tw_ref, store)


def small_product(a, b):
    total = a[:, 0:1] * b[0:1, :]
    for k in range(1, KRYLOV):
        total = total + a[:, k : k + 1] * b[k : k + 1, :]
    return total


def krylov_exp(diagonals, couplings):
    row = lax.broadcasted_iota(jnp.int32, (8, 128), 0)
    lane = lax.broadcasted_iota(jnp.int32, (8, 128), 1)
    zero = jnp.zeros((8, 128), F32)
    scale = step_length / 2.0**squarings
    mid, low, high = zero, zero, zero
    for j in range(KRYLOV):
        mid = jnp.where(row == j, diagonals[j] * scale, mid)
        if j + 1 < KRYLOV:
            high = jnp.where(row == j, couplings[j] * scale, high)
            low = jnp.where(row == j + 1, couplings[j] * scale, low)
    term = jnp.where(row == lane, 1.0, 0.0).astype(F32)
    real, imag = term, zero
    for order in range(1, taylor_terms + 1):
        term = mid * term + low * pltpu.roll(term, 1, 0) + high * pltpu.roll(term, 7, 0)
        term = term * (1.0 / order)
        signed = -term if order % 4 in (2, 3) else term
        if order % 2:
            imag = imag + signed
        else:
            real = real + signed
    for _ in range(squarings):
        real, imag = (
            small_product(real, real) - small_product(imag, imag),
            2.0 * small_product(real, imag),
        )
    return real, imag


def mode_gains(weight, lam, own):
    rest = jnp.sqrt(weight)
    grown = jnp.ones((8, 128), F32)
    diagonals, couplings, polys = [], [], []
    for step in range(KRYLOV):
        spread = lam * rest
        square = whole_sum(rest * rest) + epsilon
        diagonal = whole_sum(spread * rest)
        if step:
            overlap = whole_sum(rest * vector)
        inverse = lax.rsqrt(square)
        coupling = square * inverse
        diagonal = diagonal * inverse * inverse
        if step:
            diagonal = diagonal - overlap
        diagonals.append(diagonal)
        couplings.append(coupling)
        poly = grown * inverse
        polys.append(poly)
        if step + 1 < KRYLOV:
            rest = rest * inverse
            image = spread * inverse
            grown = own * poly
            if step:
                image = image - coupling * vector
                grown = grown - coupling * before
            vector, before = rest, poly
            rest = image - diagonal * vector
            grown = grown - diagonal * before
    scale_zero = couplings[0]
    real, imag = krylov_exp(diagonals, couplings[1:])
    gains = []
    for part in (real, imag):
        gain = part[0:1, 0:1] * polys[0]
        for j in range(1, KRYLOV):
            gain = gain + part[j : j + 1, 0:1] * polys[j]
        gains.append(gain * scale_zero)
    return gains


def propagate_kernel(side_ref, weight_ref, lam_ref, modes_ref, mat_ref, out_ref, scaled):
    own = jnp.broadcast_to(side_ref[6:7, :], (8, 128))
    lane = lax.broadcasted_iota(jnp.int32, (NS, 128), 1)
    weight = jnp.where(lane < 64, weight_ref[:, 0, :], 0.0)
    gains = mode_gains(weight, lam_ref[...], own)
    gain_re, gain_im = (
        jnp.broadcast_to(gain[0:1, :], (128, 128)).T[0:64, :] for gain in gains
    )
    for c in range(NK):
        a = modes_ref[0:64, c * 128 : (c + 1) * 128]
        b = modes_ref[64:128, c * 128 : (c + 1) * 128]
        scaled[0:64, :] = gain_re * a - gain_im * b
        scaled[64:128, :] = gain_im * a + gain_re * b
        back = mm(mat_ref[...], scaled[...])
        out_ref[:, :, c * 128 : (c + 1) * 128] = back.reshape(NS, 8, 128)


def kerr_kernel(
    tile_ref, in_ref, mat_ref, tw_ref, fwd_ref, bwd_ref, raman_ref,
    out_ref, field, delayed, one, two, done, sems
):
    kerr = tile_ref[0, 0:1, 64:65]
    field[...] = mm(mat_ref[...], in_ref[...].reshape(128, NT))

    def load(side, r0, a):
        lanes = slice(a * NB, (a + 1) * NB)
        re = field[32 * side + r0 : 32 * side + r0 + 8, lanes]
        im = field[64 + 32 * side + r0 : 64 + 32 * side + r0 + 8, lanes]
        return re * re + im * im

    outer_forward(load, 32, tw_ref, one)
    two[...] = mm_split(one[...], fwd_ref)
    filter_spectrum(two, 32, raman_ref[0], raman_ref[1])
    one[...] = mm_split(two[...], bwd_ref)

    def store(r0, a, re, im):
        lanes = slice(a * NB, (a + 1) * NB)
        delayed[r0 : r0 + 8, lanes] = re
        delayed[32 + r0 : 32 + r0 + 8, lanes] = im

    outer_backward(one, 32, tw_ref, store)

    copies = []
    for r0 in range(0, 64, 8):
        re, im = field[r0 : r0 + 8, :], field[64 + r0 : 64 + r0 + 8, :]
        late = delayed[r0 : r0 + 8, :]
        rotation = kerr * ((1.0 - raman_share) * (re * re + im * im) + raman_share * late)
        c, s = turn(rotation)
        done[r0 : r0 + 8, :] = re * c - im * s
        done[64 + r0 : 64 + r0 + 8, :] = re * s + im * c
        if r0 % 16 == 8:
            for lo in (r0 - 8, 64 + r0 - 8):
                rows = pl.ds(lo, 16)
                copy = pltpu.make_async_copy(done.at[rows], out_ref.at[rows], sems.at[lo // 16])
                copy.start()
                copies.append(copy)
    for copy in copies:
        copy.wait()


VMEM = pl.BlockSpec(memory_space=pltpu.VMEM)
HBM = pl.BlockSpec(memory_space=pltpu.HBM)


def near(*shape):
    return pltpu.VMEM(shape, F32)


def hold(value):
    return pltpu.with_memory_space_constraint(value, pltpu.VMEM)


def cost(flops, moved):
    return pl.CostEstimate(flops=flops, bytes_accessed=moved, transcendentals=0)


def exchange(value):
    return lax.all_to_all(value, "shard", split_axis=0, concat_axis=0, tiled=True)


def pass_on(value):
    count = lax.axis_size("blk")
    return lax.ppermute(value, "blk", [(b, (b + 1) % count) for b in range(count)])


def per_device(seed_field, segment_order, seg_disp, seg_kerr, seg_gain, seg_sat):
    t = tables()
    near_tables = {name: hold(jnp.asarray(value)) for name, value in t.items()}
    seed = seed_field.reshape(128, NT)

    ymodes = pl.pallas_call(
        ymode_kernel,
        out_shape=near(NS, 72, 128),
        in_specs=[VMEM] * 8,
        out_specs=VMEM,
        name="ymode",
    )(
        seed, t["to_ymode"], t["lam_all"], segment_order.reshape(1, 1),
        *(each.reshape(1, 32) for each in (seg_disp, seg_gain, seg_sat, seg_kerr)),
    )
    gathered = exchange(ymodes)
    modes, side, tile = pl.pallas_call(
        xmode_kernel,
        out_shape=(near(128, NT), near(8, 128), near(NS, 1, 128)),
        in_specs=[VMEM] * 2,
        out_specs=(VMEM,) * 3,
        name="xmode",
    )(hold(gathered), near_tables["to_xmode"])
    shifted = pass_on(tile)
    modes = pl.pallas_call(
        disperse_kernel,
        out_shape=near(128, NT),
        in_specs=[VMEM] * 6,
        out_specs=VMEM,
        scratch_shapes=[pltpu.VMEM((512, 256), F32)] * 2,
        cost_estimate=cost(6 * 4 * 512 * 256 * 256, 2**20),
        name="disperse",
    )(
        hold(modes), hold(side),
        *(near_tables[name] for name in ("w", "twiddle", "forward", "backward")),
    )
    modes, shifted = lax.optimization_barrier((modes, shifted))
    modes = pass_on(modes)
    weights = exchange(shifted)
    xback = pl.pallas_call(
        propagate_kernel,
        out_shape=near(NS, 8, NT),
        in_specs=[VMEM] * 5,
        out_specs=VMEM,
        scratch_shapes=[pltpu.VMEM((128, 128), F32)],
        name="propagate",
    )(
        hold(side), hold(weights), near_tables["lam_all"], hold(modes),
        near_tables["from_xmode"],
    )
    rows = exchange(xback)
    result = pl.pallas_call(
        kerr_kernel,
        out_shape=jax.ShapeDtypeStruct((128, NT), F32),
        in_specs=[VMEM] * 7,
        out_specs=HBM,
        scratch_shapes=[pltpu.VMEM((128, NT), F32), pltpu.VMEM((64, NT), F32)]
        + [pltpu.VMEM((256, 256), F32)] * 2
        + [pltpu.VMEM((128, NT), F32), pltpu.SemaphoreType.DMA((8,))],
        name="kerr",
    )(
        hold(shifted), hold(rows),
        *(
            near_tables[name]
            for name in ("from_ymode", "twiddle", "forward_split", "backward_split", "raman")
        ),
    )
    return result.reshape(seed_field.shape)


def solution(mesh):
    in_specs = (P("blk", None, "shard", None, None), P("blk"), P(), P(), P(), P())
    out_specs = P("blk", None, "shard", None, None)
    return jax.shard_map(
        per_device, mesh=mesh, in_specs=in_specs, out_specs=out_specs, check_vma=False
    )
```

```python
import functools
import math

import jax
import jax.numpy as jnp
import numpy as np
from jax import lax
from jax.experimental import pallas as pl
from jax.experimental.pallas import tpu as pltpu
from jax.sharding import PartitionSpec as P

KRYLOV = 8
EXPANDED = 5
NS = 16
NG = 32
NT = 1024
NK = 8
WIDE = 2
NB = 128

epsilon = 1e-06
step_length = 2.5
grin_depth = 1.5
squarings = 8
taylor_terms = 10
gain_width = 0.25
loss_rate = 0.5
disp_scale = 60.0
raman_share = 0.18
raman_freq = 0.05
raman_damp = 0.035

F32 = jnp.float32
HIGHEST = lax.Precision.HIGHEST


@functools.cache
def tables():
    cell = (np.arange(NG) - (NG - 1) / 2.0) / (NG / 2.0)
    line = np.diag(-grin_depth * cell * cell)
    line = line + 0.5 * (np.eye(NG, k=1) + np.eye(NG, k=-1))
    values, q = np.linalg.eigh(line)

    to_ymode = np.zeros((NS, 2, 2, 2, 2, 2, NG))
    to_xmode = np.zeros((2, 2, NG, NS, 2, 2, 2))
    for part in range(2):
        for side in range(2):
            for jj in range(2):
                to_ymode[:, part, jj, side, part, side, :] = q[:, jj::2].T
                to_xmode[part, jj, :, :, part, jj, side] = q[side::2, :].T
    to_ymode = to_ymode.reshape(128, 128)
    to_xmode = to_xmode.reshape(128, 128)

    pair = values.reshape(NS, 2)
    lam = pair[:, None, :, None] + values[None, None, None, :] + np.zeros((1, 2, 1, 1))
    lam_all = lam.reshape(NS, 128)

    inner = np.arange(NB)
    angle = 2.0 * np.pi * ((inner[:, None] * inner[None, :]) % NB) / NB
    c, s = np.cos(angle), np.sin(angle)
    forward = np.block([[c, -s], [s, c]])
    backward = np.block([[c, s], [-s, c]])
    turn = 2.0 * np.pi * (np.arange(NK)[:, None] * inner[None, :]) / NT
    tw_cos, tw_sin = np.cos(turn), np.sin(turn)

    freq = np.arange(NK)[:, None] + NK * inner[None, :]
    signed = np.where(freq >= NT // 2, freq - NT, freq)
    w = signed / (NT / 2.0)
    resonance = raman_freq * raman_freq
    raman = resonance / (resonance - w * w - 1j * raman_damp * w)
    ram_re = raman.real / NT
    ram_im = np.where(signed == -(NT // 2), 0.0, raman.imag) / NT

    f32 = lambda a: np.ascontiguousarray(a, dtype=np.float32)
    return dict(
        to_ymode=widen(f32(to_ymode)),
        from_ymode=widen(f32(to_ymode.T)),
        to_xmode=widen(f32(to_xmode)),
        from_xmode=widen(f32(to_xmode.T)),
        lam_all=f32(lam_all),
        forward_split=split(f32(forward)),
        backward_split=split(f32(backward)),
        forward=f32(forward),
        backward=f32(backward),
        lines=f32(np.stack([tw_cos, tw_sin, w, ram_re, ram_im])),
    )


def split(table):
    high = table.astype(jnp.bfloat16)
    return np.stack([high, (table - high.astype(np.float32)).astype(jnp.bfloat16)])


def parts_of(value):
    high = value.astype(jnp.bfloat16)
    rest = value - high.astype(F32)
    middle = rest.astype(jnp.bfloat16)
    low = (rest - middle.astype(F32)).astype(jnp.bfloat16)
    return high, middle, low


def widen(table):
    high = table.astype(jnp.bfloat16)
    rest = table - high.astype(np.float32)
    middle = rest.astype(jnp.bfloat16)
    low = (rest - middle.astype(np.float32)).astype(jnp.bfloat16)
    return np.concatenate([high, middle, low, high, middle, high], axis=1)


def mm_wide(table, b):
    high, middle, low = parts_of(b)
    stacked = jnp.concatenate([high, high, high, middle, middle, low], axis=0)
    return jnp.dot(table, stacked, preferred_element_type=F32)


def mm_split(a, b_ref):
    high = a.astype(jnp.bfloat16)
    low = (a - high.astype(F32)).astype(jnp.bfloat16)
    dot = functools.partial(jnp.dot, preferred_element_type=F32)
    return dot(high, b_ref[0]) + (dot(high, b_ref[1]) + dot(low, b_ref[0]))


def mm(a, b):
    return jnp.dot(a, b, precision=HIGHEST, preferred_element_type=F32)


def fourier8(re, im, sign):
    def four(r, i):
        pr, pi = r[0] + r[2], i[0] + i[2]
        mr, mi = r[0] - r[2], i[0] - i[2]
        qr, qi = r[1] + r[3], i[1] + i[3]
        nr, ni = r[1] - r[3], i[1] - i[3]
        tr, ti = (-ni, nr) if sign > 0 else (ni, -nr)
        return (
            [pr + qr, mr + tr, pr - qr, mr - tr],
            [pi + qi, mi + ti, pi - qi, mi - ti],
        )

    er, ei = four(re[0::2], im[0::2])
    orr, oi = four(re[1::2], im[1::2])
    h = np.float32(np.sqrt(0.5))
    if sign > 0:
        w1 = ((orr[1] - oi[1]) * h, (orr[1] + oi[1]) * h)
        w2 = (-oi[2], orr[2])
        w3 = (-(orr[3] + oi[3]) * h, (orr[3] - oi[3]) * h)
    else:
        w1 = ((orr[1] + oi[1]) * h, (oi[1] - orr[1]) * h)
        w2 = (oi[2], -orr[2])
        w3 = ((oi[3] - orr[3]) * h, -(orr[3] + oi[3]) * h)
    tr = [orr[0], w1[0], w2[0], w3[0]]
    ti = [oi[0], w1[1], w2[1], w3[1]]
    out_r = [er[k] + tr[k] for k in range(4)] + [er[k] - tr[k] for k in range(4)]
    out_i = [ei[k] + ti[k] for k in range(4)] + [ei[k] - ti[k] for k in range(4)]
    return out_r, out_i


def outer_forward(load, rows, tw_ref, dest):
    for r0 in range(0, rows, 8):
        re = [load(0, r0, a) for a in range(NK)]
        im = [load(1, r0, a) for a in range(NK)]
        re, im = fourier8(re, im, -1)
        for k in range(NK):
            if k:
                c, s = tw_ref[0, k : k + 1, :], tw_ref[1, k : k + 1, :]
                re[k], im[k] = re[k] * c + im[k] * s, im[k] * c - re[k] * s
            dest[k * rows + r0 : k * rows + r0 + 8, 0:NB] = re[k]
            dest[k * rows + r0 : k * rows + r0 + 8, NB : 2 * NB] = im[k]


def outer_backward(src, rows, tw_ref, store):
    for r0 in range(0, rows, 8):
        re, im = [], []
        for k in range(NK):
            a = src[k * rows + r0 : k * rows + r0 + 8, 0:NB]
            b = src[k * rows + r0 : k * rows + r0 + 8, NB : 2 * NB]
            if k:
                c, s = tw_ref[0, k : k + 1, :], tw_ref[1, k : k + 1, :]
                a, b = a * c - b * s, a * s + b * c
            re.append(a)
            im.append(b)
        re, im = fourier8(re, im, 1)
        for a in range(NK):
            store(r0, a, re[a], im[a])


def filter_spectrum(spec, rows, factor_re, factor_im):
    for k in range(NK):
        fr, fi = factor_re[k : k + 1, :], factor_im[k : k + 1, :]
        lo, hi = k * rows, (k + 1) * rows
        a, b = spec[lo:hi, 0:NB], spec[lo:hi, NB : 2 * NB]
        spec[lo:hi, 0:NB] = a * fr - b * fi
        spec[lo:hi, NB : 2 * NB] = a * fi + b * fr


def ymode_kernel(
    seed_ref, mat_ref, lam_ref, kind_ref, disp_ref, gain_ref, sat_ref, kerr_ref, out_ref
):
    total = jnp.zeros((8, 128), F32)
    for c0 in range(0, NK, WIDE):
        block = seed_ref[:, c0 * 128 : (c0 + WIDE) * 128]
        square = block * block
        modes = mm_wide(mat_ref[...], block)
        for c in range(WIDE):
            lanes = slice(c * 128, c * 128 + 128)
            for r in range(16):
                total = total + square[8 * r : 8 * r + 8, lanes]
            place = 8 * (c0 + c)
            out_ref[:, place : place + 8, :] = modes[:, lanes].reshape(NS, 8, 128)
    row = lax.broadcasted_iota(jnp.int32, (8, 128), 0)
    chosen = lax.broadcasted_iota(jnp.int32, (1, 32), 1) == kind_ref[...]
    side = jnp.broadcast_to(jnp.sum(total, axis=0, keepdims=True), (8, 128))
    for place, ref in ((2, disp_ref), (3, gain_ref), (4, sat_ref), (5, kerr_ref)):
        value = jnp.sum(jnp.where(chosen, ref[...], 0.0), axis=1, keepdims=True)
        side = jnp.where(row == place, value, side)
    for d in range(NS):
        out_ref[d, 64:72, :] = jnp.where(row == 6, lam_ref[d : d + 1, :], side)


def xmode_kernel(in_ref, mat_ref, modes_ref, side_ref, tile_ref):
    square = jnp.zeros((128, 128), F32)
    for c0 in range(0, NK, WIDE):
        block = jnp.concatenate(
            [in_ref[:, 8 * c : 8 * c + 8, :].reshape(128, 128) for c in range(c0, c0 + WIDE)],
            axis=1,
        )
        modes = mm_wide(mat_ref[...], block)
        modes_ref[:, c0 * 128 : (c0 + WIDE) * 128] = modes
        for c in range(WIDE):
            square = square + modes[:, c * 128 : c * 128 + 128] ** 2
    weight = lax.dot_general(
        jnp.ones((8, 128), F32),
        square,
        (((1,), (1,)), ((), ())),
        precision=HIGHEST,
        preferred_element_type=F32,
    )
    side = in_ref[0, 64:72, :]
    energy = side
    for d in range(1, NS):
        energy = energy + in_ref[d, 64:72, :]
    row = lax.broadcasted_iota(jnp.int32, (8, 128), 0)
    side_ref[...] = jnp.where(row == 1, energy, side)
    lane = lax.broadcasted_iota(jnp.int32, (8, 128), 1)
    tile = jnp.where(lane < 64, weight + pltpu.roll(weight, 64, 1), side[5:6, :])
    for d in range(NS):
        tile_ref[d] = tile[0:1, :]


def turn(angle):
    count = jnp.floor(angle * np.float32(2.0 / np.pi) + 0.5)
    x = angle - count * 1.5703125
    x = x - count * 4.837512969970703e-4
    x = x - count * 7.549789948768648e-8
    x = jnp.clip(x, -0.8, 0.8)
    z = x * x
    sine = ((-1.9515295891e-4 * z + 8.3321608736e-3) * z - 1.6666654611e-1) * z * x + x
    cosine = ((2.443315711809948e-5 * z - 1.388731625493765e-3) * z + 4.166664568298827e-2) * z
    cosine = cosine * z - 0.5 * z + 1.0
    quarter = count.astype(jnp.int32)
    odd = (quarter & 1) == 1
    c, s = jnp.where(odd, sine, cosine), jnp.where(odd, cosine, sine)
    c = jnp.where(((quarter + 1) & 2) == 2, -c, c)
    s = jnp.where((quarter & 2) == 2, -s, s)
    return c, s


def whole_sum(value):
    return jnp.sum(jnp.sum(value, axis=0, keepdims=True), axis=1, keepdims=True)


def disperse_kernel(
    modes_ref, side_ref, tw_ref, fwd_ref, bwd_ref, out_ref, one, two
):

    def load(part, r0, a):
        return modes_ref[64 * part + r0 : 64 * part + r0 + 8, a * NB : (a + 1) * NB]

    outer_forward(load, 64, tw_ref, one)
    two[...] = mm(one[...], fwd_ref[...])

    energy = whole_sum(side_ref[1:2, :])
    dispersion, gain_peak = side_ref[2:3, :], side_ref[3:4, :]
    gain = gain_peak / (1.0 + energy / (NG * NG * NT) / side_ref[4:5, :])
    w = tw_ref[2]
    relative = w / gain_width
    amplitude = jnp.exp(0.5 * gain / (1.0 + relative * relative) - loss_rate) * (1.0 / NT)
    angle = disp_scale * dispersion * w * w
    filter_spectrum(two, 64, amplitude * jnp.cos(angle), amplitude * jnp.sin(angle))

    one[...] = mm(two[...], bwd_ref[...])

    def store(r0, a, re, im):
        out_ref[r0 : r0 + 8, a * NB : (a + 1) * NB] = re
        out_ref[64 + r0 : 64 + r0 + 8, a * NB : (a + 1) * NB] = im

    outer_backward(one, 64, tw_ref, store)


def small_product(a, b):
    total = a[:, 0:1] * b[0:1, :]
    for k in range(1, KRYLOV):
        total = total + a[:, k : k + 1] * b[k : k + 1, :]
    return total


def expanded_ratios():
    series = np.array([1.0 / math.factorial(k) for k in range(taylor_terms + 1)])
    series = series / 2.0 ** (EXPANDED * np.arange(taylor_terms + 1))
    for _ in range(EXPANDED):
        series = np.convolve(series, series)
    series = series[series >= np.finfo(np.float32).tiny]
    return [float(ratio) for ratio in series[1:] / series[:-1]]


def krylov_exp(diagonals, couplings):
    row = lax.broadcasted_iota(jnp.int32, (8, 128), 0)
    lane = lax.broadcasted_iota(jnp.int32, (8, 128), 1)
    zero = jnp.zeros((8, 128), F32)
    scale = step_length / 2.0 ** (squarings - EXPANDED)
    mid, low, high = zero, zero, zero
    for j in range(KRYLOV):
        mid = jnp.where(row == j, diagonals[j] * scale, mid)
        if j + 1 < KRYLOV:
            high = jnp.where(row == j, couplings[j] * scale, high)
            low = jnp.where(row == j + 1, couplings[j] * scale, low)
    term = jnp.where(row == lane, 1.0, 0.0).astype(F32)
    real, imag = term, zero
    for order, ratio in enumerate(expanded_ratios(), 1):
        term = mid * term + low * pltpu.roll(term, 1, 0) + high * pltpu.roll(term, 7, 0)
        term = term * ratio
        signed = -term if order % 4 in (2, 3) else term
        if order % 2:
            imag = imag + signed
        else:
            real = real + signed
    for _ in range(squarings - EXPANDED):
        real, imag = (
            small_product(real, real) - small_product(imag, imag),
            2.0 * small_product(real, imag),
        )
    return real, imag


def mode_gains(weight, lam, own):
    rest = jnp.sqrt(weight)
    grown = jnp.ones((8, 128), F32)
    diagonals, couplings, polys = [], [], []
    for step in range(KRYLOV):
        spread = lam * rest
        square = whole_sum(rest * rest) + epsilon
        diagonal = whole_sum(spread * rest)
        if step:
            overlap = whole_sum(rest * vector)
        inverse = lax.rsqrt(square)
        coupling = square * inverse
        diagonal = diagonal * inverse * inverse
        if step:
            diagonal = diagonal - overlap
        diagonals.append(diagonal)
        couplings.append(coupling)
        poly = grown * inverse
        polys.append(poly)
        if step + 1 < KRYLOV:
            rest = rest * inverse
            image = spread * inverse
            grown = own * poly
            if step:
                image = image - coupling * vector
                grown = grown - coupling * before
            vector, before = rest, poly
            rest = image - diagonal * vector
            grown = grown - diagonal * before
    scale_zero = couplings[0]
    real, imag = krylov_exp(diagonals, couplings[1:])
    gains = []
    for part in (real, imag):
        gain = part[0:1, 0:1] * polys[0]
        for j in range(1, KRYLOV):
            gain = gain + part[j : j + 1, 0:1] * polys[j]
        gains.append(gain * scale_zero)
    return gains


def propagate_kernel(side_ref, weight_ref, lam_ref, modes_ref, mat_ref, out_ref, scaled):
    own = jnp.broadcast_to(side_ref[6:7, :], (8, 128))
    lane = lax.broadcasted_iota(jnp.int32, (NS, 128), 1)
    weight = jnp.where(lane < 64, weight_ref[:, 0, :], 0.0)
    gains = mode_gains(weight, lam_ref[...], own)
    gain_re, gain_im = (
        jnp.broadcast_to(gain[0:1, :], (128, 128)).T[0:64, :] for gain in gains
    )
    for c0 in range(0, NK, WIDE):
        for c in range(c0, c0 + WIDE):
            lanes = slice(c * 128, c * 128 + 128)
            a, b = modes_ref[0:64, lanes], modes_ref[64:128, lanes]
            scaled[0:64, lanes] = gain_re * a - gain_im * b
            scaled[64:128, lanes] = gain_im * a + gain_re * b
        lanes = slice(c0 * 128, (c0 + WIDE) * 128)
        back = mm_wide(mat_ref[...], scaled[:, lanes])
        out_ref[:, :, lanes] = back.reshape(NS, 8, WIDE * 128)


def kerr_kernel(
    tile_ref, in_ref, mat_ref, tw_ref, fwd_ref, bwd_ref,
    out_ref, field, delayed, one, two, done, sems
):
    kerr = tile_ref[0, 0:1, 64:65]
    field[...] = mm_wide(mat_ref[...], in_ref[...].reshape(128, NT))

    def load(side, r0, a):
        lanes = slice(a * NB, (a + 1) * NB)
        re = field[32 * side + r0 : 32 * side + r0 + 8, lanes]
        im = field[64 + 32 * side + r0 : 64 + 32 * side + r0 + 8, lanes]
        return re * re + im * im

    outer_forward(load, 32, tw_ref, one)
    two[...] = mm_split(one[...], fwd_ref)
    filter_spectrum(two, 32, tw_ref[3], tw_ref[4])
    one[...] = mm_split(two[...], bwd_ref)

    def store(r0, a, re, im):
        lanes = slice(a * NB, (a + 1) * NB)
        delayed[r0 : r0 + 8, lanes] = re
        delayed[32 + r0 : 32 + r0 + 8, lanes] = im

    outer_backward(one, 32, tw_ref, store)

    copies = []
    for r0 in range(0, 64, 8):
        re, im = field[r0 : r0 + 8, :], field[64 + r0 : 64 + r0 + 8, :]
        late = delayed[r0 : r0 + 8, :]
        rotation = kerr * ((1.0 - raman_share) * (re * re + im * im) + raman_share * late)
        c, s = turn(rotation)
        done[r0 : r0 + 8, :] = re * c - im * s
        done[64 + r0 : 64 + r0 + 8, :] = re * s + im * c
        if r0 % 16 == 8:
            for lo in (r0 - 8, 64 + r0 - 8):
                rows = pl.ds(lo, 16)
                copy = pltpu.make_async_copy(done.at[rows], out_ref.at[rows], sems.at[lo // 16])
                copy.start()
                copies.append(copy)
    for copy in copies:
        copy.wait()


VMEM = pl.BlockSpec(memory_space=pltpu.VMEM)
HBM = pl.BlockSpec(memory_space=pltpu.HBM)


def near(*shape):
    return pltpu.VMEM(shape, F32)


def hold(value):
    return pltpu.with_memory_space_constraint(value, pltpu.VMEM)


def cost(flops, moved):
    return pl.CostEstimate(flops=flops, bytes_accessed=moved, transcendentals=0)


def exchange(value):
    return lax.all_to_all(value, "shard", split_axis=0, concat_axis=0, tiled=True)


def pass_on(value):
    count = lax.axis_size("blk")
    return lax.ppermute(value, "blk", [(b, (b + 1) % count) for b in range(count)])


def per_device(seed_field, segment_order, seg_disp, seg_kerr, seg_gain, seg_sat):
    t = tables()
    near_tables = {name: hold(jnp.asarray(value)) for name, value in t.items()}
    seed = seed_field.reshape(128, NT)

    ymodes = pl.pallas_call(
        ymode_kernel,
        out_shape=near(NS, 72, 128),
        in_specs=[VMEM] * 8,
        out_specs=VMEM,
        name="ymode",
    )(
        seed, t["to_ymode"], t["lam_all"], segment_order.reshape(1, 1),
        *(each.reshape(1, 32) for each in (seg_disp, seg_gain, seg_sat, seg_kerr)),
    )
    gathered = exchange(ymodes)
    modes, side, tile = pl.pallas_call(
        xmode_kernel,
        out_shape=(near(128, NT), near(8, 128), near(NS, 1, 128)),
        in_specs=[VMEM] * 2,
        out_specs=(VMEM,) * 3,
        name="xmode",
    )(hold(gathered), near_tables["to_xmode"])
    shifted = pass_on(tile)
    modes = pl.pallas_call(
        disperse_kernel,
        out_shape=near(128, NT),
        in_specs=[VMEM] * 5,
        out_specs=VMEM,
        scratch_shapes=[pltpu.VMEM((512, 256), F32)] * 2,
        cost_estimate=cost(6 * 4 * 512 * 256 * 256, 2**20),
        name="disperse",
    )(
        hold(modes), hold(side),
        *(near_tables[name] for name in ("lines", "forward", "backward")),
    )
    modes, shifted = lax.optimization_barrier((modes, shifted))
    modes = pass_on(modes)
    weights = exchange(shifted)
    xback = pl.pallas_call(
        propagate_kernel,
        out_shape=near(NS, 8, NT),
        in_specs=[VMEM] * 5,
        out_specs=VMEM,
        scratch_shapes=[pltpu.VMEM((128, NT), F32)],
        name="propagate",
    )(
        hold(side), hold(weights), near_tables["lam_all"], hold(modes),
        near_tables["from_xmode"],
    )
    rows = exchange(xback)
    result = pl.pallas_call(
        kerr_kernel,
        out_shape=jax.ShapeDtypeStruct((128, NT), F32),
        in_specs=[VMEM] * 6,
        out_specs=HBM,
        scratch_shapes=[pltpu.VMEM((128, NT), F32), pltpu.VMEM((64, NT), F32)]
        + [pltpu.VMEM((256, 256), F32)] * 2
        + [pltpu.VMEM((128, NT), F32), pltpu.SemaphoreType.DMA((8,))],
        name="kerr",
    )(
        hold(shifted), hold(rows),
        *(
            near_tables[name]
            for name in ("from_ymode", "lines", "forward_split", "backward_split")
        ),
    )
    return result.reshape(seed_field.shape)


def solution(mesh):
    in_specs = (P("blk", None, "shard", None, None), P("blk"), P(), P(), P(), P())
    out_specs = P("blk", None, "shard", None, None)
    return jax.shard_map(
        per_device, mesh=mesh, in_specs=in_specs, out_specs=out_specs, check_vma=False
    )
```

```python
import functools
import math

import jax
import jax.numpy as jnp
import numpy as np
from jax import lax
from jax.experimental import pallas as pl
from jax.experimental.pallas import tpu as pltpu
from jax.sharding import PartitionSpec as P

KRYLOV = 8
EXPANDED = 6
NS = 16
NG = 32
NT = 1024
NK = 8
WIDE = 2
NB = 128

epsilon = 1e-06
step_length = 2.5
grin_depth = 1.5
squarings = 8
taylor_terms = 10
gain_width = 0.25
loss_rate = 0.5
disp_scale = 60.0
raman_share = 0.18
raman_freq = 0.05
raman_damp = 0.035

F32 = jnp.float32
HIGHEST = lax.Precision.HIGHEST


@functools.cache
def tables():
    cell = (np.arange(NG) - (NG - 1) / 2.0) / (NG / 2.0)
    line = np.diag(-grin_depth * cell * cell)
    line = line + 0.5 * (np.eye(NG, k=1) + np.eye(NG, k=-1))
    values, q = np.linalg.eigh(line)

    to_ymode = np.zeros((NS, 2, 2, 2, 2, 2, NG))
    to_xmode = np.zeros((2, 2, NG, NS, 2, 2, 2))
    for part in range(2):
        for side in range(2):
            for jj in range(2):
                to_ymode[:, part, jj, side, part, side, :] = q[:, jj::2].T
                to_xmode[part, jj, :, :, part, jj, side] = q[side::2, :].T
    to_ymode = to_ymode.reshape(128, 128)
    to_xmode = to_xmode.reshape(128, 128)

    pair = values.reshape(NS, 2)
    lam = pair[:, None, :, None] + values[None, None, None, :] + np.zeros((1, 2, 1, 1))
    lam_all = lam.reshape(NS, 128)

    inner = np.arange(NB)
    angle = 2.0 * np.pi * ((inner[:, None] * inner[None, :]) % NB) / NB
    c, s = np.cos(angle), np.sin(angle)
    forward = np.block([[c, -s], [s, c]])
    backward = np.block([[c, s], [-s, c]])
    turn = 2.0 * np.pi * (np.arange(NK)[:, None] * inner[None, :]) / NT
    tw_cos, tw_sin = np.cos(turn), np.sin(turn)

    freq = np.arange(NK)[:, None] + NK * inner[None, :]
    signed = np.where(freq >= NT // 2, freq - NT, freq)
    w = signed / (NT / 2.0)
    resonance = raman_freq * raman_freq
    raman = resonance / (resonance - w * w - 1j * raman_damp * w)
    ram_re = raman.real / NT
    ram_im = np.where(signed == -(NT // 2), 0.0, raman.imag) / NT

    f32 = lambda a: np.ascontiguousarray(a, dtype=np.float32)
    return dict(
        to_ymode=widen(f32(to_ymode)),
        from_ymode=widen(f32(to_ymode.T)),
        to_xmode=widen(f32(to_xmode)),
        from_xmode=widen(f32(to_xmode.T)),
        lam_all=f32(lam_all),
        forward_split=split(f32(forward)),
        backward_split=split(f32(backward)),
        forward=f32(forward),
        backward=f32(backward),
        lines=f32(np.stack([tw_cos, tw_sin, w, ram_re, ram_im])),
    )


def split(table):
    high = table.astype(jnp.bfloat16)
    return np.stack([high, (table - high.astype(np.float32)).astype(jnp.bfloat16)])


def parts_of(value):
    high = value.astype(jnp.bfloat16)
    rest = value - high.astype(F32)
    middle = rest.astype(jnp.bfloat16)
    low = (rest - middle.astype(F32)).astype(jnp.bfloat16)
    return high, middle, low


def widen(table):
    high = table.astype(jnp.bfloat16)
    rest = table - high.astype(np.float32)
    middle = rest.astype(jnp.bfloat16)
    low = (rest - middle.astype(np.float32)).astype(jnp.bfloat16)
    return np.concatenate([high, middle, low, high, middle, high], axis=1)


def mm_wide(table, b):
    high, middle, low = parts_of(b)
    stacked = jnp.concatenate([high, high, high, middle, middle, low], axis=0)
    return jnp.dot(table, stacked, preferred_element_type=F32)


def mm_split(a, b_ref):
    high = a.astype(jnp.bfloat16)
    low = (a - high.astype(F32)).astype(jnp.bfloat16)
    dot = functools.partial(jnp.dot, preferred_element_type=F32)
    return dot(high, b_ref[0]) + (dot(high, b_ref[1]) + dot(low, b_ref[0]))


def mm(a, b):
    return jnp.dot(a, b, precision=HIGHEST, preferred_element_type=F32)


def fourier8(re, im, sign):
    def four(r, i):
        pr, pi = r[0] + r[2], i[0] + i[2]
        mr, mi = r[0] - r[2], i[0] - i[2]
        qr, qi = r[1] + r[3], i[1] + i[3]
        nr, ni = r[1] - r[3], i[1] - i[3]
        tr, ti = (-ni, nr) if sign > 0 else (ni, -nr)
        return (
            [pr + qr, mr + tr, pr - qr, mr - tr],
            [pi + qi, mi + ti, pi - qi, mi - ti],
        )

    er, ei = four(re[0::2], im[0::2])
    orr, oi = four(re[1::2], im[1::2])
    h = np.float32(np.sqrt(0.5))
    if sign > 0:
        w1 = ((orr[1] - oi[1]) * h, (orr[1] + oi[1]) * h)
        w2 = (-oi[2], orr[2])
        w3 = (-(orr[3] + oi[3]) * h, (orr[3] - oi[3]) * h)
    else:
        w1 = ((orr[1] + oi[1]) * h, (oi[1] - orr[1]) * h)
        w2 = (oi[2], -orr[2])
        w3 = ((oi[3] - orr[3]) * h, -(orr[3] + oi[3]) * h)
    tr = [orr[0], w1[0], w2[0], w3[0]]
    ti = [oi[0], w1[1], w2[1], w3[1]]
    out_r = [er[k] + tr[k] for k in range(4)] + [er[k] - tr[k] for k in range(4)]
    out_i = [ei[k] + ti[k] for k in range(4)] + [ei[k] - ti[k] for k in range(4)]
    return out_r, out_i


def outer_forward(load, rows, tw_ref, dest):
    for r0 in range(0, rows, 8):
        re = [load(0, r0, a) for a in range(NK)]
        im = [load(1, r0, a) for a in range(NK)]
        re, im = fourier8(re, im, -1)
        for k in range(NK):
            if k:
                c, s = tw_ref[0, k : k + 1, :], tw_ref[1, k : k + 1, :]
                re[k], im[k] = re[k] * c + im[k] * s, im[k] * c - re[k] * s
            dest[k * rows + r0 : k * rows + r0 + 8, 0:NB] = re[k]
            dest[k * rows + r0 : k * rows + r0 + 8, NB : 2 * NB] = im[k]


def outer_backward(src, rows, tw_ref, store):
    for r0 in range(0, rows, 8):
        re, im = [], []
        for k in range(NK):
            a = src[k * rows + r0 : k * rows + r0 + 8, 0:NB]
            b = src[k * rows + r0 : k * rows + r0 + 8, NB : 2 * NB]
            if k:
                c, s = tw_ref[0, k : k + 1, :], tw_ref[1, k : k + 1, :]
                a, b = a * c - b * s, a * s + b * c
            re.append(a)
            im.append(b)
        re, im = fourier8(re, im, 1)
        for a in range(NK):
            store(r0, a, re[a], im[a])


def filter_spectrum(spec, rows, factor_re, factor_im):
    for k in range(NK):
        fr, fi = factor_re[k : k + 1, :], factor_im[k : k + 1, :]
        lo, hi = k * rows, (k + 1) * rows
        a, b = spec[lo:hi, 0:NB], spec[lo:hi, NB : 2 * NB]
        spec[lo:hi, 0:NB] = a * fr - b * fi
        spec[lo:hi, NB : 2 * NB] = a * fi + b * fr


def whole_sum(value):
    return jnp.sum(jnp.sum(value, axis=0, keepdims=True), axis=1, keepdims=True)


def ymode_kernel(
    seed_ref, mat_ref, lam_ref, kind_ref, disp_ref, gain_ref, sat_ref, kerr_ref, out_ref
):
    total = jnp.zeros((8, 128), F32)
    for c0 in range(0, NK, WIDE):
        block = seed_ref[:, c0 * 128 : (c0 + WIDE) * 128]
        square = block * block
        modes = mm_wide(mat_ref[...], block)
        for c in range(WIDE):
            lanes = slice(c * 128, c * 128 + 128)
            for r in range(16):
                total = total + square[8 * r : 8 * r + 8, lanes]
            place = 8 * (c0 + c)
            for d in range(NS):
                out_ref[d, place : place + 8, 0, :] = modes[8 * d : 8 * d + 8, lanes]
    lane = lax.broadcasted_iota(jnp.int32, (NS, 128), 1)
    chosen = lax.broadcasted_iota(jnp.int32, (1, 32), 1) == kind_ref[...]
    side = jnp.where(lane < 64, lam_ref[...], whole_sum(total))
    for place, ref in ((65, disp_ref), (66, gain_ref), (67, sat_ref), (68, kerr_ref)):
        value = jnp.sum(jnp.where(chosen, ref[...], 0.0), axis=1, keepdims=True)
        side = jnp.where(lane == place, value, side)
    out_ref[:, 64, 0, :] = side


def xmode_kernel(in_ref, mat_ref, modes_ref, side_ref, tile_ref):
    square = jnp.zeros((128, 128), F32)
    for c0 in range(0, NK, WIDE):
        block = jnp.concatenate(
            [
                jnp.concatenate([in_ref[d, 8 * c : 8 * c + 8, 0, :] for d in range(NS)], axis=0)
                for c in range(c0, c0 + WIDE)
            ],
            axis=1,
        )
        modes = mm_wide(mat_ref[...], block)
        modes_ref[:, c0 * 128 : (c0 + WIDE) * 128] = modes
        for c in range(WIDE):
            square = square + modes[:, c * 128 : c * 128 + 128] ** 2
    weight = lax.dot_general(
        jnp.ones((8, 128), F32),
        square,
        (((1,), (1,)), ((), ())),
        precision=HIGHEST,
        preferred_element_type=F32,
    )
    lane = lax.broadcasted_iota(jnp.int32, (1, 128), 1)
    sides = in_ref[:, 64, 0, :]
    side = jnp.where(lane == 64, jnp.sum(sides, axis=0, keepdims=True), sides[0:1, :])
    side_ref[...] = jnp.broadcast_to(side, (8, 128))
    tile = jnp.where(lane < 64, (weight + pltpu.roll(weight, 64, 1))[0:1, :], side[:, 68:69])
    for d in range(NS):
        tile_ref[d] = tile[0:1, :]


def turn(angle):
    count = jnp.floor(angle * np.float32(2.0 / np.pi) + 0.5)
    x = angle - count * 1.5703125
    x = x - count * 4.837512969970703e-4
    x = x - count * 7.549789948768648e-8
    x = jnp.clip(x, -0.8, 0.8)
    z = x * x
    sine = ((-1.9515295891e-4 * z + 8.3321608736e-3) * z - 1.6666654611e-1) * z * x + x
    cosine = ((2.443315711809948e-5 * z - 1.388731625493765e-3) * z + 4.166664568298827e-2) * z
    cosine = cosine * z - 0.5 * z + 1.0
    quarter = count.astype(jnp.int32)
    odd = (quarter & 1) == 1
    c, s = jnp.where(odd, sine, cosine), jnp.where(odd, cosine, sine)
    c = jnp.where(((quarter + 1) & 2) == 2, -c, c)
    s = jnp.where((quarter & 2) == 2, -s, s)
    return c, s


def disperse_kernel(
    modes_ref, side_ref, tw_ref, fwd_ref, bwd_ref, out_ref, one, two
):

    def load(part, r0, a):
        return modes_ref[64 * part + r0 : 64 * part + r0 + 8, a * NB : (a + 1) * NB]

    outer_forward(load, 64, tw_ref, one)
    two[...] = mm(one[...], fwd_ref[...])

    energy = side_ref[0:1, 64:65]
    dispersion, gain_peak = side_ref[0:1, 65:66], side_ref[0:1, 66:67]
    gain = gain_peak / (1.0 + energy / (NG * NG * NT) / side_ref[0:1, 67:68])
    w = tw_ref[2]
    relative = w / gain_width
    amplitude = jnp.exp(0.5 * gain / (1.0 + relative * relative) - loss_rate) * (1.0 / NT)
    angle = disp_scale * dispersion * w * w
    filter_spectrum(two, 64, amplitude * jnp.cos(angle), amplitude * jnp.sin(angle))

    one[...] = mm(two[...], bwd_ref[...])

    def store(r0, a, re, im):
        out_ref[r0 : r0 + 8, a * NB : (a + 1) * NB] = re
        out_ref[64 + r0 : 64 + r0 + 8, a * NB : (a + 1) * NB] = im

    outer_backward(one, 64, tw_ref, store)


def small_product(a, b):
    total = a[:, 0:1] * b[0:1, :]
    for k in range(1, KRYLOV):
        total = total + a[:, k : k + 1] * b[k : k + 1, :]
    return total


def expanded_ratios():
    series = np.array([1.0 / math.factorial(k) for k in range(taylor_terms + 1)])
    series = series / 2.0 ** (EXPANDED * np.arange(taylor_terms + 1))
    for _ in range(EXPANDED):
        series = np.convolve(series, series)
    series = series[series >= np.finfo(np.float32).tiny]
    return [float(ratio) for ratio in series[1:] / series[:-1]]


def krylov_exp(diagonals, couplings):
    row = lax.broadcasted_iota(jnp.int32, (8, 128), 0)
    lane = lax.broadcasted_iota(jnp.int32, (8, 128), 1)
    zero = jnp.zeros((8, 128), F32)
    scale = step_length / 2.0 ** (squarings - EXPANDED)
    mid, low, high = zero, zero, zero
    for j in range(KRYLOV):
        mid = jnp.where(row == j, diagonals[j] * scale, mid)
        if j + 1 < KRYLOV:
            high = jnp.where(row == j, couplings[j] * scale, high)
            low = jnp.where(row == j + 1, couplings[j] * scale, low)
    term = jnp.where(row == lane, 1.0, 0.0).astype(F32)
    real, imag = term, zero
    for order, ratio in enumerate(expanded_ratios(), 1):
        term = mid * term + low * pltpu.roll(term, 1, 0) + high * pltpu.roll(term, 7, 0)
        term = term * ratio
        signed = -term if order % 4 in (2, 3) else term
        if order % 2:
            imag = imag + signed
        else:
            real = real + signed
    for _ in range(squarings - EXPANDED):
        real, imag = (
            small_product(real, real) - small_product(imag, imag),
            2.0 * small_product(real, imag),
        )
    return real, imag


def mode_gains(weight, lam, own):
    rest = jnp.sqrt(weight)
    grown = jnp.ones((8, 128), F32)
    diagonals, couplings, polys = [], [], []
    for step in range(KRYLOV):
        spread = lam * rest
        square = whole_sum(rest * rest) + epsilon
        diagonal = whole_sum(spread * rest)
        if step:
            overlap = whole_sum(rest * vector)
        inverse = lax.rsqrt(square)
        coupling = square * inverse
        diagonal = diagonal * inverse * inverse
        if step:
            diagonal = diagonal - overlap
        diagonals.append(diagonal)
        couplings.append(coupling)
        poly = grown * inverse
        polys.append(poly)
        if step + 1 < KRYLOV:
            rest = rest * inverse
            image = spread * inverse
            grown = own * poly
            if step:
                image = image - coupling * vector
                grown = grown - coupling * before
            vector, before = rest, poly
            rest = image - diagonal * vector
            grown = grown - diagonal * before
    scale_zero = couplings[0]
    real, imag = krylov_exp(diagonals, couplings[1:])
    gains = []
    for part in (real, imag):
        gain = part[0:1, 0:1] * polys[0]
        for j in range(1, KRYLOV):
            gain = gain + part[j : j + 1, 0:1] * polys[j]
        gains.append(gain * scale_zero)
    return gains


def propagate_kernel(side_ref, weight_ref, lam_ref, modes_ref, mat_ref, out_ref, scaled):
    lane = lax.broadcasted_iota(jnp.int32, (NS, 128), 1)
    own = jnp.where(lane[0:8, :] < 64, side_ref[...], pltpu.roll(side_ref[...], 64, 1))
    weight = jnp.where(lane < 64, weight_ref[:, 0, :], 0.0)
    gains = mode_gains(weight, lam_ref[...], own)
    gain_re, gain_im = (
        jnp.broadcast_to(gain[0:1, :], (128, 128)).T[0:64, :] for gain in gains
    )
    for c0 in range(0, NK, WIDE):
        for c in range(c0, c0 + WIDE):
            lanes = slice(c * 128, c * 128 + 128)
            a, b = modes_ref[0:64, lanes], modes_ref[64:128, lanes]
            scaled[0:64, lanes] = gain_re * a - gain_im * b
            scaled[64:128, lanes] = gain_im * a + gain_re * b
        lanes = slice(c0 * 128, (c0 + WIDE) * 128)
        back = mm_wide(mat_ref[...], scaled[:, lanes])
        out_ref[:, :, lanes] = back.reshape(NS, 8, WIDE * 128)


def kerr_kernel(
    tile_ref, in_ref, mat_ref, tw_ref, fwd_ref, bwd_ref,
    out_ref, field, delayed, one, two, done, sems
):
    kerr = tile_ref[0, 0:1, 64:65]
    field[...] = mm_wide(mat_ref[...], in_ref[...].reshape(128, NT))

    def load(side, r0, a):
        lanes = slice(a * NB, (a + 1) * NB)
        re = field[32 * side + r0 : 32 * side + r0 + 8, lanes]
        im = field[64 + 32 * side + r0 : 64 + 32 * side + r0 + 8, lanes]
        return re * re + im * im

    outer_forward(load, 32, tw_ref, one)
    two[...] = mm_split(one[...], fwd_ref)
    filter_spectrum(two, 32, tw_ref[3], tw_ref[4])
    one[...] = mm_split(two[...], bwd_ref)

    def store(r0, a, re, im):
        lanes = slice(a * NB, (a + 1) * NB)
        delayed[r0 : r0 + 8, lanes] = re
        delayed[32 + r0 : 32 + r0 + 8, lanes] = im

    outer_backward(one, 32, tw_ref, store)

    copies = []
    for r0 in range(0, 64, 8):
        re, im = field[r0 : r0 + 8, :], field[64 + r0 : 64 + r0 + 8, :]
        late = delayed[r0 : r0 + 8, :]
        rotation = kerr * ((1.0 - raman_share) * (re * re + im * im) + raman_share * late)
        c, s = turn(rotation)
        done[r0 : r0 + 8, :] = re * c - im * s
        done[64 + r0 : 64 + r0 + 8, :] = re * s + im * c
        if r0 % 16 == 8:
            for lo in (r0 - 8, 64 + r0 - 8):
                rows = pl.ds(lo, 16)
                copy = pltpu.make_async_copy(done.at[rows], out_ref.at[rows], sems.at[lo // 16])
                copy.start()
                copies.append(copy)
    for copy in copies:
        copy.wait()


VMEM = pl.BlockSpec(memory_space=pltpu.VMEM)
HBM = pl.BlockSpec(memory_space=pltpu.HBM)


def near(*shape):
    return pltpu.VMEM(shape, F32)


def hold(value):
    return pltpu.with_memory_space_constraint(value, pltpu.VMEM)


def cost(flops, moved):
    return pl.CostEstimate(flops=flops, bytes_accessed=moved, transcendentals=0)


def exchange(value):
    return lax.all_to_all(value, "shard", split_axis=0, concat_axis=0, tiled=True)


def pass_on(value):
    count = lax.axis_size("blk")
    return lax.ppermute(value, "blk", [(b, (b + 1) % count) for b in range(count)])


def per_device(seed_field, segment_order, seg_disp, seg_kerr, seg_gain, seg_sat):
    t = tables()
    near_tables = {name: hold(jnp.asarray(value)) for name, value in t.items()}
    seed = seed_field.reshape(128, NT)

    ymodes = pl.pallas_call(
        ymode_kernel,
        out_shape=near(NS, 65, 1, 128),
        in_specs=[VMEM] * 8,
        out_specs=VMEM,
        name="ymode",
    )(
        seed, t["to_ymode"], t["lam_all"], segment_order.reshape(1, 1),
        *(each.reshape(1, 32) for each in (seg_disp, seg_gain, seg_sat, seg_kerr)),
    )
    gathered = exchange(ymodes)
    modes, side, tile = pl.pallas_call(
        xmode_kernel,
        out_shape=(near(128, NT), near(8, 128), near(NS, 1, 128)),
        in_specs=[VMEM] * 2,
        out_specs=(VMEM,) * 3,
        name="xmode",
    )(hold(gathered), near_tables["to_xmode"])
    shifted = pass_on(tile)
    modes = pl.pallas_call(
        disperse_kernel,
        out_shape=near(128, NT),
        in_specs=[VMEM] * 5,
        out_specs=VMEM,
        scratch_shapes=[pltpu.VMEM((512, 256), F32)] * 2,
        cost_estimate=cost(6 * 4 * 512 * 256 * 256, 2**20),
        name="disperse",
    )(
        hold(modes), hold(side),
        *(near_tables[name] for name in ("lines", "forward", "backward")),
    )
    modes, shifted = lax.optimization_barrier((modes, shifted))
    modes = pass_on(modes)
    weights = exchange(shifted)
    xback = pl.pallas_call(
        propagate_kernel,
        out_shape=near(NS, 8, NT),
        in_specs=[VMEM] * 5,
        out_specs=VMEM,
        scratch_shapes=[pltpu.VMEM((128, NT), F32)],
        name="propagate",
    )(
        hold(side), hold(weights), near_tables["lam_all"], hold(modes),
        near_tables["from_xmode"],
    )
    rows = exchange(xback)
    result = pl.pallas_call(
        kerr_kernel,
        out_shape=jax.ShapeDtypeStruct((128, NT), F32),
        in_specs=[VMEM] * 6,
        out_specs=HBM,
        scratch_shapes=[pltpu.VMEM((128, NT), F32), pltpu.VMEM((64, NT), F32)]
        + [pltpu.VMEM((256, 256), F32)] * 2
        + [pltpu.VMEM((128, NT), F32), pltpu.SemaphoreType.DMA((8,))],
        name="kerr",
    )(
        hold(shifted), hold(rows),
        *(
            near_tables[name]
            for name in ("from_ymode", "lines", "forward_split", "backward_split")
        ),
    )
    return result.reshape(seed_field.shape)


def solution(mesh):
    in_specs = (P("blk", None, "shard", None, None), P("blk"), P(), P(), P(), P())
    out_specs = P("blk", None, "shard", None, None)
    return jax.shard_map(
        per_device, mesh=mesh, in_specs=in_specs, out_specs=out_specs, check_vma=False
    )
```

```python
import functools
import math

import jax
import jax.numpy as jnp
import numpy as np
from jax import lax
from jax.experimental import pallas as pl
from jax.experimental.pallas import tpu as pltpu
from jax.sharding import PartitionSpec as P

KRYLOV = 8
EXPANDED = 6
NS = 16
NG = 32
NT = 1024
NK = 8
WIDE = 2
NB = 128

epsilon = 1e-06
step_length = 2.5
grin_depth = 1.5
squarings = 8
taylor_terms = 10
gain_width = 0.25
loss_rate = 0.5
disp_scale = 60.0
raman_share = 0.18
raman_freq = 0.05
raman_damp = 0.035

F32 = jnp.float32
HIGHEST = lax.Precision.HIGHEST


@functools.cache
def tables():
    cell = (np.arange(NG) - (NG - 1) / 2.0) / (NG / 2.0)
    line = np.diag(-grin_depth * cell * cell)
    line = line + 0.5 * (np.eye(NG, k=1) + np.eye(NG, k=-1))
    values, q = np.linalg.eigh(line)

    to_ymode = np.zeros((NS, 2, 2, 2, 2, 2, NG))
    to_xmode = np.zeros((2, 2, NG, NS, 2, 2, 2))
    for part in range(2):
        for side in range(2):
            for jj in range(2):
                to_ymode[:, part, jj, side, part, side, :] = q[:, jj::2].T
                to_xmode[part, jj, :, :, part, jj, side] = q[side::2, :].T
    to_ymode = to_ymode.reshape(128, 128)
    to_xmode = to_xmode.reshape(128, 128)

    pair = values.reshape(NS, 2)
    lam = pair[:, None, :, None] + values[None, None, None, :] + np.zeros((1, 2, 1, 1))
    lam_all = lam.reshape(NS, 128)

    inner = np.arange(NB)
    angle = 2.0 * np.pi * ((inner[:, None] * inner[None, :]) % NB) / NB
    c, s = np.cos(angle), np.sin(angle)
    forward = np.block([[c, -s], [s, c]])
    backward = np.block([[c, s], [-s, c]])
    turn = 2.0 * np.pi * (np.arange(NK)[:, None] * inner[None, :]) / NT
    tw_cos, tw_sin = np.cos(turn), np.sin(turn)

    freq = np.arange(NK)[:, None] + NK * inner[None, :]
    signed = np.where(freq >= NT // 2, freq - NT, freq)
    w = signed / (NT / 2.0)
    resonance = raman_freq * raman_freq
    raman = resonance / (resonance - w * w - 1j * raman_damp * w)
    ram_re = raman.real / NT
    ram_im = np.where(signed == -(NT // 2), 0.0, raman.imag) / NT

    f32 = lambda a: np.ascontiguousarray(a, dtype=np.float32)
    return dict(
        to_ymode=widen(f32(to_ymode)),
        from_ymode=widen(f32(to_ymode.T)),
        to_xmode=widen(f32(to_xmode)),
        from_xmode=widen(f32(to_xmode.T)),
        lam_all=f32(lam_all),
        forward_split=split(f32(forward)),
        backward_split=split(f32(backward)),
        forward=f32(forward),
        backward=f32(backward),
        lines=f32(np.stack([tw_cos, tw_sin, w, ram_re, ram_im])),
    )


def split(table):
    high = table.astype(jnp.bfloat16)
    return np.stack([high, (table - high.astype(np.float32)).astype(jnp.bfloat16)])


def parts_of(value):
    high = value.astype(jnp.bfloat16)
    rest = value - high.astype(F32)
    middle = rest.astype(jnp.bfloat16)
    low = (rest - middle.astype(F32)).astype(jnp.bfloat16)
    return high, middle, low


def widen(table):
    high = table.astype(jnp.bfloat16)
    rest = table - high.astype(np.float32)
    middle = rest.astype(jnp.bfloat16)
    low = (rest - middle.astype(np.float32)).astype(jnp.bfloat16)
    return np.concatenate([high, middle, low, high, middle, high], axis=1)


def mm_wide(table, b):
    high, middle, low = parts_of(b)
    stacked = jnp.concatenate([high, high, high, middle, middle, low], axis=0)
    return jnp.dot(table, stacked, preferred_element_type=F32)


def mm_split(a, b_ref):
    high = a.astype(jnp.bfloat16)
    low = (a - high.astype(F32)).astype(jnp.bfloat16)
    dot = functools.partial(jnp.dot, preferred_element_type=F32)
    return dot(high, b_ref[0]) + (dot(high, b_ref[1]) + dot(low, b_ref[0]))


def mm(a, b):
    return jnp.dot(a, b, precision=HIGHEST, preferred_element_type=F32)


def fourier8(re, im, sign):
    def four(r, i):
        pr, pi = r[0] + r[2], i[0] + i[2]
        mr, mi = r[0] - r[2], i[0] - i[2]
        qr, qi = r[1] + r[3], i[1] + i[3]
        nr, ni = r[1] - r[3], i[1] - i[3]
        tr, ti = (-ni, nr) if sign > 0 else (ni, -nr)
        return (
            [pr + qr, mr + tr, pr - qr, mr - tr],
            [pi + qi, mi + ti, pi - qi, mi - ti],
        )

    er, ei = four(re[0::2], im[0::2])
    orr, oi = four(re[1::2], im[1::2])
    h = np.float32(np.sqrt(0.5))
    if sign > 0:
        w1 = ((orr[1] - oi[1]) * h, (orr[1] + oi[1]) * h)
        w2 = (-oi[2], orr[2])
        w3 = (-(orr[3] + oi[3]) * h, (orr[3] - oi[3]) * h)
    else:
        w1 = ((orr[1] + oi[1]) * h, (oi[1] - orr[1]) * h)
        w2 = (oi[2], -orr[2])
        w3 = ((oi[3] - orr[3]) * h, -(orr[3] + oi[3]) * h)
    tr = [orr[0], w1[0], w2[0], w3[0]]
    ti = [oi[0], w1[1], w2[1], w3[1]]
    out_r = [er[k] + tr[k] for k in range(4)] + [er[k] - tr[k] for k in range(4)]
    out_i = [ei[k] + ti[k] for k in range(4)] + [ei[k] - ti[k] for k in range(4)]
    return out_r, out_i


def outer_forward(load, rows, tw_ref, dest):
    for r0 in range(0, rows, 8):
        re = [load(0, r0, a) for a in range(NK)]
        im = [load(1, r0, a) for a in range(NK)]
        re, im = fourier8(re, im, -1)
        for k in range(NK):
            if k:
                c, s = tw_ref[0, k : k + 1, :], tw_ref[1, k : k + 1, :]
                re[k], im[k] = re[k] * c + im[k] * s, im[k] * c - re[k] * s
            dest[k * rows + r0 : k * rows + r0 + 8, 0:NB] = re[k]
            dest[k * rows + r0 : k * rows + r0 + 8, NB : 2 * NB] = im[k]


def outer_backward(src, rows, tw_ref, store):
    for r0 in range(0, rows, 8):
        re, im = [], []
        for k in range(NK):
            a = src[k * rows + r0 : k * rows + r0 + 8, 0:NB]
            b = src[k * rows + r0 : k * rows + r0 + 8, NB : 2 * NB]
            if k:
                c, s = tw_ref[0, k : k + 1, :], tw_ref[1, k : k + 1, :]
                a, b = a * c - b * s, a * s + b * c
            re.append(a)
            im.append(b)
        re, im = fourier8(re, im, 1)
        for a in range(NK):
            store(r0, a, re[a], im[a])


def filter_spectrum(spec, rows, factor_re, factor_im):
    for k in range(NK):
        fr, fi = factor_re[k : k + 1, :], factor_im[k : k + 1, :]
        lo, hi = k * rows, (k + 1) * rows
        a, b = spec[lo:hi, 0:NB], spec[lo:hi, NB : 2 * NB]
        spec[lo:hi, 0:NB] = a * fr - b * fi
        spec[lo:hi, NB : 2 * NB] = a * fi + b * fr


def whole_sum(value):
    return jnp.sum(jnp.sum(value, axis=0, keepdims=True), axis=1, keepdims=True)


def ymode_kernel(
    seed_ref, mat_ref, lam_ref, kind_ref, disp_ref, gain_ref, sat_ref, kerr_ref, out_ref
):
    total = jnp.zeros((8, 128), F32)
    for c0 in range(0, NK, WIDE):
        block = seed_ref[:, c0 * 128 : (c0 + WIDE) * 128]
        square = block * block
        modes = mm_wide(mat_ref[...], block)
        for c in range(WIDE):
            lanes = slice(c * 128, c * 128 + 128)
            for r in range(16):
                total = total + square[8 * r : 8 * r + 8, lanes]
            place = 8 * (c0 + c)
            for d in range(NS):
                out_ref[d, place : place + 8, 0, :] = modes[8 * d : 8 * d + 8, lanes]
    lane = lax.broadcasted_iota(jnp.int32, (NS, 128), 1)
    chosen = lax.broadcasted_iota(jnp.int32, (1, 32), 1) == kind_ref[...]
    side = jnp.where(lane < 64, lam_ref[...], whole_sum(total))
    for place, ref in ((65, disp_ref), (66, gain_ref), (67, sat_ref), (68, kerr_ref)):
        value = jnp.sum(jnp.where(chosen, ref[...], 0.0), axis=1, keepdims=True)
        side = jnp.where(lane == place, value, side)
    out_ref[:, 64, 0, :] = side


def xmode_kernel(in_ref, mat_ref, modes_ref, side_ref, tile_ref):
    square = jnp.zeros((128, 128), F32)
    for c0 in range(0, NK, WIDE):
        block = jnp.concatenate(
            [
                jnp.concatenate([in_ref[d, 8 * c : 8 * c + 8, 0, :] for d in range(NS)], axis=0)
                for c in range(c0, c0 + WIDE)
            ],
            axis=1,
        )
        modes = mm_wide(mat_ref[...], block)
        modes_ref[0:128, c0 * 128 : (c0 + WIDE) * 128] = modes
        for c in range(WIDE):
            square = square + modes[:, c * 128 : c * 128 + 128] ** 2
    weight = lax.dot_general(
        jnp.ones((8, 128), F32),
        square,
        (((1,), (1,)), ((), ())),
        precision=HIGHEST,
        preferred_element_type=F32,
    )
    lane = lax.broadcasted_iota(jnp.int32, (1, 128), 1)
    sides = in_ref[:, 64, 0, :]
    side = jnp.where(lane == 64, jnp.sum(sides, axis=0, keepdims=True), sides[0:1, :])
    side_ref[...] = jnp.broadcast_to(side, (8, 128))
    modes_ref[128:136, 0:128] = jnp.broadcast_to(side, (8, 128))
    modes_ref[128:136, 128:NT] = jnp.zeros((8, NT - 128), F32)
    tile = (weight + pltpu.roll(weight, 64, 1))[0:1, :]
    for d in range(NS):
        tile_ref[d] = tile[0:1, :]


def turn(angle):
    count = jnp.floor(angle * np.float32(2.0 / np.pi) + 0.5)
    x = angle - count * 1.5703125
    x = x - count * 4.837512969970703e-4
    x = x - count * 7.549789948768648e-8
    x = jnp.clip(x, -0.8, 0.8)
    z = x * x
    sine = ((-1.9515295891e-4 * z + 8.3321608736e-3) * z - 1.6666654611e-1) * z * x + x
    cosine = ((2.443315711809948e-5 * z - 1.388731625493765e-3) * z + 4.166664568298827e-2) * z
    cosine = cosine * z - 0.5 * z + 1.0
    quarter = count.astype(jnp.int32)
    odd = (quarter & 1) == 1
    c, s = jnp.where(odd, sine, cosine), jnp.where(odd, cosine, sine)
    c = jnp.where(((quarter + 1) & 2) == 2, -c, c)
    s = jnp.where((quarter & 2) == 2, -s, s)
    return c, s


def disperse_kernel(
    modes_ref, tw_ref, fwd_ref, bwd_ref, out_ref, one, two
):

    def load(part, r0, a):
        return modes_ref[64 * part + r0 : 64 * part + r0 + 8, a * NB : (a + 1) * NB]

    outer_forward(load, 64, tw_ref, one)
    two[...] = mm(one[...], fwd_ref[...])

    energy = modes_ref[128:129, 64:65]
    dispersion, gain_peak = modes_ref[128:129, 65:66], modes_ref[128:129, 66:67]
    gain = gain_peak / (1.0 + energy / (NG * NG * NT) / modes_ref[128:129, 67:68])
    w = tw_ref[2]
    relative = w / gain_width
    amplitude = jnp.exp(0.5 * gain / (1.0 + relative * relative) - loss_rate) * (1.0 / NT)
    angle = disp_scale * dispersion * w * w
    filter_spectrum(two, 64, amplitude * jnp.cos(angle), amplitude * jnp.sin(angle))

    one[...] = mm(two[...], bwd_ref[...])

    def store(r0, a, re, im):
        out_ref[r0 : r0 + 8, a * NB : (a + 1) * NB] = re
        out_ref[64 + r0 : 64 + r0 + 8, a * NB : (a + 1) * NB] = im

    outer_backward(one, 64, tw_ref, store)


def small_product(a, b):
    total = a[:, 0:1] * b[0:1, :]
    for k in range(1, KRYLOV):
        total = total + a[:, k : k + 1] * b[k : k + 1, :]
    return total


def expanded_ratios():
    series = np.array([1.0 / math.factorial(k) for k in range(taylor_terms + 1)])
    series = series / 2.0 ** (EXPANDED * np.arange(taylor_terms + 1))
    for _ in range(EXPANDED):
        series = np.convolve(series, series)
    series = series[series >= np.finfo(np.float32).tiny]
    return [float(ratio) for ratio in series[1:] / series[:-1]]


def krylov_exp(diagonals, couplings):
    row = lax.broadcasted_iota(jnp.int32, (8, 128), 0)
    lane = lax.broadcasted_iota(jnp.int32, (8, 128), 1)
    zero = jnp.zeros((8, 128), F32)
    scale = step_length / 2.0 ** (squarings - EXPANDED)
    mid, low, high = zero, zero, zero
    for j in range(KRYLOV):
        mid = jnp.where(row == j, diagonals[j] * scale, mid)
        if j + 1 < KRYLOV:
            high = jnp.where(row == j, couplings[j] * scale, high)
            low = jnp.where(row == j + 1, couplings[j] * scale, low)
    term = jnp.where(row == lane, 1.0, 0.0).astype(F32)
    real, imag = term, zero
    for order, ratio in enumerate(expanded_ratios(), 1):
        term = mid * term + low * pltpu.roll(term, 1, 0) + high * pltpu.roll(term, 7, 0)
        term = term * ratio
        signed = -term if order % 4 in (2, 3) else term
        if order % 2:
            imag = imag + signed
        else:
            real = real + signed
    for _ in range(squarings - EXPANDED):
        real, imag = (
            small_product(real, real) - small_product(imag, imag),
            2.0 * small_product(real, imag),
        )
    return real, imag


def mode_gains(weight, lam, own):
    rest = jnp.sqrt(weight)
    grown = jnp.ones((8, 128), F32)
    diagonals, couplings, polys = [], [], []
    for step in range(KRYLOV):
        spread = lam * rest
        square = whole_sum(rest * rest) + epsilon
        diagonal = whole_sum(spread * rest)
        if step:
            overlap = whole_sum(rest * vector)
        inverse = lax.rsqrt(square)
        coupling = square * inverse
        diagonal = diagonal * inverse * inverse
        if step:
            diagonal = diagonal - overlap
        diagonals.append(diagonal)
        couplings.append(coupling)
        poly = grown * inverse
        polys.append(poly)
        if step + 1 < KRYLOV:
            rest = rest * inverse
            image = spread * inverse
            grown = own * poly
            if step:
                image = image - coupling * vector
                grown = grown - coupling * before
            vector, before = rest, poly
            rest = image - diagonal * vector
            grown = grown - diagonal * before
    scale_zero = couplings[0]
    real, imag = krylov_exp(diagonals, couplings[1:])
    gains = []
    for part in (real, imag):
        gain = part[0:1, 0:1] * polys[0]
        for j in range(1, KRYLOV):
            gain = gain + part[j : j + 1, 0:1] * polys[j]
        gains.append(gain * scale_zero)
    return gains


def lanczos_kernel(side_ref, weight_ref, lam_ref, factor_ref):
    lane = lax.broadcasted_iota(jnp.int32, (NS, 128), 1)
    own = jnp.where(lane[0:8, :] < 64, side_ref[...], pltpu.roll(side_ref[...], 64, 1))
    weight = jnp.where(lane < 64, weight_ref[:, 0, :], 0.0)
    gain_re, gain_im = mode_gains(weight, lam_ref[...], own)
    row = lax.broadcasted_iota(jnp.int32, (8, 128), 0)
    factor_ref[...] = jnp.where(row == 0, gain_re, gain_im)


def propagate_kernel(factor_ref, modes_ref, mat_ref, out_ref, scaled):
    gain_re, gain_im = (
        jnp.broadcast_to(factor_ref[row : row + 1, :], (128, 128)).T[0:64, :]
        for row in range(2)
    )
    for c0 in range(0, NK, WIDE):
        for c in range(c0, c0 + WIDE):
            lanes = slice(c * 128, c * 128 + 128)
            a, b = modes_ref[0:64, lanes], modes_ref[64:128, lanes]
            scaled[0:64, lanes] = gain_re * a - gain_im * b
            scaled[64:128, lanes] = gain_im * a + gain_re * b
        lanes = slice(c0 * 128, (c0 + WIDE) * 128)
        back = mm_wide(mat_ref[...], scaled[:, lanes])
        out_ref[:, :, lanes] = back.reshape(NS, 8, WIDE * 128)


def kerr_kernel(
    modes_ref, in_ref, mat_ref, tw_ref, fwd_ref, bwd_ref,
    out_ref, field, delayed, one, two, done, sems
):
    kerr = modes_ref[128:129, 68:69]
    field[...] = mm_wide(mat_ref[...], in_ref[...].reshape(128, NT))

    def load(side, r0, a):
        lanes = slice(a * NB, (a + 1) * NB)
        re = field[32 * side + r0 : 32 * side + r0 + 8, lanes]
        im = field[64 + 32 * side + r0 : 64 + 32 * side + r0 + 8, lanes]
        return re * re + im * im

    outer_forward(load, 32, tw_ref, one)
    two[...] = mm_split(one[...], fwd_ref)
    filter_spectrum(two, 32, tw_ref[3], tw_ref[4])
    one[...] = mm_split(two[...], bwd_ref)

    def store(r0, a, re, im):
        lanes = slice(a * NB, (a + 1) * NB)
        delayed[r0 : r0 + 8, lanes] = re
        delayed[32 + r0 : 32 + r0 + 8, lanes] = im

    outer_backward(one, 32, tw_ref, store)

    copies = []
    for r0 in range(0, 64, 8):
        re, im = field[r0 : r0 + 8, :], field[64 + r0 : 64 + r0 + 8, :]
        late = delayed[r0 : r0 + 8, :]
        rotation = kerr * ((1.0 - raman_share) * (re * re + im * im) + raman_share * late)
        c, s = turn(rotation)
        done[r0 : r0 + 8, :] = re * c - im * s
        done[64 + r0 : 64 + r0 + 8, :] = re * s + im * c
        if r0 % 16 == 8:
            for lo in (r0 - 8, 64 + r0 - 8):
                rows = pl.ds(lo, 16)
                copy = pltpu.make_async_copy(done.at[rows], out_ref.at[rows], sems.at[lo // 16])
                copy.start()
                copies.append(copy)
    for copy in copies:
        copy.wait()


VMEM = pl.BlockSpec(memory_space=pltpu.VMEM)
HBM = pl.BlockSpec(memory_space=pltpu.HBM)


def near(*shape):
    return pltpu.VMEM(shape, F32)


def hold(value):
    return pltpu.with_memory_space_constraint(value, pltpu.VMEM)


def cost(flops, moved):
    return pl.CostEstimate(flops=flops, bytes_accessed=moved, transcendentals=0)


def exchange(value):
    return lax.all_to_all(value, "shard", split_axis=0, concat_axis=0, tiled=True)


def pass_on(value):
    count = lax.axis_size("blk")
    return lax.ppermute(value, "blk", [(b, (b + 1) % count) for b in range(count)])


def per_device(seed_field, segment_order, seg_disp, seg_kerr, seg_gain, seg_sat):
    t = tables()
    near_tables = {name: hold(jnp.asarray(value)) for name, value in t.items()}
    seed = seed_field.reshape(128, NT)

    ymodes = pl.pallas_call(
        ymode_kernel,
        out_shape=near(NS, 65, 1, 128),
        in_specs=[VMEM] * 8,
        out_specs=VMEM,
        name="ymode",
    )(
        seed, t["to_ymode"], t["lam_all"], segment_order.reshape(1, 1),
        *(each.reshape(1, 32) for each in (seg_disp, seg_gain, seg_sat, seg_kerr)),
    )
    gathered = exchange(ymodes)
    modes, side, tile = pl.pallas_call(
        xmode_kernel,
        out_shape=(near(136, NT), near(8, 128), near(NS, 1, 128)),
        in_specs=[VMEM] * 2,
        out_specs=(VMEM,) * 3,
        name="xmode",
    )(hold(gathered), near_tables["to_xmode"])
    shifted = pass_on(modes)
    weights = exchange(tile)
    factor = pl.pallas_call(
        lanczos_kernel,
        out_shape=near(8, 128),
        in_specs=[VMEM] * 3,
        out_specs=VMEM,
        cost_estimate=cost(6 * 2 * 512 * 256 * 256, 2**20),
        name="lanczos",
    )(hold(side), hold(weights), near_tables["lam_all"])
    shifted, factor = lax.optimization_barrier((shifted, factor))
    factor = pass_on(factor)
    dispersed = pl.pallas_call(
        disperse_kernel,
        out_shape=near(128, NT),
        in_specs=[VMEM] * 4,
        out_specs=VMEM,
        scratch_shapes=[pltpu.VMEM((512, 256), F32)] * 2,
        cost_estimate=cost(6 * 4 * 512 * 256 * 256, 2**20),
        name="disperse",
    )(hold(shifted), *(near_tables[name] for name in ("lines", "forward", "backward")))
    xback = pl.pallas_call(
        propagate_kernel,
        out_shape=near(NS, 8, NT),
        in_specs=[VMEM] * 3,
        out_specs=VMEM,
        scratch_shapes=[pltpu.VMEM((128, NT), F32)],
        name="propagate",
    )(hold(factor), hold(dispersed), near_tables["from_xmode"])
    rows = exchange(xback)
    result = pl.pallas_call(
        kerr_kernel,
        out_shape=jax.ShapeDtypeStruct((128, NT), F32),
        in_specs=[VMEM] * 6,
        out_specs=HBM,
        scratch_shapes=[pltpu.VMEM((128, NT), F32), pltpu.VMEM((64, NT), F32)]
        + [pltpu.VMEM((256, 256), F32)] * 2
        + [pltpu.VMEM((128, NT), F32), pltpu.SemaphoreType.DMA((8,))],
        name="kerr",
    )(
        hold(shifted), hold(rows),
        *(
            near_tables[name]
            for name in ("from_ymode", "lines", "forward_split", "backward_split")
        ),
    )
    return result.reshape(seed_field.shape)


def solution(mesh):
    in_specs = (P("blk", None, "shard", None, None), P("blk"), P(), P(), P(), P())
    out_specs = P("blk", None, "shard", None, None)
    return jax.shard_map(
        per_device, mesh=mesh, in_specs=in_specs, out_specs=out_specs, check_vma=False
    )
```

```python
import functools
import math

import jax
import jax.numpy as jnp
import numpy as np
from jax import lax
from jax.experimental import pallas as pl
from jax.experimental.pallas import tpu as pltpu
from jax.sharding import PartitionSpec as P

KRYLOV = 8
EXPANDED = 6
NS = 16
NG = 32
NT = 1024
NK = 8
WIDE = 2
NB = 128

epsilon = 1e-06
step_length = 2.5
grin_depth = 1.5
squarings = 8
taylor_terms = 10
gain_width = 0.25
loss_rate = 0.5
disp_scale = 60.0
raman_share = 0.18
raman_freq = 0.05
raman_damp = 0.035

F32 = jnp.float32
HIGHEST = lax.Precision.HIGHEST


@functools.cache
def tables():
    cell = (np.arange(NG) - (NG - 1) / 2.0) / (NG / 2.0)
    line = np.diag(-grin_depth * cell * cell)
    line = line + 0.5 * (np.eye(NG, k=1) + np.eye(NG, k=-1))
    values, q = np.linalg.eigh(line)

    to_ymode = np.zeros((NS, 2, 2, 2, 2, 2, NG))
    to_xmode = np.zeros((2, 2, NG, NS, 2, 2, 2))
    for part in range(2):
        for side in range(2):
            for jj in range(2):
                to_ymode[:, part, jj, side, part, side, :] = q[:, jj::2].T
                to_xmode[part, jj, :, :, part, jj, side] = q[side::2, :].T
    to_ymode = to_ymode.reshape(128, 128)
    to_xmode = to_xmode.reshape(128, 128)

    pair = values.reshape(NS, 2)
    lam = pair[:, None, :, None] + values[None, None, None, :] + np.zeros((1, 2, 1, 1))
    lam_all = lam.reshape(NS, 128)

    inner = np.arange(NB)
    angle = 2.0 * np.pi * ((inner[:, None] * inner[None, :]) % NB) / NB
    c, s = np.cos(angle), np.sin(angle)
    forward = np.block([[c, -s], [s, c]])
    backward = np.block([[c, s], [-s, c]])
    turn = 2.0 * np.pi * (np.arange(NK)[:, None] * inner[None, :]) / NT
    tw_cos, tw_sin = np.cos(turn), np.sin(turn)

    freq = np.arange(NK)[:, None] + NK * inner[None, :]
    signed = np.where(freq >= NT // 2, freq - NT, freq)
    w = signed / (NT / 2.0)
    resonance = raman_freq * raman_freq
    raman = resonance / (resonance - w * w - 1j * raman_damp * w)
    ram_re = raman.real / NT
    ram_im = np.where(signed == -(NT // 2), 0.0, raman.imag) / NT

    f32 = lambda a: np.ascontiguousarray(a, dtype=np.float32)
    return dict(
        to_ymode=widen(f32(to_ymode)),
        from_ymode=widen(f32(to_ymode.T)),
        to_xmode=widen(f32(to_xmode)),
        from_xmode=widen(f32(to_xmode.T)),
        lam_all=f32(lam_all),
        forward_split=split(f32(forward)),
        backward_split=split(f32(backward)),
        forward=f32(forward),
        backward=f32(backward),
        lines=f32(np.stack([tw_cos, tw_sin, w, ram_re, ram_im])),
    )


def split(table):
    high = table.astype(jnp.bfloat16)
    return np.stack([high, (table - high.astype(np.float32)).astype(jnp.bfloat16)])


def parts_of(value):
    high = value.astype(jnp.bfloat16)
    rest = value - high.astype(F32)
    middle = rest.astype(jnp.bfloat16)
    low = (rest - middle.astype(F32)).astype(jnp.bfloat16)
    return high, middle, low


def widen(table):
    high = table.astype(jnp.bfloat16)
    rest = table - high.astype(np.float32)
    middle = rest.astype(jnp.bfloat16)
    low = (rest - middle.astype(np.float32)).astype(jnp.bfloat16)
    return np.concatenate([high, middle, low, high, middle, high], axis=1)


def mm_wide(table, b):
    high, middle, low = parts_of(b)
    stacked = jnp.concatenate([high, high, high, middle, middle, low], axis=0)
    return jnp.dot(table, stacked, preferred_element_type=F32)


def mm_split(a, b_ref):
    high = a.astype(jnp.bfloat16)
    low = (a - high.astype(F32)).astype(jnp.bfloat16)
    dot = functools.partial(jnp.dot, preferred_element_type=F32)
    return dot(high, b_ref[0]) + (dot(high, b_ref[1]) + dot(low, b_ref[0]))


def mm(a, b):
    return jnp.dot(a, b, precision=HIGHEST, preferred_element_type=F32)


def fourier8(re, im, sign):
    def four(r, i):
        pr, pi = r[0] + r[2], i[0] + i[2]
        mr, mi = r[0] - r[2], i[0] - i[2]
        qr, qi = r[1] + r[3], i[1] + i[3]
        nr, ni = r[1] - r[3], i[1] - i[3]
        tr, ti = (-ni, nr) if sign > 0 else (ni, -nr)
        return (
            [pr + qr, mr + tr, pr - qr, mr - tr],
            [pi + qi, mi + ti, pi - qi, mi - ti],
        )

    er, ei = four(re[0::2], im[0::2])
    orr, oi = four(re[1::2], im[1::2])
    h = np.float32(np.sqrt(0.5))
    if sign > 0:
        w1 = ((orr[1] - oi[1]) * h, (orr[1] + oi[1]) * h)
        w2 = (-oi[2], orr[2])
        w3 = (-(orr[3] + oi[3]) * h, (orr[3] - oi[3]) * h)
    else:
        w1 = ((orr[1] + oi[1]) * h, (oi[1] - orr[1]) * h)
        w2 = (oi[2], -orr[2])
        w3 = ((oi[3] - orr[3]) * h, -(orr[3] + oi[3]) * h)
    tr = [orr[0], w1[0], w2[0], w3[0]]
    ti = [oi[0], w1[1], w2[1], w3[1]]
    out_r = [er[k] + tr[k] for k in range(4)] + [er[k] - tr[k] for k in range(4)]
    out_i = [ei[k] + ti[k] for k in range(4)] + [ei[k] - ti[k] for k in range(4)]
    return out_r, out_i


def outer_forward(load, rows, tw_ref, dest):
    for r0 in range(0, rows, 8):
        re = [load(0, r0, a) for a in range(NK)]
        im = [load(1, r0, a) for a in range(NK)]
        re, im = fourier8(re, im, -1)
        for k in range(NK):
            if k:
                c, s = tw_ref[0, k : k + 1, :], tw_ref[1, k : k + 1, :]
                re[k], im[k] = re[k] * c + im[k] * s, im[k] * c - re[k] * s
            dest[k * rows + r0 : k * rows + r0 + 8, 0:NB] = re[k]
            dest[k * rows + r0 : k * rows + r0 + 8, NB : 2 * NB] = im[k]


def outer_backward(src, rows, tw_ref, store):
    for r0 in range(0, rows, 8):
        re, im = [], []
        for k in range(NK):
            a = src[k * rows + r0 : k * rows + r0 + 8, 0:NB]
            b = src[k * rows + r0 : k * rows + r0 + 8, NB : 2 * NB]
            if k:
                c, s = tw_ref[0, k : k + 1, :], tw_ref[1, k : k + 1, :]
                a, b = a * c - b * s, a * s + b * c
            re.append(a)
            im.append(b)
        re, im = fourier8(re, im, 1)
        for a in range(NK):
            store(r0, a, re[a], im[a])


def filter_spectrum(spec, rows, factor_re, factor_im):
    for k in range(NK):
        fr, fi = factor_re[k : k + 1, :], factor_im[k : k + 1, :]
        lo, hi = k * rows, (k + 1) * rows
        a, b = spec[lo:hi, 0:NB], spec[lo:hi, NB : 2 * NB]
        spec[lo:hi, 0:NB] = a * fr - b * fi
        spec[lo:hi, NB : 2 * NB] = a * fi + b * fr


def whole_sum(value):
    return jnp.sum(jnp.sum(value, axis=0, keepdims=True), axis=1, keepdims=True)


def ymode_kernel(
    seed_ref, mat_ref, lam_ref, kind_ref, disp_ref, gain_ref, sat_ref, kerr_ref, out_ref
):
    total = jnp.zeros((8, 128), F32)
    for c0 in range(0, NK, WIDE):
        block = seed_ref[:, c0 * 128 : (c0 + WIDE) * 128]
        square = block * block
        modes = mm_wide(mat_ref[...], block)
        for c in range(WIDE):
            lanes = slice(c * 128, c * 128 + 128)
            for r in range(16):
                total = total + square[8 * r : 8 * r + 8, lanes]
            place = 8 * (c0 + c)
            for d in range(NS):
                out_ref[d, place : place + 8, 0, :] = modes[8 * d : 8 * d + 8, lanes]
    lane = lax.broadcasted_iota(jnp.int32, (NS, 128), 1)
    chosen = lax.broadcasted_iota(jnp.int32, (1, 32), 1) == kind_ref[...]
    side = jnp.where(lane < 64, lam_ref[...], whole_sum(total))
    for place, ref in ((65, disp_ref), (66, gain_ref), (67, sat_ref), (68, kerr_ref)):
        value = jnp.sum(jnp.where(chosen, ref[...], 0.0), axis=1, keepdims=True)
        side = jnp.where(lane == place, value, side)
    out_ref[:, 64, 0, :] = side


def xmode_kernel(in_ref, mat_ref, modes_ref, side_ref, tile_ref):
    square = jnp.zeros((128, 128), F32)
    for c0 in range(0, NK, WIDE):
        block = jnp.concatenate(
            [
                jnp.concatenate([in_ref[d, 8 * c : 8 * c + 8, 0, :] for d in range(NS)], axis=0)
                for c in range(c0, c0 + WIDE)
            ],
            axis=1,
        )
        modes = mm_wide(mat_ref[...], block)
        modes_ref[0:128, c0 * 128 : (c0 + WIDE) * 128] = modes
        for c in range(WIDE):
            square = square + modes[:, c * 128 : c * 128 + 128] ** 2
    both = square[0:64, :] + square[64:128, :]
    both = jnp.concatenate([both, both], axis=0)
    tile = jnp.sum(both.T, axis=0, keepdims=True)
    lane = lax.broadcasted_iota(jnp.int32, (1, 128), 1)
    sides = in_ref[:, 64, 0, :]
    side = jnp.where(lane == 64, jnp.sum(sides, axis=0, keepdims=True), sides[0:1, :])
    side_ref[...] = jnp.broadcast_to(side, (8, 128))
    modes_ref[128:136, 0:128] = jnp.broadcast_to(side, (8, 128))
    modes_ref[128:136, 128:NT] = jnp.zeros((8, NT - 128), F32)
    for d in range(NS):
        tile_ref[d] = tile


def turn(angle):
    count = jnp.floor(angle * np.float32(2.0 / np.pi) + 0.5)
    x = angle - count * 1.5703125
    x = x - count * 4.837512969970703e-4
    x = x - count * 7.549789948768648e-8
    x = jnp.clip(x, -0.8, 0.8)
    z = x * x
    sine = ((-1.9515295891e-4 * z + 8.3321608736e-3) * z - 1.6666654611e-1) * z * x + x
    cosine = ((2.443315711809948e-5 * z - 1.388731625493765e-3) * z + 4.166664568298827e-2) * z
    cosine = cosine * z - 0.5 * z + 1.0
    quarter = count.astype(jnp.int32)
    odd = (quarter & 1) == 1
    c, s = jnp.where(odd, sine, cosine), jnp.where(odd, cosine, sine)
    c = jnp.where(((quarter + 1) & 2) == 2, -c, c)
    s = jnp.where((quarter & 2) == 2, -s, s)
    return c, s


def disperse_kernel(
    modes_ref, tw_ref, fwd_ref, bwd_ref, out_ref, one, two
):

    def load(part, r0, a):
        return modes_ref[64 * part + r0 : 64 * part + r0 + 8, a * NB : (a + 1) * NB]

    outer_forward(load, 64, tw_ref, one)
    two[...] = mm(one[...], fwd_ref[...])

    energy = modes_ref[128:129, 64:65]
    dispersion, gain_peak = modes_ref[128:129, 65:66], modes_ref[128:129, 66:67]
    gain = gain_peak / (1.0 + energy / (NG * NG * NT) / modes_ref[128:129, 67:68])
    w = tw_ref[2]
    relative = w / gain_width
    amplitude = jnp.exp(0.5 * gain / (1.0 + relative * relative) - loss_rate) * (1.0 / NT)
    angle = disp_scale * dispersion * w * w
    filter_spectrum(two, 64, amplitude * jnp.cos(angle), amplitude * jnp.sin(angle))

    one[...] = mm(two[...], bwd_ref[...])

    def store(r0, a, re, im):
        out_ref[r0 : r0 + 8, a * NB : (a + 1) * NB] = re
        out_ref[64 + r0 : 64 + r0 + 8, a * NB : (a + 1) * NB] = im

    outer_backward(one, 64, tw_ref, store)


def small_product(a, b):
    total = a[:, 0:1] * b[0:1, :]
    for k in range(1, KRYLOV):
        total = total + a[:, k : k + 1] * b[k : k + 1, :]
    return total


def expanded_ratios():
    series = np.array([1.0 / math.factorial(k) for k in range(taylor_terms + 1)])
    series = series / 2.0 ** (EXPANDED * np.arange(taylor_terms + 1))
    for _ in range(EXPANDED):
        series = np.convolve(series, series)
    series = series[series >= np.finfo(np.float32).tiny]
    return [float(ratio) for ratio in series[1:] / series[:-1]]


def krylov_exp(diagonals, couplings):
    row = lax.broadcasted_iota(jnp.int32, (8, 128), 0)
    lane = lax.broadcasted_iota(jnp.int32, (8, 128), 1)
    zero = jnp.zeros((8, 128), F32)
    scale = step_length / 2.0 ** (squarings - EXPANDED)
    mid, low, high = zero, zero, zero
    for j in range(KRYLOV):
        mid = jnp.where(row == j, diagonals[j] * scale, mid)
        if j + 1 < KRYLOV:
            high = jnp.where(row == j, couplings[j] * scale, high)
            low = jnp.where(row == j + 1, couplings[j] * scale, low)
    term = jnp.where(row == lane, 1.0, 0.0).astype(F32)
    real, imag = term, zero
    for order, ratio in enumerate(expanded_ratios(), 1):
        term = mid * term + low * pltpu.roll(term, 1, 0) + high * pltpu.roll(term, 7, 0)
        term = term * ratio
        signed = -term if order % 4 in (2, 3) else term
        if order % 2:
            imag = imag + signed
        else:
            real = real + signed
    for _ in range(squarings - EXPANDED):
        real, imag = (
            small_product(real, real) - small_product(imag, imag),
            2.0 * small_product(real, imag),
        )
    return real, imag


def mode_gains(weight, lam, own):
    rest = jnp.sqrt(weight)
    grown = jnp.ones((8, 128), F32)
    diagonals, couplings, polys = [], [], []
    for step in range(KRYLOV):
        spread = lam * rest
        square = whole_sum(rest * rest) + epsilon
        diagonal = whole_sum(spread * rest)
        if step:
            overlap = whole_sum(rest * vector)
        inverse = lax.rsqrt(square)
        coupling = square * inverse
        diagonal = diagonal * inverse * inverse
        if step:
            diagonal = diagonal - overlap
        diagonals.append(diagonal)
        couplings.append(coupling)
        poly = grown * inverse
        polys.append(poly)
        if step + 1 < KRYLOV:
            rest = rest * inverse
            image = spread * inverse
            grown = own * poly
            if step:
                image = image - coupling * vector
                grown = grown - coupling * before
            vector, before = rest, poly
            rest = image - diagonal * vector
            grown = grown - diagonal * before
    scale_zero = couplings[0]
    real, imag = krylov_exp(diagonals, couplings[1:])
    gains = []
    for part in (real, imag):
        gain = part[0:1, 0:1] * polys[0]
        for j in range(1, KRYLOV):
            gain = gain + part[j : j + 1, 0:1] * polys[j]
        gains.append(gain * scale_zero)
    return gains


def lanczos_kernel(side_ref, weight_ref, lam_ref, factor_ref):
    lane = lax.broadcasted_iota(jnp.int32, (NS, 128), 1)
    own = jnp.where(lane[0:8, :] < 64, side_ref[...], pltpu.roll(side_ref[...], 64, 1))
    weight = jnp.where(lane < 64, weight_ref[:, 0, :], 0.0)
    gain_re, gain_im = mode_gains(weight, lam_ref[...], own)
    row = lax.broadcasted_iota(jnp.int32, (8, 128), 0)
    factor_ref[...] = jnp.where(row == 0, gain_re, gain_im)


def propagate_kernel(factor_ref, modes_ref, mat_ref, out_ref, scaled):
    gain_re, gain_im = (
        jnp.broadcast_to(factor_ref[row : row + 1, :], (128, 128)).T[0:64, :]
        for row in range(2)
    )
    for c0 in range(0, NK, WIDE):
        for c in range(c0, c0 + WIDE):
            lanes = slice(c * 128, c * 128 + 128)
            a, b = modes_ref[0:64, lanes], modes_ref[64:128, lanes]
            scaled[0:64, lanes] = gain_re * a - gain_im * b
            scaled[64:128, lanes] = gain_im * a + gain_re * b
        lanes = slice(c0 * 128, (c0 + WIDE) * 128)
        back = mm_wide(mat_ref[...], scaled[:, lanes])
        out_ref[:, :, lanes] = back.reshape(NS, 8, WIDE * 128)


def kerr_kernel(
    modes_ref, in_ref, mat_ref, tw_ref, fwd_ref, bwd_ref,
    out_ref, field, delayed, one, two, done, sems
):
    kerr = modes_ref[128:129, 68:69]
    field[...] = mm_wide(mat_ref[...], in_ref[...].reshape(128, NT))

    def load(side, r0, a):
        lanes = slice(a * NB, (a + 1) * NB)
        re = field[32 * side + r0 : 32 * side + r0 + 8, lanes]
        im = field[64 + 32 * side + r0 : 64 + 32 * side + r0 + 8, lanes]
        return re * re + im * im

    outer_forward(load, 32, tw_ref, one)
    two[...] = mm_split(one[...], fwd_ref)
    filter_spectrum(two, 32, tw_ref[3], tw_ref[4])
    one[...] = mm_split(two[...], bwd_ref)

    def store(r0, a, re, im):
        lanes = slice(a * NB, (a + 1) * NB)
        delayed[r0 : r0 + 8, lanes] = re
        delayed[32 + r0 : 32 + r0 + 8, lanes] = im

    outer_backward(one, 32, tw_ref, store)

    copies = []
    for r0 in range(0, 64, 8):
        re, im = field[r0 : r0 + 8, :], field[64 + r0 : 64 + r0 + 8, :]
        late = delayed[r0 : r0 + 8, :]
        rotation = kerr * ((1.0 - raman_share) * (re * re + im * im) + raman_share * late)
        c, s = turn(rotation)
        done[r0 : r0 + 8, :] = re * c - im * s
        done[64 + r0 : 64 + r0 + 8, :] = re * s + im * c
        if r0 % 16 == 8:
            for lo in (r0 - 8, 64 + r0 - 8):
                rows = pl.ds(lo, 16)
                copy = pltpu.make_async_copy(done.at[rows], out_ref.at[rows], sems.at[lo // 16])
                copy.start()
                copies.append(copy)
    for copy in copies:
        copy.wait()


VMEM = pl.BlockSpec(memory_space=pltpu.VMEM)
HBM = pl.BlockSpec(memory_space=pltpu.HBM)


def near(*shape):
    return pltpu.VMEM(shape, F32)


def hold(value):
    return pltpu.with_memory_space_constraint(value, pltpu.VMEM)


def cost(flops, moved):
    return pl.CostEstimate(flops=flops, bytes_accessed=moved, transcendentals=0)


def exchange(value):
    return lax.all_to_all(value, "shard", split_axis=0, concat_axis=0, tiled=True)


def pass_on(value):
    count = lax.axis_size("blk")
    return lax.ppermute(value, "blk", [(b, (b + 1) % count) for b in range(count)])


def per_device(seed_field, segment_order, seg_disp, seg_kerr, seg_gain, seg_sat):
    t = tables()
    near_tables = {name: hold(jnp.asarray(value)) for name, value in t.items()}
    seed = seed_field.reshape(128, NT)

    ymodes = pl.pallas_call(
        ymode_kernel,
        out_shape=near(NS, 65, 1, 128),
        in_specs=[VMEM] * 8,
        out_specs=VMEM,
        name="ymode",
    )(
        seed, t["to_ymode"], t["lam_all"], segment_order.reshape(1, 1),
        *(each.reshape(1, 32) for each in (seg_disp, seg_gain, seg_sat, seg_kerr)),
    )
    gathered = exchange(ymodes)
    modes, side, tile = pl.pallas_call(
        xmode_kernel,
        out_shape=(near(136, NT), near(8, 128), near(NS, 1, 128)),
        in_specs=[VMEM] * 2,
        out_specs=(VMEM,) * 3,
        name="xmode",
    )(hold(gathered), near_tables["to_xmode"])
    shifted = pass_on(modes)
    weights = exchange(tile)
    factor = pl.pallas_call(
        lanczos_kernel,
        out_shape=near(8, 128),
        in_specs=[VMEM] * 3,
        out_specs=VMEM,
        cost_estimate=cost(6 * 2 * 512 * 256 * 256, 2**20),
        name="lanczos",
    )(hold(side), hold(weights), near_tables["lam_all"])
    shifted, factor = lax.optimization_barrier((shifted, factor))
    factor = pass_on(factor)
    dispersed = pl.pallas_call(
        disperse_kernel,
        out_shape=near(128, NT),
        in_specs=[VMEM] * 4,
        out_specs=VMEM,
        scratch_shapes=[pltpu.VMEM((512, 256), F32)] * 2,
        cost_estimate=cost(6 * 4 * 512 * 256 * 256, 2**20),
        name="disperse",
    )(hold(shifted), *(near_tables[name] for name in ("lines", "forward", "backward")))
    xback = pl.pallas_call(
        propagate_kernel,
        out_shape=near(NS, 8, NT),
        in_specs=[VMEM] * 3,
        out_specs=VMEM,
        scratch_shapes=[pltpu.VMEM((128, NT), F32)],
        name="propagate",
    )(hold(factor), hold(dispersed), near_tables["from_xmode"])
    rows = exchange(xback)
    result = pl.pallas_call(
        kerr_kernel,
        out_shape=jax.ShapeDtypeStruct((128, NT), F32),
        in_specs=[VMEM] * 6,
        out_specs=HBM,
        scratch_shapes=[pltpu.VMEM((128, NT), F32), pltpu.VMEM((64, NT), F32)]
        + [pltpu.VMEM((256, 256), F32)] * 2
        + [pltpu.VMEM((128, NT), F32), pltpu.SemaphoreType.DMA((8,))],
        name="kerr",
    )(
        hold(shifted), hold(rows),
        *(
            near_tables[name]
            for name in ("from_ymode", "lines", "forward_split", "backward_split")
        ),
    )
    return result.reshape(seed_field.shape)


def solution(mesh):
    in_specs = (P("blk", None, "shard", None, None), P("blk"), P(), P(), P(), P())
    out_specs = P("blk", None, "shard", None, None)
    return jax.shard_map(
        per_device, mesh=mesh, in_specs=in_specs, out_specs=out_specs, check_vma=False
    )
```

```python
import functools
import math

import jax
import jax.numpy as jnp
import numpy as np
from jax import lax
from jax.experimental import pallas as pl
from jax.experimental.pallas import tpu as pltpu
from jax.sharding import PartitionSpec as P

KRYLOV = 8
EXPANDED = 6
NS = 16
NG = 32
NT = 1024
NK = 8
WIDE = 2
NB = 128

epsilon = 1e-06
step_length = 2.5
grin_depth = 1.5
squarings = 8
taylor_terms = 10
gain_width = 0.25
loss_rate = 0.5
disp_scale = 60.0
raman_share = 0.18
raman_freq = 0.05
raman_damp = 0.035

F32 = jnp.float32
HIGHEST = lax.Precision.HIGHEST


@functools.cache
def tables():
    cell = (np.arange(NG) - (NG - 1) / 2.0) / (NG / 2.0)
    line = np.diag(-grin_depth * cell * cell)
    line = line + 0.5 * (np.eye(NG, k=1) + np.eye(NG, k=-1))
    values, q = np.linalg.eigh(line)

    to_ymode = np.zeros((NS, 2, 2, 2, 2, 2, NG))
    to_xmode = np.zeros((2, 2, NG, NS, 2, 2, 2))
    for part in range(2):
        for side in range(2):
            for jj in range(2):
                to_ymode[:, part, jj, side, part, side, :] = q[:, jj::2].T
                to_xmode[part, jj, :, :, part, jj, side] = q[side::2, :].T
    to_ymode = to_ymode.reshape(128, 128)
    to_xmode = to_xmode.reshape(128, 128)

    pair = values.reshape(NS, 2)
    lam = pair[:, None, :, None] + values[None, None, None, :] + np.zeros((1, 2, 1, 1))
    lam_all = lam.reshape(NS, 128)

    inner = np.arange(NB)
    angle = 2.0 * np.pi * ((inner[:, None] * inner[None, :]) % NB) / NB
    c, s = np.cos(angle), np.sin(angle)
    forward = np.block([[c, -s], [s, c]])
    backward = np.block([[c, s], [-s, c]])
    turn = 2.0 * np.pi * (np.arange(NK)[:, None] * inner[None, :]) / NT
    tw_cos, tw_sin = np.cos(turn), np.sin(turn)

    freq = np.arange(NK)[:, None] + NK * inner[None, :]
    signed = np.where(freq >= NT // 2, freq - NT, freq)
    w = signed / (NT / 2.0)
    resonance = raman_freq * raman_freq
    raman = resonance / (resonance - w * w - 1j * raman_damp * w)
    ram_re = raman.real / NT
    ram_im = np.where(signed == -(NT // 2), 0.0, raman.imag) / NT

    f32 = lambda a: np.ascontiguousarray(a, dtype=np.float32)
    return dict(
        to_ymode=widen(f32(to_ymode)),
        from_ymode=widen(f32(to_ymode.T)),
        to_xmode=widen(f32(to_xmode)),
        from_xmode=widen(f32(to_xmode.T)),
        lam_all=f32(lam_all),
        forward_split=split(f32(forward)),
        backward_split=split(f32(backward)),
        forward=f32(forward),
        backward=f32(backward),
        lines=f32(np.stack([tw_cos, tw_sin, w, ram_re, ram_im])),
    )


def split(table):
    high = table.astype(jnp.bfloat16)
    return np.stack([high, (table - high.astype(np.float32)).astype(jnp.bfloat16)])


def parts_of(value):
    high = value.astype(jnp.bfloat16)
    rest = value - high.astype(F32)
    middle = rest.astype(jnp.bfloat16)
    low = (rest - middle.astype(F32)).astype(jnp.bfloat16)
    return high, middle, low


def widen(table):
    high = table.astype(jnp.bfloat16)
    rest = table - high.astype(np.float32)
    middle = rest.astype(jnp.bfloat16)
    low = (rest - middle.astype(np.float32)).astype(jnp.bfloat16)
    return np.concatenate([high, middle, low, high, middle, high], axis=1)


def mm_wide(table, b):
    high, middle, low = parts_of(b)
    stacked = jnp.concatenate([high, high, high, middle, middle, low], axis=0)
    return jnp.dot(table, stacked, preferred_element_type=F32)


def mm_split(a, b_ref):
    high = a.astype(jnp.bfloat16)
    low = (a - high.astype(F32)).astype(jnp.bfloat16)
    dot = functools.partial(jnp.dot, preferred_element_type=F32)
    return dot(high, b_ref[0]) + (dot(high, b_ref[1]) + dot(low, b_ref[0]))


def mm(a, b):
    return jnp.dot(a, b, precision=HIGHEST, preferred_element_type=F32)


def fourier8(re, im, sign):
    def four(r, i):
        pr, pi = r[0] + r[2], i[0] + i[2]
        mr, mi = r[0] - r[2], i[0] - i[2]
        qr, qi = r[1] + r[3], i[1] + i[3]
        nr, ni = r[1] - r[3], i[1] - i[3]
        tr, ti = (-ni, nr) if sign > 0 else (ni, -nr)
        return (
            [pr + qr, mr + tr, pr - qr, mr - tr],
            [pi + qi, mi + ti, pi - qi, mi - ti],
        )

    er, ei = four(re[0::2], im[0::2])
    orr, oi = four(re[1::2], im[1::2])
    h = np.float32(np.sqrt(0.5))
    if sign > 0:
        w1 = ((orr[1] - oi[1]) * h, (orr[1] + oi[1]) * h)
        w2 = (-oi[2], orr[2])
        w3 = (-(orr[3] + oi[3]) * h, (orr[3] - oi[3]) * h)
    else:
        w1 = ((orr[1] + oi[1]) * h, (oi[1] - orr[1]) * h)
        w2 = (oi[2], -orr[2])
        w3 = ((oi[3] - orr[3]) * h, -(orr[3] + oi[3]) * h)
    tr = [orr[0], w1[0], w2[0], w3[0]]
    ti = [oi[0], w1[1], w2[1], w3[1]]
    out_r = [er[k] + tr[k] for k in range(4)] + [er[k] - tr[k] for k in range(4)]
    out_i = [ei[k] + ti[k] for k in range(4)] + [ei[k] - ti[k] for k in range(4)]
    return out_r, out_i


def outer_forward(load, rows, tw_ref, dest):
    for r0 in range(0, rows, 8):
        re = [load(0, r0, a) for a in range(NK)]
        im = [load(1, r0, a) for a in range(NK)]
        re, im = fourier8(re, im, -1)
        for k in range(NK):
            if k:
                c, s = tw_ref[0, k : k + 1, :], tw_ref[1, k : k + 1, :]
                re[k], im[k] = re[k] * c + im[k] * s, im[k] * c - re[k] * s
            dest[k * rows + r0 : k * rows + r0 + 8, 0:NB] = re[k]
            dest[k * rows + r0 : k * rows + r0 + 8, NB : 2 * NB] = im[k]


def outer_backward(src, rows, tw_ref, store):
    for r0 in range(0, rows, 8):
        re, im = [], []
        for k in range(NK):
            a = src[k * rows + r0 : k * rows + r0 + 8, 0:NB]
            b = src[k * rows + r0 : k * rows + r0 + 8, NB : 2 * NB]
            if k:
                c, s = tw_ref[0, k : k + 1, :], tw_ref[1, k : k + 1, :]
                a, b = a * c - b * s, a * s + b * c
            re.append(a)
            im.append(b)
        re, im = fourier8(re, im, 1)
        for a in range(NK):
            store(r0, a, re[a], im[a])


def filter_spectrum(spec, rows, factor_re, factor_im):
    for k in range(NK):
        fr, fi = factor_re[k : k + 1, :], factor_im[k : k + 1, :]
        lo, hi = k * rows, (k + 1) * rows
        a, b = spec[lo:hi, 0:NB], spec[lo:hi, NB : 2 * NB]
        spec[lo:hi, 0:NB] = a * fr - b * fi
        spec[lo:hi, NB : 2 * NB] = a * fi + b * fr


def whole_sum(value):
    return jnp.sum(jnp.sum(value, axis=0, keepdims=True), axis=1, keepdims=True)


def ymode_kernel(
    seed_ref, mat_ref, lam_ref, kind_ref, disp_ref, gain_ref, sat_ref, kerr_ref, out_ref
):
    total = jnp.zeros((8, 128), F32)
    for c0 in range(0, NK, WIDE):
        block = seed_ref[:, c0 * 128 : (c0 + WIDE) * 128]
        square = block * block
        modes = mm_wide(mat_ref[...], block)
        for c in range(WIDE):
            lanes = slice(c * 128, c * 128 + 128)
            for r in range(16):
                total = total + square[8 * r : 8 * r + 8, lanes]
            place = 8 * (c0 + c)
            for d in range(NS):
                out_ref[d, place : place + 8, 0, :] = modes[8 * d : 8 * d + 8, lanes]
    lane = lax.broadcasted_iota(jnp.int32, (NS, 128), 1)
    chosen = lax.broadcasted_iota(jnp.int32, (1, 32), 1) == kind_ref[...]
    side = jnp.where(lane < 64, lam_ref[...], whole_sum(total))
    for place, ref in ((65, disp_ref), (66, gain_ref), (67, sat_ref), (68, kerr_ref)):
        value = jnp.sum(jnp.where(chosen, ref[...], 0.0), axis=1, keepdims=True)
        side = jnp.where(lane == place, value, side)
    out_ref[:, 64, 0, :] = side


def xmode_kernel(in_ref, mat_ref, modes_ref, side_ref, tile_ref):
    square = jnp.zeros((128, 128), F32)
    for c0 in range(0, NK, WIDE):
        block = jnp.concatenate(
            [
                jnp.concatenate([in_ref[d, 8 * c : 8 * c + 8, 0, :] for d in range(NS)], axis=0)
                for c in range(c0, c0 + WIDE)
            ],
            axis=1,
        )
        modes = mm_wide(mat_ref[...], block)
        modes_ref[0:128, c0 * 128 : (c0 + WIDE) * 128] = modes
        for c in range(WIDE):
            square = square + modes[:, c * 128 : c * 128 + 128] ** 2
    both = square[0:64, :] + square[64:128, :]
    both = jnp.concatenate([both, both], axis=0)
    tile = jnp.sum(both.T, axis=0, keepdims=True)
    lane = lax.broadcasted_iota(jnp.int32, (1, 128), 1)
    sides = in_ref[:, 64, 0, :]
    side = jnp.where(lane == 64, jnp.sum(sides, axis=0, keepdims=True), sides[0:1, :])
    side_ref[...] = jnp.broadcast_to(side, (8, 128))
    modes_ref[128:136, 0:128] = jnp.broadcast_to(side, (8, 128))
    modes_ref[128:136, 128:NT] = jnp.zeros((8, NT - 128), F32)
    for d in range(NS):
        tile_ref[d] = tile


def turn(angle):
    count = jnp.floor(angle * np.float32(2.0 / np.pi) + 0.5)
    x = angle - count * 1.5703125
    x = x - count * 4.837512969970703e-4
    x = x - count * 7.549789948768648e-8
    x = jnp.clip(x, -0.8, 0.8)
    z = x * x
    sine = ((-1.9515295891e-4 * z + 8.3321608736e-3) * z - 1.6666654611e-1) * z * x + x
    cosine = ((2.443315711809948e-5 * z - 1.388731625493765e-3) * z + 4.166664568298827e-2) * z
    cosine = cosine * z - 0.5 * z + 1.0
    quarter = count.astype(jnp.int32)
    odd = (quarter & 1) == 1
    c, s = jnp.where(odd, sine, cosine), jnp.where(odd, cosine, sine)
    c = jnp.where(((quarter + 1) & 2) == 2, -c, c)
    s = jnp.where((quarter & 2) == 2, -s, s)
    return c, s


def disperse_kernel(
    modes_ref, tw_ref, fwd_ref, bwd_ref, out_ref, one, two
):

    def load(part, r0, a):
        return modes_ref[64 * part + r0 : 64 * part + r0 + 8, a * NB : (a + 1) * NB]

    outer_forward(load, 64, tw_ref, one)
    two[...] = mm_split(one[...], fwd_ref)

    energy = modes_ref[128:129, 64:65]
    dispersion, gain_peak = modes_ref[128:129, 65:66], modes_ref[128:129, 66:67]
    gain = gain_peak / (1.0 + energy / (NG * NG * NT) / modes_ref[128:129, 67:68])
    w = tw_ref[2]
    relative = w / gain_width
    amplitude = jnp.exp(0.5 * gain / (1.0 + relative * relative) - loss_rate) * (1.0 / NT)
    angle = disp_scale * dispersion * w * w
    filter_spectrum(two, 64, amplitude * jnp.cos(angle), amplitude * jnp.sin(angle))

    one[...] = mm_split(two[...], bwd_ref)

    def store(r0, a, re, im):
        out_ref[r0 : r0 + 8, a * NB : (a + 1) * NB] = re
        out_ref[64 + r0 : 64 + r0 + 8, a * NB : (a + 1) * NB] = im

    outer_backward(one, 64, tw_ref, store)


def small_product(a, b):
    total = a[:, 0:1] * b[0:1, :]
    for k in range(1, KRYLOV):
        total = total + a[:, k : k + 1] * b[k : k + 1, :]
    return total


def expanded_ratios():
    series = np.array([1.0 / math.factorial(k) for k in range(taylor_terms + 1)])
    series = series / 2.0 ** (EXPANDED * np.arange(taylor_terms + 1))
    for _ in range(EXPANDED):
        series = np.convolve(series, series)
    series = series[series >= np.finfo(np.float32).tiny]
    return [float(ratio) for ratio in series[1:] / series[:-1]]


def krylov_exp(diagonals, couplings):
    row = lax.broadcasted_iota(jnp.int32, (8, 128), 0)
    lane = lax.broadcasted_iota(jnp.int32, (8, 128), 1)
    zero = jnp.zeros((8, 128), F32)
    scale = step_length / 2.0 ** (squarings - EXPANDED)
    mid, low, high = zero, zero, zero
    for j in range(KRYLOV):
        mid = jnp.where(row == j, diagonals[j] * scale, mid)
        if j + 1 < KRYLOV:
            high = jnp.where(row == j, couplings[j] * scale, high)
            low = jnp.where(row == j + 1, couplings[j] * scale, low)
    term = jnp.where(row == lane, 1.0, 0.0).astype(F32)
    real, imag = term, zero
    for order, ratio in enumerate(expanded_ratios(), 1):
        term = mid * term + low * pltpu.roll(term, 1, 0) + high * pltpu.roll(term, 7, 0)
        term = term * ratio
        signed = -term if order % 4 in (2, 3) else term
        if order % 2:
            imag = imag + signed
        else:
            real = real + signed
    for _ in range(squarings - EXPANDED):
        real, imag = (
            small_product(real, real) - small_product(imag, imag),
            2.0 * small_product(real, imag),
        )
    return real, imag


def mode_gains(weight, lam, own):
    rest = jnp.sqrt(weight)
    grown = jnp.ones((8, 128), F32)
    diagonals, couplings, polys = [], [], []
    for step in range(KRYLOV):
        spread = lam * rest
        square = whole_sum(rest * rest) + epsilon
        diagonal = whole_sum(spread * rest)
        if step:
            overlap = whole_sum(rest * vector)
        inverse = lax.rsqrt(square)
        coupling = square * inverse
        diagonal = diagonal * inverse * inverse
        if step:
            diagonal = diagonal - overlap
        diagonals.append(diagonal)
        couplings.append(coupling)
        poly = grown * inverse
        polys.append(poly)
        if step + 1 < KRYLOV:
            rest = rest * inverse
            image = spread * inverse
            grown = own * poly
            if step:
                image = image - coupling * vector
                grown = grown - coupling * before
            vector, before = rest, poly
            rest = image - diagonal * vector
            grown = grown - diagonal * before
    scale_zero = couplings[0]
    real, imag = krylov_exp(diagonals, couplings[1:])
    gains = []
    for part in (real, imag):
        gain = part[0:1, 0:1] * polys[0]
        for j in range(1, KRYLOV):
            gain = gain + part[j : j + 1, 0:1] * polys[j]
        gains.append(gain * scale_zero)
    return gains


def lanczos_kernel(side_ref, weight_ref, lam_ref, factor_ref):
    lane = lax.broadcasted_iota(jnp.int32, (NS, 128), 1)
    own = jnp.where(lane[0:8, :] < 64, side_ref[...], pltpu.roll(side_ref[...], 64, 1))
    weight = jnp.where(lane < 64, weight_ref[:, 0, :], 0.0)
    gain_re, gain_im = mode_gains(weight, lam_ref[...], own)
    row = lax.broadcasted_iota(jnp.int32, (8, 128), 0)
    factor_ref[...] = jnp.where(row == 0, gain_re, gain_im)


def propagate_kernel(factor_ref, modes_ref, mat_ref, out_ref, scaled):
    gain_re, gain_im = (
        jnp.broadcast_to(factor_ref[row : row + 1, :], (128, 128)).T[0:64, :]
        for row in range(2)
    )
    for c0 in range(0, NK, WIDE):
        for c in range(c0, c0 + WIDE):
            lanes = slice(c * 128, c * 128 + 128)
            a, b = modes_ref[0:64, lanes], modes_ref[64:128, lanes]
            scaled[0:64, lanes] = gain_re * a - gain_im * b
            scaled[64:128, lanes] = gain_im * a + gain_re * b
        lanes = slice(c0 * 128, (c0 + WIDE) * 128)
        back = mm_wide(mat_ref[...], scaled[:, lanes])
        out_ref[:, :, lanes] = back.reshape(NS, 8, WIDE * 128)


def kerr_kernel(
    modes_ref, in_ref, mat_ref, tw_ref, fwd_ref, bwd_ref,
    out_ref, field, delayed, one, two, done, sems
):
    kerr = modes_ref[128:129, 68:69]
    field[...] = mm_wide(mat_ref[...], in_ref[...].reshape(128, NT))

    def load(side, r0, a):
        lanes = slice(a * NB, (a + 1) * NB)
        re = field[32 * side + r0 : 32 * side + r0 + 8, lanes]
        im = field[64 + 32 * side + r0 : 64 + 32 * side + r0 + 8, lanes]
        return re * re + im * im

    outer_forward(load, 32, tw_ref, one)
    two[...] = mm_split(one[...], fwd_ref)
    filter_spectrum(two, 32, tw_ref[3], tw_ref[4])
    one[...] = mm_split(two[...], bwd_ref)

    def store(r0, a, re, im):
        lanes = slice(a * NB, (a + 1) * NB)
        delayed[r0 : r0 + 8, lanes] = re
        delayed[32 + r0 : 32 + r0 + 8, lanes] = im

    outer_backward(one, 32, tw_ref, store)

    copies = []
    for r0 in range(0, 64, 8):
        re, im = field[r0 : r0 + 8, :], field[64 + r0 : 64 + r0 + 8, :]
        late = delayed[r0 : r0 + 8, :]
        rotation = kerr * ((1.0 - raman_share) * (re * re + im * im) + raman_share * late)
        c, s = turn(rotation)
        done[r0 : r0 + 8, :] = re * c - im * s
        done[64 + r0 : 64 + r0 + 8, :] = re * s + im * c
        if r0 % 16 == 8:
            for lo in (r0 - 8, 64 + r0 - 8):
                rows = pl.ds(lo, 16)
                copy = pltpu.make_async_copy(done.at[rows], out_ref.at[rows], sems.at[lo // 16])
                copy.start()
                copies.append(copy)
    for copy in copies:
        copy.wait()


VMEM = pl.BlockSpec(memory_space=pltpu.VMEM)
HBM = pl.BlockSpec(memory_space=pltpu.HBM)


def near(*shape):
    return pltpu.VMEM(shape, F32)


def hold(value):
    return pltpu.with_memory_space_constraint(value, pltpu.VMEM)


def cost(flops, moved):
    return pl.CostEstimate(flops=flops, bytes_accessed=moved, transcendentals=0)


def exchange(value):
    return lax.all_to_all(value, "shard", split_axis=0, concat_axis=0, tiled=True)


def pass_on(value):
    count = lax.axis_size("blk")
    return lax.ppermute(value, "blk", [(b, (b + 1) % count) for b in range(count)])


def per_device(seed_field, segment_order, seg_disp, seg_kerr, seg_gain, seg_sat):
    t = tables()
    near_tables = {name: hold(jnp.asarray(value)) for name, value in t.items()}
    seed = seed_field.reshape(128, NT)

    ymodes = pl.pallas_call(
        ymode_kernel,
        out_shape=near(NS, 65, 1, 128),
        in_specs=[VMEM] * 8,
        out_specs=VMEM,
        name="ymode",
    )(
        seed, t["to_ymode"], t["lam_all"], segment_order.reshape(1, 1),
        *(each.reshape(1, 32) for each in (seg_disp, seg_gain, seg_sat, seg_kerr)),
    )
    gathered = exchange(ymodes)
    modes, side, tile = pl.pallas_call(
        xmode_kernel,
        out_shape=(near(136, NT), near(8, 128), near(NS, 1, 128)),
        in_specs=[VMEM] * 2,
        out_specs=(VMEM,) * 3,
        name="xmode",
    )(hold(gathered), near_tables["to_xmode"])
    shifted = pass_on(modes)
    weights = exchange(tile)
    factor = pl.pallas_call(
        lanczos_kernel,
        out_shape=near(8, 128),
        in_specs=[VMEM] * 3,
        out_specs=VMEM,
        cost_estimate=cost(6 * 2 * 512 * 256 * 256, 2**20),
        name="lanczos",
    )(hold(side), hold(weights), near_tables["lam_all"])
    shifted, factor = lax.optimization_barrier((shifted, factor))
    factor = pass_on(factor)
    dispersed = pl.pallas_call(
        disperse_kernel,
        out_shape=near(128, NT),
        in_specs=[VMEM] * 4,
        out_specs=VMEM,
        scratch_shapes=[pltpu.VMEM((512, 256), F32)] * 2,
        cost_estimate=cost(6 * 4 * 512 * 256 * 256, 2**20),
        name="disperse",
    )(hold(shifted), *(near_tables[name] for name in ("lines", "forward_split", "backward_split")))
    xback = pl.pallas_call(
        propagate_kernel,
        out_shape=near(NS, 8, NT),
        in_specs=[VMEM] * 3,
        out_specs=VMEM,
        scratch_shapes=[pltpu.VMEM((128, NT), F32)],
        name="propagate",
    )(hold(factor), hold(dispersed), near_tables["from_xmode"])
    rows = exchange(xback)
    result = pl.pallas_call(
        kerr_kernel,
        out_shape=jax.ShapeDtypeStruct((128, NT), F32),
        in_specs=[VMEM] * 6,
        out_specs=HBM,
        scratch_shapes=[pltpu.VMEM((128, NT), F32), pltpu.VMEM((64, NT), F32)]
        + [pltpu.VMEM((256, 256), F32)] * 2
        + [pltpu.VMEM((128, NT), F32), pltpu.SemaphoreType.DMA((8,))],
        name="kerr",
    )(
        hold(shifted), hold(rows),
        *(
            near_tables[name]
            for name in ("from_ymode", "lines", "forward_split", "backward_split")
        ),
    )
    return result.reshape(seed_field.shape)


def solution(mesh):
    in_specs = (P("blk", None, "shard", None, None), P("blk"), P(), P(), P(), P())
    out_specs = P("blk", None, "shard", None, None)
    return jax.shard_map(
        per_device, mesh=mesh, in_specs=in_specs, out_specs=out_specs, check_vma=False
    )
```

```python
import functools
import math

import jax
import jax.numpy as jnp
import numpy as np
from jax import lax
from jax.experimental import pallas as pl
from jax.experimental.pallas import tpu as pltpu
from jax.sharding import PartitionSpec as P

KRYLOV = 8
EXPANDED = 6
NS = 16
NG = 32
NT = 1024
NK = 8
WIDE = 2
NB = 128

epsilon = 1e-06
step_length = 2.5
grin_depth = 1.5
squarings = 8
taylor_terms = 10
gain_width = 0.25
loss_rate = 0.5
disp_scale = 60.0
raman_share = 0.18
raman_freq = 0.05
raman_damp = 0.035

F32 = jnp.float32
HIGHEST = lax.Precision.HIGHEST


@functools.cache
def tables():
    cell = (np.arange(NG) - (NG - 1) / 2.0) / (NG / 2.0)
    line = np.diag(-grin_depth * cell * cell)
    line = line + 0.5 * (np.eye(NG, k=1) + np.eye(NG, k=-1))
    values, q = np.linalg.eigh(line)

    to_ymode = np.zeros((NS, 2, 2, 2, 2, 2, NG))
    to_xmode = np.zeros((2, 2, NG, NS, 2, 2, 2))
    for part in range(2):
        for side in range(2):
            for jj in range(2):
                to_ymode[:, part, jj, side, part, side, :] = q[:, jj::2].T
                to_xmode[part, jj, :, :, part, jj, side] = q[side::2, :].T
    to_ymode = to_ymode.reshape(128, 128)
    to_xmode = to_xmode.reshape(128, 128)

    pair = values.reshape(NS, 2)
    lam = pair[:, None, :, None] + values[None, None, None, :] + np.zeros((1, 2, 1, 1))
    lam_all = lam.reshape(NS, 128)

    inner = np.arange(NB)
    angle = 2.0 * np.pi * ((inner[:, None] * inner[None, :]) % NB) / NB
    c, s = np.cos(angle), np.sin(angle)
    forward = np.block([[c, -s], [s, c]])
    backward = np.block([[c, s], [-s, c]])
    turn = 2.0 * np.pi * (np.arange(NK)[:, None] * inner[None, :]) / NT
    tw_cos, tw_sin = np.cos(turn), np.sin(turn)

    freq = np.arange(NK)[:, None] + NK * inner[None, :]
    signed = np.where(freq >= NT // 2, freq - NT, freq)
    w = signed / (NT / 2.0)
    resonance = raman_freq * raman_freq
    raman = resonance / (resonance - w * w - 1j * raman_damp * w)
    ram_re = raman.real / NT
    ram_im = np.where(signed == -(NT // 2), 0.0, raman.imag) / NT

    f32 = lambda a: np.ascontiguousarray(a, dtype=np.float32)
    return dict(
        to_ymode=widen(f32(to_ymode)),
        from_ymode=widen(f32(to_ymode.T)),
        to_xmode=widen(f32(to_xmode)),
        from_xmode=widen(f32(to_xmode.T)),
        lam_all=f32(lam_all),
        forward_split=split(f32(forward)),
        backward_split=split(f32(backward)),
        forward=f32(forward),
        backward=f32(backward),
        lines=f32(np.stack([tw_cos, tw_sin, w, ram_re, ram_im])),
    )


def split(table):
    high = table.astype(jnp.bfloat16)
    return np.stack([high, (table - high.astype(np.float32)).astype(jnp.bfloat16)])


def parts_of(value):
    high = value.astype(jnp.bfloat16)
    rest = value - high.astype(F32)
    middle = rest.astype(jnp.bfloat16)
    low = (rest - middle.astype(F32)).astype(jnp.bfloat16)
    return high, middle, low


def widen(table):
    high = table.astype(jnp.bfloat16)
    rest = table - high.astype(np.float32)
    middle = rest.astype(jnp.bfloat16)
    low = (rest - middle.astype(np.float32)).astype(jnp.bfloat16)
    return np.concatenate([high, middle, high], axis=1)


def mm_wide(table, b):
    high, middle, low = parts_of(b)
    stacked = jnp.concatenate([high, high, middle], axis=0)
    return jnp.dot(table, stacked, preferred_element_type=F32)


def mm_split(a, b_ref):
    high = a.astype(jnp.bfloat16)
    low = (a - high.astype(F32)).astype(jnp.bfloat16)
    dot = functools.partial(jnp.dot, preferred_element_type=F32)
    return dot(high, b_ref[0]) + (dot(high, b_ref[1]) + dot(low, b_ref[0]))


def mm(a, b):
    return jnp.dot(a, b, precision=HIGHEST, preferred_element_type=F32)


def fourier8(re, im, sign):
    def four(r, i):
        pr, pi = r[0] + r[2], i[0] + i[2]
        mr, mi = r[0] - r[2], i[0] - i[2]
        qr, qi = r[1] + r[3], i[1] + i[3]
        nr, ni = r[1] - r[3], i[1] - i[3]
        tr, ti = (-ni, nr) if sign > 0 else (ni, -nr)
        return (
            [pr + qr, mr + tr, pr - qr, mr - tr],
            [pi + qi, mi + ti, pi - qi, mi - ti],
        )

    er, ei = four(re[0::2], im[0::2])
    orr, oi = four(re[1::2], im[1::2])
    h = np.float32(np.sqrt(0.5))
    if sign > 0:
        w1 = ((orr[1] - oi[1]) * h, (orr[1] + oi[1]) * h)
        w2 = (-oi[2], orr[2])
        w3 = (-(orr[3] + oi[3]) * h, (orr[3] - oi[3]) * h)
    else:
        w1 = ((orr[1] + oi[1]) * h, (oi[1] - orr[1]) * h)
        w2 = (oi[2], -orr[2])
        w3 = ((oi[3] - orr[3]) * h, -(orr[3] + oi[3]) * h)
    tr = [orr[0], w1[0], w2[0], w3[0]]
    ti = [oi[0], w1[1], w2[1], w3[1]]
    out_r = [er[k] + tr[k] for k in range(4)] + [er[k] - tr[k] for k in range(4)]
    out_i = [ei[k] + ti[k] for k in range(4)] + [ei[k] - ti[k] for k in range(4)]
    return out_r, out_i


def outer_forward(load, rows, tw_ref, dest):
    for r0 in range(0, rows, 8):
        re = [load(0, r0, a) for a in range(NK)]
        im = [load(1, r0, a) for a in range(NK)]
        re, im = fourier8(re, im, -1)
        for k in range(NK):
            if k:
                c, s = tw_ref[0, k : k + 1, :], tw_ref[1, k : k + 1, :]
                re[k], im[k] = re[k] * c + im[k] * s, im[k] * c - re[k] * s
            dest[k * rows + r0 : k * rows + r0 + 8, 0:NB] = re[k]
            dest[k * rows + r0 : k * rows + r0 + 8, NB : 2 * NB] = im[k]


def outer_backward(src, rows, tw_ref, store):
    for r0 in range(0, rows, 8):
        re, im = [], []
        for k in range(NK):
            a = src[k * rows + r0 : k * rows + r0 + 8, 0:NB]
            b = src[k * rows + r0 : k * rows + r0 + 8, NB : 2 * NB]
            if k:
                c, s = tw_ref[0, k : k + 1, :], tw_ref[1, k : k + 1, :]
                a, b = a * c - b * s, a * s + b * c
            re.append(a)
            im.append(b)
        re, im = fourier8(re, im, 1)
        for a in range(NK):
            store(r0, a, re[a], im[a])


def filter_spectrum(spec, rows, factor_re, factor_im):
    for k in range(NK):
        fr, fi = factor_re[k : k + 1, :], factor_im[k : k + 1, :]
        lo, hi = k * rows, (k + 1) * rows
        a, b = spec[lo:hi, 0:NB], spec[lo:hi, NB : 2 * NB]
        spec[lo:hi, 0:NB] = a * fr - b * fi
        spec[lo:hi, NB : 2 * NB] = a * fi + b * fr


def whole_sum(value):
    return jnp.sum(jnp.sum(value, axis=0, keepdims=True), axis=1, keepdims=True)


def ymode_kernel(
    seed_ref, mat_ref, lam_ref, kind_ref, disp_ref, gain_ref, sat_ref, kerr_ref, out_ref
):
    total = jnp.zeros((8, 128), F32)
    for c0 in range(0, NK, WIDE):
        block = seed_ref[:, c0 * 128 : (c0 + WIDE) * 128]
        square = block * block
        modes = mm_wide(mat_ref[...], block)
        for c in range(WIDE):
            lanes = slice(c * 128, c * 128 + 128)
            for r in range(16):
                total = total + square[8 * r : 8 * r + 8, lanes]
            place = 8 * (c0 + c)
            for d in range(NS):
                out_ref[d, place : place + 8, 0, :] = modes[8 * d : 8 * d + 8, lanes]
    lane = lax.broadcasted_iota(jnp.int32, (NS, 128), 1)
    chosen = lax.broadcasted_iota(jnp.int32, (1, 32), 1) == kind_ref[...]
    side = jnp.where(lane < 64, lam_ref[...], whole_sum(total))
    for place, ref in ((65, disp_ref), (66, gain_ref), (67, sat_ref), (68, kerr_ref)):
        value = jnp.sum(jnp.where(chosen, ref[...], 0.0), axis=1, keepdims=True)
        side = jnp.where(lane == place, value, side)
    out_ref[:, 64, 0, :] = side


def xmode_kernel(in_ref, mat_ref, modes_ref, side_ref, tile_ref):
    square = jnp.zeros((128, 128), F32)
    for c0 in range(0, NK, WIDE):
        block = jnp.concatenate(
            [
                jnp.concatenate([in_ref[d, 8 * c : 8 * c + 8, 0, :] for d in range(NS)], axis=0)
                for c in range(c0, c0 + WIDE)
            ],
            axis=1,
        )
        modes = mm_wide(mat_ref[...], block)
        modes_ref[0:128, c0 * 128 : (c0 + WIDE) * 128] = modes
        for c in range(WIDE):
            square = square + modes[:, c * 128 : c * 128 + 128] ** 2
    both = square[0:64, :] + square[64:128, :]
    both = jnp.concatenate([both, both], axis=0)
    tile = jnp.sum(both.T, axis=0, keepdims=True)
    lane = lax.broadcasted_iota(jnp.int32, (1, 128), 1)
    sides = in_ref[:, 64, 0, :]
    side = jnp.where(lane == 64, jnp.sum(sides, axis=0, keepdims=True), sides[0:1, :])
    side_ref[...] = jnp.broadcast_to(side, (8, 128))
    modes_ref[128:136, 0:128] = jnp.broadcast_to(side, (8, 128))
    modes_ref[128:136, 128:NT] = jnp.zeros((8, NT - 128), F32)
    for d in range(NS):
        tile_ref[d] = tile


def turn(angle):
    count = jnp.floor(angle * np.float32(2.0 / np.pi) + 0.5)
    x = angle - count * 1.5703125
    x = x - count * 4.837512969970703e-4
    x = x - count * 7.549789948768648e-8
    x = jnp.clip(x, -0.8, 0.8)
    z = x * x
    sine = ((-1.9515295891e-4 * z + 8.3321608736e-3) * z - 1.6666654611e-1) * z * x + x
    cosine = ((2.443315711809948e-5 * z - 1.388731625493765e-3) * z + 4.166664568298827e-2) * z
    cosine = cosine * z - 0.5 * z + 1.0
    quarter = count.astype(jnp.int32)
    odd = (quarter & 1) == 1
    c, s = jnp.where(odd, sine, cosine), jnp.where(odd, cosine, sine)
    c = jnp.where(((quarter + 1) & 2) == 2, -c, c)
    s = jnp.where((quarter & 2) == 2, -s, s)
    return c, s


def disperse_kernel(
    modes_ref, tw_ref, fwd_ref, bwd_ref, out_ref, one, two
):

    def load(part, r0, a):
        return modes_ref[64 * part + r0 : 64 * part + r0 + 8, a * NB : (a + 1) * NB]

    outer_forward(load, 64, tw_ref, one)
    two[...] = mm_split(one[...], fwd_ref)

    energy = modes_ref[128:129, 64:65]
    dispersion, gain_peak = modes_ref[128:129, 65:66], modes_ref[128:129, 66:67]
    gain = gain_peak / (1.0 + energy / (NG * NG * NT) / modes_ref[128:129, 67:68])
    w = tw_ref[2]
    relative = w / gain_width
    amplitude = jnp.exp(0.5 * gain / (1.0 + relative * relative) - loss_rate) * (1.0 / NT)
    angle = disp_scale * dispersion * w * w
    filter_spectrum(two, 64, amplitude * jnp.cos(angle), amplitude * jnp.sin(angle))

    one[...] = mm_split(two[...], bwd_ref)

    def store(r0, a, re, im):
        out_ref[r0 : r0 + 8, a * NB : (a + 1) * NB] = re
        out_ref[64 + r0 : 64 + r0 + 8, a * NB : (a + 1) * NB] = im

    outer_backward(one, 64, tw_ref, store)


def small_product(a, b):
    total = a[:, 0:1] * b[0:1, :]
    for k in range(1, KRYLOV):
        total = total + a[:, k : k + 1] * b[k : k + 1, :]
    return total


def expanded_ratios():
    series = np.array([1.0 / math.factorial(k) for k in range(taylor_terms + 1)])
    series = series / 2.0 ** (EXPANDED * np.arange(taylor_terms + 1))
    for _ in range(EXPANDED):
        series = np.convolve(series, series)
    series = series[series >= np.finfo(np.float32).tiny]
    return [float(ratio) for ratio in series[1:] / series[:-1]]


def krylov_exp(diagonals, couplings):
    row = lax.broadcasted_iota(jnp.int32, (8, 128), 0)
    lane = lax.broadcasted_iota(jnp.int32, (8, 128), 1)
    zero = jnp.zeros((8, 128), F32)
    scale = step_length / 2.0 ** (squarings - EXPANDED)
    mid, low, high = zero, zero, zero
    for j in range(KRYLOV):
        mid = jnp.where(row == j, diagonals[j] * scale, mid)
        if j + 1 < KRYLOV:
            high = jnp.where(row == j, couplings[j] * scale, high)
            low = jnp.where(row == j + 1, couplings[j] * scale, low)
    term = jnp.where(row == lane, 1.0, 0.0).astype(F32)
    real, imag = term, zero
    for order, ratio in enumerate(expanded_ratios(), 1):
        term = mid * term + low * pltpu.roll(term, 1, 0) + high * pltpu.roll(term, 7, 0)
        term = term * ratio
        signed = -term if order % 4 in (2, 3) else term
        if order % 2:
            imag = imag + signed
        else:
            real = real + signed
    for _ in range(squarings - EXPANDED):
        real, imag = (
            small_product(real, real) - small_product(imag, imag),
            2.0 * small_product(real, imag),
        )
    return real, imag


def mode_gains(weight, lam, own):
    rest = jnp.sqrt(weight)
    grown = jnp.ones((8, 128), F32)
    diagonals, couplings, polys = [], [], []
    for step in range(KRYLOV):
        spread = lam * rest
        square = whole_sum(rest * rest) + epsilon
        diagonal = whole_sum(spread * rest)
        if step:
            overlap = whole_sum(rest * vector)
        inverse = lax.rsqrt(square)
        coupling = square * inverse
        diagonal = diagonal * inverse * inverse
        if step:
            diagonal = diagonal - overlap
        diagonals.append(diagonal)
        couplings.append(coupling)
        poly = grown * inverse
        polys.append(poly)
        if step + 1 < KRYLOV:
            rest = rest * inverse
            image = spread * inverse
            grown = own * poly
            if step:
                image = image - coupling * vector
                grown = grown - coupling * before
            vector, before = rest, poly
            rest = image - diagonal * vector
            grown = grown - diagonal * before
    scale_zero = couplings[0]
    real, imag = krylov_exp(diagonals, couplings[1:])
    gains = []
    for part in (real, imag):
        gain = part[0:1, 0:1] * polys[0]
        for j in range(1, KRYLOV):
            gain = gain + part[j : j + 1, 0:1] * polys[j]
        gains.append(gain * scale_zero)
    return gains


def lanczos_kernel(side_ref, weight_ref, lam_ref, factor_ref):
    lane = lax.broadcasted_iota(jnp.int32, (NS, 128), 1)
    own = jnp.where(lane[0:8, :] < 64, side_ref[...], pltpu.roll(side_ref[...], 64, 1))
    weight = jnp.where(lane < 64, weight_ref[:, 0, :], 0.0)
    gain_re, gain_im = mode_gains(weight, lam_ref[...], own)
    row = lax.broadcasted_iota(jnp.int32, (8, 128), 0)
    factor_ref[...] = jnp.where(row == 0, gain_re, gain_im)


def propagate_kernel(factor_ref, modes_ref, mat_ref, out_ref, scaled):
    gain_re, gain_im = (
        jnp.broadcast_to(factor_ref[row : row + 1, :], (128, 128)).T[0:64, :]
        for row in range(2)
    )
    for c0 in range(0, NK, WIDE):
        for c in range(c0, c0 + WIDE):
            lanes = slice(c * 128, c * 128 + 128)
            a, b = modes_ref[0:64, lanes], modes_ref[64:128, lanes]
            scaled[0:64, lanes] = gain_re * a - gain_im * b
            scaled[64:128, lanes] = gain_im * a + gain_re * b
        lanes = slice(c0 * 128, (c0 + WIDE) * 128)
        back = mm_wide(mat_ref[...], scaled[:, lanes])
        out_ref[:, :, lanes] = back.reshape(NS, 8, WIDE * 128)


def kerr_kernel(
    modes_ref, in_ref, mat_ref, tw_ref, fwd_ref, bwd_ref,
    out_ref, field, delayed, one, two, done, sems
):
    kerr = modes_ref[128:129, 68:69]
    field[...] = mm_wide(mat_ref[...], in_ref[...].reshape(128, NT))

    def load(side, r0, a):
        lanes = slice(a * NB, (a + 1) * NB)
        re = field[32 * side + r0 : 32 * side + r0 + 8, lanes]
        im = field[64 + 32 * side + r0 : 64 + 32 * side + r0 + 8, lanes]
        return re * re + im * im

    outer_forward(load, 32, tw_ref, one)
    two[...] = mm_split(one[...], fwd_ref)
    filter_spectrum(two, 32, tw_ref[3], tw_ref[4])
    one[...] = mm_split(two[...], bwd_ref)

    def store(r0, a, re, im):
        lanes = slice(a * NB, (a + 1) * NB)
        delayed[r0 : r0 + 8, lanes] = re
        delayed[32 + r0 : 32 + r0 + 8, lanes] = im

    outer_backward(one, 32, tw_ref, store)

    copies = []
    for r0 in range(0, 64, 8):
        re, im = field[r0 : r0 + 8, :], field[64 + r0 : 64 + r0 + 8, :]
        late = delayed[r0 : r0 + 8, :]
        rotation = kerr * ((1.0 - raman_share) * (re * re + im * im) + raman_share * late)
        c, s = turn(rotation)
        done[r0 : r0 + 8, :] = re * c - im * s
        done[64 + r0 : 64 + r0 + 8, :] = re * s + im * c
        if r0 % 16 == 8:
            for lo in (r0 - 8, 64 + r0 - 8):
                rows = pl.ds(lo, 16)
                copy = pltpu.make_async_copy(done.at[rows], out_ref.at[rows], sems.at[lo // 16])
                copy.start()
                copies.append(copy)
    for copy in copies:
        copy.wait()


VMEM = pl.BlockSpec(memory_space=pltpu.VMEM)
HBM = pl.BlockSpec(memory_space=pltpu.HBM)


def near(*shape):
    return pltpu.VMEM(shape, F32)


def hold(value):
    return pltpu.with_memory_space_constraint(value, pltpu.VMEM)


def cost(flops, moved):
    return pl.CostEstimate(flops=flops, bytes_accessed=moved, transcendentals=0)


def exchange(value):
    return lax.all_to_all(value, "shard", split_axis=0, concat_axis=0, tiled=True)


def pass_on(value):
    count = lax.axis_size("blk")
    return lax.ppermute(value, "blk", [(b, (b + 1) % count) for b in range(count)])


def per_device(seed_field, segment_order, seg_disp, seg_kerr, seg_gain, seg_sat):
    t = tables()
    near_tables = {name: hold(jnp.asarray(value)) for name, value in t.items()}
    seed = seed_field.reshape(128, NT)

    ymodes = pl.pallas_call(
        ymode_kernel,
        out_shape=near(NS, 65, 1, 128),
        in_specs=[VMEM] * 8,
        out_specs=VMEM,
        name="ymode",
    )(
        seed, t["to_ymode"], t["lam_all"], segment_order.reshape(1, 1),
        *(each.reshape(1, 32) for each in (seg_disp, seg_gain, seg_sat, seg_kerr)),
    )
    gathered = exchange(ymodes)
    modes, side, tile = pl.pallas_call(
        xmode_kernel,
        out_shape=(near(136, NT), near(8, 128), near(NS, 1, 128)),
        in_specs=[VMEM] * 2,
        out_specs=(VMEM,) * 3,
        name="xmode",
    )(hold(gathered), near_tables["to_xmode"])
    shifted = pass_on(modes)
    weights = exchange(tile)
    factor = pl.pallas_call(
        lanczos_kernel,
        out_shape=near(8, 128),
        in_specs=[VMEM] * 3,
        out_specs=VMEM,
        cost_estimate=cost(6 * 2 * 512 * 256 * 256, 2**20),
        name="lanczos",
    )(hold(side), hold(weights), near_tables["lam_all"])
    shifted, factor = lax.optimization_barrier((shifted, factor))
    factor = pass_on(factor)
    dispersed = pl.pallas_call(
        disperse_kernel,
        out_shape=near(128, NT),
        in_specs=[VMEM] * 4,
        out_specs=VMEM,
        scratch_shapes=[pltpu.VMEM((512, 256), F32)] * 2,
        cost_estimate=cost(6 * 4 * 512 * 256 * 256, 2**20),
        name="disperse",
    )(hold(shifted), *(near_tables[name] for name in ("lines", "forward_split", "backward_split")))
    xback = pl.pallas_call(
        propagate_kernel,
        out_shape=near(NS, 8, NT),
        in_specs=[VMEM] * 3,
        out_specs=VMEM,
        scratch_shapes=[pltpu.VMEM((128, NT), F32)],
        name="propagate",
    )(hold(factor), hold(dispersed), near_tables["from_xmode"])
    rows = exchange(xback)
    result = pl.pallas_call(
        kerr_kernel,
        out_shape=jax.ShapeDtypeStruct((128, NT), F32),
        in_specs=[VMEM] * 6,
        out_specs=HBM,
        scratch_shapes=[pltpu.VMEM((128, NT), F32), pltpu.VMEM((64, NT), F32)]
        + [pltpu.VMEM((256, 256), F32)] * 2
        + [pltpu.VMEM((128, NT), F32), pltpu.SemaphoreType.DMA((8,))],
        name="kerr",
    )(
        hold(shifted), hold(rows),
        *(
            near_tables[name]
            for name in ("from_ymode", "lines", "forward_split", "backward_split")
        ),
    )
    return result.reshape(seed_field.shape)


def solution(mesh):
    in_specs = (P("blk", None, "shard", None, None), P("blk"), P(), P(), P(), P())
    out_specs = P("blk", None, "shard", None, None)
    return jax.shard_map(
        per_device, mesh=mesh, in_specs=in_specs, out_specs=out_specs, check_vma=False
    )
```

```python
import functools
import math

import jax
import jax.numpy as jnp
import numpy as np
from jax import lax
from jax.experimental import pallas as pl
from jax.experimental.pallas import tpu as pltpu
from jax.sharding import PartitionSpec as P

KRYLOV = 8
EXPANDED = 6
NS = 16
NG = 32
NT = 1024
NK = 8
WIDE = 2
NB = 128

epsilon = 1e-06
step_length = 2.5
grin_depth = 1.5
squarings = 8
taylor_terms = 10
gain_width = 0.25
loss_rate = 0.5
disp_scale = 60.0
raman_share = 0.18
raman_freq = 0.05
raman_damp = 0.035

F32 = jnp.float32
HIGHEST = lax.Precision.HIGHEST


@functools.cache
def tables():
    cell = (np.arange(NG) - (NG - 1) / 2.0) / (NG / 2.0)
    line = np.diag(-grin_depth * cell * cell)
    line = line + 0.5 * (np.eye(NG, k=1) + np.eye(NG, k=-1))
    values, q = np.linalg.eigh(line)

    to_ymode = np.zeros((NS, 2, 2, 2, 2, 2, NG))
    to_xmode = np.zeros((2, 2, NG, NS, 2, 2, 2))
    for part in range(2):
        for side in range(2):
            for jj in range(2):
                to_ymode[:, part, jj, side, part, side, :] = q[:, jj::2].T
                to_xmode[part, jj, :, :, part, jj, side] = q[side::2, :].T
    to_ymode = to_ymode.reshape(128, 128)
    to_xmode = to_xmode.reshape(128, 128)

    pair = values.reshape(NS, 2)
    lam = pair[:, None, :, None] + values[None, None, None, :] + np.zeros((1, 2, 1, 1))
    lam_all = lam.reshape(NS, 128)

    inner = np.arange(NB)
    angle = 2.0 * np.pi * ((inner[:, None] * inner[None, :]) % NB) / NB
    c, s = np.cos(angle), np.sin(angle)
    forward = np.block([[c, -s], [s, c]])
    backward = np.block([[c, s], [-s, c]])
    turn = 2.0 * np.pi * (np.arange(NK)[:, None] * inner[None, :]) / NT
    tw_cos, tw_sin = np.cos(turn), np.sin(turn)

    freq = np.arange(NK)[:, None] + NK * inner[None, :]
    signed = np.where(freq >= NT // 2, freq - NT, freq)
    w = signed / (NT / 2.0)
    resonance = raman_freq * raman_freq
    raman = resonance / (resonance - w * w - 1j * raman_damp * w)
    ram_re = raman.real / NT
    ram_im = np.where(signed == -(NT // 2), 0.0, raman.imag) / NT

    f32 = lambda a: np.ascontiguousarray(a, dtype=np.float32)
    return dict(
        to_ymode=widen(f32(to_ymode)),
        from_ymode=widen(f32(to_ymode.T)),
        to_xmode=widen(f32(to_xmode)),
        from_xmode=widen(f32(to_xmode.T)),
        lam_all=f32(lam_all),
        forward_split=split(f32(forward)),
        backward_split=split(f32(backward)),
        forward=f32(forward),
        backward=f32(backward),
        lines=f32(np.stack([tw_cos, tw_sin, w, ram_re, ram_im])),
    )


def split(table):
    high = table.astype(jnp.bfloat16)
    return np.stack([high, (table - high.astype(np.float32)).astype(jnp.bfloat16)])


def parts_of(value):
    high = value.astype(jnp.bfloat16)
    rest = value - high.astype(F32)
    middle = rest.astype(jnp.bfloat16)
    low = (rest - middle.astype(F32)).astype(jnp.bfloat16)
    return high, middle, low


def widen(table):
    high = table.astype(jnp.bfloat16)
    rest = table - high.astype(np.float32)
    middle = rest.astype(jnp.bfloat16)
    low = (rest - middle.astype(np.float32)).astype(jnp.bfloat16)
    return np.concatenate([high, middle, high], axis=1)


def mm_wide(table, b):
    high, middle, low = parts_of(b)
    stacked = jnp.concatenate([high, high, middle], axis=0)
    return jnp.dot(table, stacked, preferred_element_type=F32)


def mm_split(a, b_ref):
    high = a.astype(jnp.bfloat16)
    low = (a - high.astype(F32)).astype(jnp.bfloat16)
    dot = functools.partial(jnp.dot, preferred_element_type=F32)
    return dot(high, b_ref[0]) + (dot(high, b_ref[1]) + dot(low, b_ref[0]))


def mm(a, b):
    return jnp.dot(a, b, precision=HIGHEST, preferred_element_type=F32)


def fourier8(re, im, sign):
    def four(r, i):
        pr, pi = r[0] + r[2], i[0] + i[2]
        mr, mi = r[0] - r[2], i[0] - i[2]
        qr, qi = r[1] + r[3], i[1] + i[3]
        nr, ni = r[1] - r[3], i[1] - i[3]
        tr, ti = (-ni, nr) if sign > 0 else (ni, -nr)
        return (
            [pr + qr, mr + tr, pr - qr, mr - tr],
            [pi + qi, mi + ti, pi - qi, mi - ti],
        )

    er, ei = four(re[0::2], im[0::2])
    orr, oi = four(re[1::2], im[1::2])
    h = np.float32(np.sqrt(0.5))
    if sign > 0:
        w1 = ((orr[1] - oi[1]) * h, (orr[1] + oi[1]) * h)
        w2 = (-oi[2], orr[2])
        w3 = (-(orr[3] + oi[3]) * h, (orr[3] - oi[3]) * h)
    else:
        w1 = ((orr[1] + oi[1]) * h, (oi[1] - orr[1]) * h)
        w2 = (oi[2], -orr[2])
        w3 = ((oi[3] - orr[3]) * h, -(orr[3] + oi[3]) * h)
    tr = [orr[0], w1[0], w2[0], w3[0]]
    ti = [oi[0], w1[1], w2[1], w3[1]]
    out_r = [er[k] + tr[k] for k in range(4)] + [er[k] - tr[k] for k in range(4)]
    out_i = [ei[k] + ti[k] for k in range(4)] + [ei[k] - ti[k] for k in range(4)]
    return out_r, out_i


def outer_forward(load, rows, tw_ref, dest):
    for r0 in range(0, rows, 8):
        re = [load(0, r0, a) for a in range(NK)]
        im = [load(1, r0, a) for a in range(NK)]
        re, im = fourier8(re, im, -1)
        for k in range(NK):
            if k:
                c, s = tw_ref[0, k : k + 1, :], tw_ref[1, k : k + 1, :]
                re[k], im[k] = re[k] * c + im[k] * s, im[k] * c - re[k] * s
            dest[k * rows + r0 : k * rows + r0 + 8, 0:NB] = re[k]
            dest[k * rows + r0 : k * rows + r0 + 8, NB : 2 * NB] = im[k]


def outer_backward(src, rows, tw_ref, store):
    for r0 in range(0, rows, 8):
        re, im = [], []
        for k in range(NK):
            a = src[k * rows + r0 : k * rows + r0 + 8, 0:NB]
            b = src[k * rows + r0 : k * rows + r0 + 8, NB : 2 * NB]
            if k:
                c, s = tw_ref[0, k : k + 1, :], tw_ref[1, k : k + 1, :]
                a, b = a * c - b * s, a * s + b * c
            re.append(a)
            im.append(b)
        re, im = fourier8(re, im, 1)
        for a in range(NK):
            store(r0, a, re[a], im[a])


def filter_spectrum(spec, rows, factor_re, factor_im):
    for k in range(NK):
        fr, fi = factor_re[k : k + 1, :], factor_im[k : k + 1, :]
        lo, hi = k * rows, (k + 1) * rows
        a, b = spec[lo:hi, 0:NB], spec[lo:hi, NB : 2 * NB]
        spec[lo:hi, 0:NB] = a * fr - b * fi
        spec[lo:hi, NB : 2 * NB] = a * fi + b * fr


def whole_sum(value):
    return jnp.sum(jnp.sum(value, axis=0, keepdims=True), axis=1, keepdims=True)


def ymode_kernel(
    seed_ref, mat_ref, lam_ref, kind_ref, disp_ref, gain_ref, sat_ref, kerr_ref, out_ref
):
    total = jnp.zeros((8, 128), F32)
    for c0 in range(0, NK, WIDE):
        block = seed_ref[:, c0 * 128 : (c0 + WIDE) * 128]
        square = block * block
        modes = mm_wide(mat_ref[...], block)
        for c in range(WIDE):
            lanes = slice(c * 128, c * 128 + 128)
            for r in range(16):
                total = total + square[8 * r : 8 * r + 8, lanes]
            place = 8 * (c0 + c)
            for d in range(NS):
                out_ref[d, place : place + 8, 0, :] = modes[8 * d : 8 * d + 8, lanes]
    lane = lax.broadcasted_iota(jnp.int32, (NS, 128), 1)
    chosen = lax.broadcasted_iota(jnp.int32, (1, 32), 1) == kind_ref[...]
    side = jnp.where(lane < 64, lam_ref[...], whole_sum(total))
    for place, ref in ((65, disp_ref), (66, gain_ref), (67, sat_ref), (68, kerr_ref)):
        value = jnp.sum(jnp.where(chosen, ref[...], 0.0), axis=1, keepdims=True)
        side = jnp.where(lane == place, value, side)
    out_ref[:, 64, 0, :] = side


def xmode_kernel(in_ref, mat_ref, modes_ref, side_ref, tile_ref):
    square = jnp.zeros((128, 128), F32)
    for c0 in range(0, NK, WIDE):
        block = jnp.concatenate(
            [
                jnp.concatenate([in_ref[d, 8 * c : 8 * c + 8, 0, :] for d in range(NS)], axis=0)
                for c in range(c0, c0 + WIDE)
            ],
            axis=1,
        )
        modes = mm_wide(mat_ref[...], block)
        modes_ref[0:128, c0 * 128 : (c0 + WIDE) * 128] = modes
        for c in range(WIDE):
            square = square + modes[:, c * 128 : c * 128 + 128] ** 2
    both = square[0:64, :] + square[64:128, :]
    both = jnp.concatenate([both, both], axis=0)
    tile = jnp.sum(both.T, axis=0, keepdims=True)
    lane = lax.broadcasted_iota(jnp.int32, (1, 128), 1)
    sides = in_ref[:, 64, 0, :]
    side = jnp.where(lane == 64, jnp.sum(sides, axis=0, keepdims=True), sides[0:1, :])
    side_ref[...] = jnp.broadcast_to(side, (8, 128))
    modes_ref[128:136, 0:128] = jnp.broadcast_to(side, (8, 128))
    modes_ref[128:136, 128:NT] = jnp.zeros((8, NT - 128), F32)
    for d in range(NS):
        tile_ref[d] = tile


def turn(angle):
    count = jnp.floor(angle * np.float32(2.0 / np.pi) + 0.5)
    x = angle - count * 1.5703125
    x = x - count * 4.837512969970703e-4
    x = x - count * 7.549789948768648e-8
    x = jnp.clip(x, -0.8, 0.8)
    z = x * x
    sine = ((-1.9515295891e-4 * z + 8.3321608736e-3) * z - 1.6666654611e-1) * z * x + x
    cosine = ((2.443315711809948e-5 * z - 1.388731625493765e-3) * z + 4.166664568298827e-2) * z
    cosine = cosine * z - 0.5 * z + 1.0
    quarter = count.astype(jnp.int32)
    odd = (quarter & 1) == 1
    c, s = jnp.where(odd, sine, cosine), jnp.where(odd, cosine, sine)
    c = jnp.where(((quarter + 1) & 2) == 2, -c, c)
    s = jnp.where((quarter & 2) == 2, -s, s)
    return c, s


def disperse_kernel(
    modes_ref, tw_ref, fwd_ref, bwd_ref, out_ref, one, two
):

    def load(part, r0, a):
        return modes_ref[64 * part + r0 : 64 * part + r0 + 8, a * NB : (a + 1) * NB]

    outer_forward(load, 64, tw_ref, one)
    two[...] = mm_split(one[...], fwd_ref)

    energy = modes_ref[128:129, 64:65]
    dispersion, gain_peak = modes_ref[128:129, 65:66], modes_ref[128:129, 66:67]
    gain = gain_peak / (1.0 + energy / (NG * NG * NT) / modes_ref[128:129, 67:68])
    w = tw_ref[2]
    relative = w / gain_width
    amplitude = jnp.exp(0.5 * gain / (1.0 + relative * relative) - loss_rate) * (1.0 / NT)
    angle = disp_scale * dispersion * w * w
    filter_spectrum(two, 64, amplitude * jnp.cos(angle), amplitude * jnp.sin(angle))

    one[...] = mm_split(two[...], bwd_ref)

    def store(r0, a, re, im):
        out_ref[r0 : r0 + 8, a * NB : (a + 1) * NB] = re
        out_ref[64 + r0 : 64 + r0 + 8, a * NB : (a + 1) * NB] = im

    outer_backward(one, 64, tw_ref, store)


def small_product(a, b):
    total = a[:, 0:1] * b[0:1, :]
    for k in range(1, KRYLOV):
        total = total + a[:, k : k + 1] * b[k : k + 1, :]
    return total


def expanded_ratios():
    series = np.array([1.0 / math.factorial(k) for k in range(taylor_terms + 1)])
    series = series / 2.0 ** (EXPANDED * np.arange(taylor_terms + 1))
    for _ in range(EXPANDED):
        series = np.convolve(series, series)
    series = series[series >= np.finfo(np.float32).tiny]
    return [float(ratio) for ratio in series[1:] / series[:-1]]


def krylov_exp(diagonals, couplings):
    row = lax.broadcasted_iota(jnp.int32, (8, 128), 0)
    lane = lax.broadcasted_iota(jnp.int32, (8, 128), 1)
    zero = jnp.zeros((8, 128), F32)
    scale = step_length / 2.0 ** (squarings - EXPANDED)
    mid, low, high = zero, zero, zero
    for j in range(KRYLOV):
        mid = jnp.where(row == j, diagonals[j] * scale, mid)
        if j + 1 < KRYLOV:
            high = jnp.where(row == j, couplings[j] * scale, high)
            low = jnp.where(row == j + 1, couplings[j] * scale, low)
    term = jnp.where(row == lane, 1.0, 0.0).astype(F32)
    real, imag = term, zero
    for order, ratio in enumerate(expanded_ratios(), 1):
        term = mid * term + low * pltpu.roll(term, 1, 0) + high * pltpu.roll(term, 7, 0)
        term = term * ratio
        signed = -term if order % 4 in (2, 3) else term
        if order % 2:
            imag = imag + signed
        else:
            real = real + signed
    for _ in range(squarings - EXPANDED):
        real, imag = (
            small_product(real, real) - small_product(imag, imag),
            2.0 * small_product(real, imag),
        )
    return real, imag


def mode_gains(weight, lam, own):
    rest = jnp.sqrt(weight)
    grown = jnp.ones((8, 128), F32)
    diagonals, couplings, polys = [], [], []
    for step in range(KRYLOV):
        spread = lam * rest
        square = whole_sum(rest * rest) + epsilon
        diagonal = whole_sum(spread * rest)
        if step:
            overlap = whole_sum(rest * vector)
        inverse = lax.rsqrt(square)
        coupling = square * inverse
        diagonal = diagonal * inverse * inverse
        if step:
            diagonal = diagonal - overlap
        diagonals.append(diagonal)
        couplings.append(coupling)
        poly = grown * inverse
        polys.append(poly)
        if step + 1 < KRYLOV:
            rest = rest * inverse
            image = spread * inverse
            grown = own * poly
            if step:
                image = image - coupling * vector
                grown = grown - coupling * before
            vector, before = rest, poly
            rest = image - diagonal * vector
            grown = grown - diagonal * before
    scale_zero = couplings[0]
    real, imag = krylov_exp(diagonals, couplings[1:])
    gains = []
    for part in (real, imag):
        gain = part[0:1, 0:1] * polys[0]
        for j in range(1, KRYLOV):
            gain = gain + part[j : j + 1, 0:1] * polys[j]
        gains.append(gain * scale_zero)
    return gains


def lanczos_kernel(side_ref, weight_ref, lam_ref, factor_ref):
    lane = lax.broadcasted_iota(jnp.int32, (NS, 128), 1)
    own = jnp.where(lane[0:8, :] < 64, side_ref[...], pltpu.roll(side_ref[...], 64, 1))
    weight = jnp.where(lane < 64, weight_ref[:, 0, :], 0.0)
    gain_re, gain_im = mode_gains(weight, lam_ref[...], own)
    row = lax.broadcasted_iota(jnp.int32, (8, 128), 0)
    factor_ref[...] = jnp.where(row == 0, gain_re, gain_im)


def propagate_kernel(factor_ref, modes_ref, mat_ref, out_ref, scaled):
    gain_re, gain_im = (
        jnp.broadcast_to(factor_ref[row : row + 1, :], (128, 128)).T[0:64, :]
        for row in range(2)
    )
    for c0 in range(0, NK, WIDE):
        for c in range(c0, c0 + WIDE):
            lanes = slice(c * 128, c * 128 + 128)
            a, b = modes_ref[0:64, lanes], modes_ref[64:128, lanes]
            scaled[0:64, lanes] = gain_re * a - gain_im * b
            scaled[64:128, lanes] = gain_im * a + gain_re * b
        lanes = slice(c0 * 128, (c0 + WIDE) * 128)
        back = mm_wide(mat_ref[...], scaled[:, lanes])
        out_ref[:, :, lanes] = back.reshape(NS, 8, WIDE * 128)


def kerr_kernel(
    modes_ref, in_ref, mat_ref, tw_ref, fwd_ref, bwd_ref,
    out_ref, field, delayed, one, two, done, sems
):
    kerr = modes_ref[128:129, 68:69]
    field[...] = mm_wide(mat_ref[...], in_ref[...].reshape(128, NT))

    def load(side, r0, a):
        lanes = slice(a * NB, (a + 1) * NB)
        re = field[32 * side + r0 : 32 * side + r0 + 8, lanes]
        im = field[64 + 32 * side + r0 : 64 + 32 * side + r0 + 8, lanes]
        return re * re + im * im

    outer_forward(load, 32, tw_ref, one)
    two[...] = mm_split(one[...], fwd_ref)
    filter_spectrum(two, 32, tw_ref[3], tw_ref[4])
    one[...] = mm_split(two[...], bwd_ref)

    def store(r0, a, re, im):
        lanes = slice(a * NB, (a + 1) * NB)
        delayed[r0 : r0 + 8, lanes] = re
        delayed[32 + r0 : 32 + r0 + 8, lanes] = im

    outer_backward(one, 32, tw_ref, store)

    copies = []
    for r0 in range(0, 64, 8):
        re, im = field[r0 : r0 + 8, :], field[64 + r0 : 64 + r0 + 8, :]
        late = delayed[r0 : r0 + 8, :]
        rotation = kerr * ((1.0 - raman_share) * (re * re + im * im) + raman_share * late)
        c, s = turn(rotation)
        done[r0 : r0 + 8, :] = re * c - im * s
        done[64 + r0 : 64 + r0 + 8, :] = re * s + im * c
        if r0 % 16 == 8:
            for lo in (r0 - 8, 64 + r0 - 8):
                rows = pl.ds(lo, 16)
                copy = pltpu.make_async_copy(done.at[rows], out_ref.at[rows], sems.at[lo // 16])
                copy.start()
                copies.append(copy)
    for copy in copies:
        copy.wait()


VMEM = pl.BlockSpec(memory_space=pltpu.VMEM)
HBM = pl.BlockSpec(memory_space=pltpu.HBM)


def near(*shape):
    return pltpu.VMEM(shape, F32)


def hold(value):
    return pltpu.with_memory_space_constraint(value, pltpu.VMEM)


def cost(flops, moved):
    return pl.CostEstimate(flops=flops, bytes_accessed=moved, transcendentals=0)


def exchange(value):
    return lax.all_to_all(value, "shard", split_axis=0, concat_axis=0, tiled=True)


def pass_on(value):
    count = lax.axis_size("blk")
    return lax.ppermute(value, "blk", [(b, (b + 1) % count) for b in range(count)])


def per_device(seed_field, segment_order, seg_disp, seg_kerr, seg_gain, seg_sat):
    t = tables()
    near_tables = {name: hold(jnp.asarray(value)) for name, value in t.items()}
    seed = seed_field.reshape(128, NT)

    ymodes = pl.pallas_call(
        ymode_kernel,
        out_shape=near(NS, 65, 1, 128),
        in_specs=[VMEM] * 8,
        out_specs=VMEM,
        name="ymode",
    )(
        seed, t["to_ymode"], t["lam_all"], segment_order.reshape(1, 1),
        *(each.reshape(1, 32) for each in (seg_disp, seg_gain, seg_sat, seg_kerr)),
    )
    gathered = exchange(ymodes)
    modes, side, tile = pl.pallas_call(
        xmode_kernel,
        out_shape=(near(136, NT), near(8, 128), near(NS, 1, 128)),
        in_specs=[VMEM] * 2,
        out_specs=(VMEM,) * 3,
        name="xmode",
    )(hold(gathered), near_tables["to_xmode"])
    shifted = pass_on(modes)
    weights = exchange(tile)
    factor = pl.pallas_call(
        lanczos_kernel,
        out_shape=near(8, 128),
        in_specs=[VMEM] * 3,
        out_specs=VMEM,
        cost_estimate=cost(6 * 2 * 512 * 256 * 256, 2**20),
        name="lanczos",
    )(hold(side), hold(weights), near_tables["lam_all"])
    factor = pass_on(factor)
    dispersed = pl.pallas_call(
        disperse_kernel,
        out_shape=near(128, NT),
        in_specs=[VMEM] * 4,
        out_specs=VMEM,
        scratch_shapes=[pltpu.VMEM((512, 256), F32)] * 2,
        cost_estimate=cost(6 * 4 * 512 * 256 * 256, 2**20),
        name="disperse",
    )(hold(shifted), *(near_tables[name] for name in ("lines", "forward_split", "backward_split")))
    xback = pl.pallas_call(
        propagate_kernel,
        out_shape=near(NS, 8, NT),
        in_specs=[VMEM] * 3,
        out_specs=VMEM,
        scratch_shapes=[pltpu.VMEM((128, NT), F32)],
        name="propagate",
    )(hold(factor), hold(dispersed), near_tables["from_xmode"])
    rows = exchange(xback)
    result = pl.pallas_call(
        kerr_kernel,
        out_shape=jax.ShapeDtypeStruct((128, NT), F32),
        in_specs=[VMEM] * 6,
        out_specs=HBM,
        scratch_shapes=[pltpu.VMEM((128, NT), F32), pltpu.VMEM((64, NT), F32)]
        + [pltpu.VMEM((256, 256), F32)] * 2
        + [pltpu.VMEM((128, NT), F32), pltpu.SemaphoreType.DMA((8,))],
        name="kerr",
    )(
        hold(shifted), hold(rows),
        *(
            near_tables[name]
            for name in ("from_ymode", "lines", "forward_split", "backward_split")
        ),
    )
    return result.reshape(seed_field.shape)


def solution(mesh):
    in_specs = (P("blk", None, "shard", None, None), P("blk"), P(), P(), P(), P())
    out_specs = P("blk", None, "shard", None, None)
    return jax.shard_map(
        per_device, mesh=mesh, in_specs=in_specs, out_specs=out_specs, check_vma=False
    )
```

```python
import functools
import math

import jax
import jax.numpy as jnp
import numpy as np
from jax import lax
from jax.experimental import pallas as pl
from jax.experimental.pallas import tpu as pltpu
from jax.sharding import PartitionSpec as P

KRYLOV = 8
EXPANDED = 6
NS = 16
NG = 32
NT = 1024
NK = 8
WIDE = 2
NB = 128

epsilon = 1e-06
step_length = 2.5
grin_depth = 1.5
squarings = 8
taylor_terms = 10
gain_width = 0.25
loss_rate = 0.5
disp_scale = 60.0
raman_share = 0.18
raman_freq = 0.05
raman_damp = 0.035

F32 = jnp.float32
HIGHEST = lax.Precision.HIGHEST


@functools.cache
def tables():
    cell = (np.arange(NG) - (NG - 1) / 2.0) / (NG / 2.0)
    line = np.diag(-grin_depth * cell * cell)
    line = line + 0.5 * (np.eye(NG, k=1) + np.eye(NG, k=-1))
    values, q = np.linalg.eigh(line)

    to_ymode = np.zeros((NS, 2, 2, 2, 2, 2, NG))
    to_xmode = np.zeros((2, 2, NG, NS, 2, 2, 2))
    for part in range(2):
        for side in range(2):
            for jj in range(2):
                to_ymode[:, part, jj, side, part, side, :] = q[:, jj::2].T
                to_xmode[part, jj, :, :, part, jj, side] = q[side::2, :].T
    to_ymode = to_ymode.reshape(128, 128)
    to_xmode = to_xmode.reshape(128, 128)

    pair = values.reshape(NS, 2)
    lam = pair[:, None, :, None] + values[None, None, None, :] + np.zeros((1, 2, 1, 1))
    lam_all = lam.reshape(NS, 128)

    inner = np.arange(NB)
    angle = 2.0 * np.pi * ((inner[:, None] * inner[None, :]) % NB) / NB
    c, s = np.cos(angle), np.sin(angle)
    forward = np.block([[c, -s], [s, c]])
    backward = np.block([[c, s], [-s, c]])
    turn = 2.0 * np.pi * (np.arange(NK)[:, None] * inner[None, :]) / NT
    tw_cos, tw_sin = np.cos(turn), np.sin(turn)

    freq = np.arange(NK)[:, None] + NK * inner[None, :]
    signed = np.where(freq >= NT // 2, freq - NT, freq)
    w = signed / (NT / 2.0)
    resonance = raman_freq * raman_freq
    raman = resonance / (resonance - w * w - 1j * raman_damp * w)
    ram_re = raman.real / NT
    ram_im = np.where(signed == -(NT // 2), 0.0, raman.imag) / NT

    f32 = lambda a: np.ascontiguousarray(a, dtype=np.float32)
    return dict(
        to_ymode=widen(f32(to_ymode)),
        from_ymode=widen(f32(to_ymode.T)),
        to_xmode=widen(f32(to_xmode)),
        from_xmode=widen(f32(to_xmode.T)),
        lam_all=f32(lam_all),
        forward_split=split(f32(forward)),
        backward_split=split(f32(backward)),
        forward=f32(forward),
        backward=f32(backward),
        lines=f32(np.stack([tw_cos, tw_sin, w, ram_re, ram_im])),
    )


def split(table):
    high = table.astype(jnp.bfloat16)
    return np.stack([high, (table - high.astype(np.float32)).astype(jnp.bfloat16)])


def parts_of(value):
    high = value.astype(jnp.bfloat16)
    rest = value - high.astype(F32)
    middle = rest.astype(jnp.bfloat16)
    low = (rest - middle.astype(F32)).astype(jnp.bfloat16)
    return high, middle, low


def widen(table):
    high = table.astype(jnp.bfloat16)
    rest = table - high.astype(np.float32)
    middle = rest.astype(jnp.bfloat16)
    low = (rest - middle.astype(np.float32)).astype(jnp.bfloat16)
    return np.concatenate([high, middle, high], axis=1)


def mm_wide(table, b):
    high, middle, low = parts_of(b)
    stacked = jnp.concatenate([high, high, middle], axis=0)
    return jnp.dot(table, stacked, preferred_element_type=F32)


def mm_split(a, b_ref):
    high = a.astype(jnp.bfloat16)
    low = (a - high.astype(F32)).astype(jnp.bfloat16)
    dot = functools.partial(jnp.dot, preferred_element_type=F32)
    return dot(high, b_ref[0]) + (dot(high, b_ref[1]) + dot(low, b_ref[0]))


def mm(a, b):
    return jnp.dot(a, b, precision=HIGHEST, preferred_element_type=F32)


def fourier8(re, im, sign):
    def four(r, i):
        pr, pi = r[0] + r[2], i[0] + i[2]
        mr, mi = r[0] - r[2], i[0] - i[2]
        qr, qi = r[1] + r[3], i[1] + i[3]
        nr, ni = r[1] - r[3], i[1] - i[3]
        tr, ti = (-ni, nr) if sign > 0 else (ni, -nr)
        return (
            [pr + qr, mr + tr, pr - qr, mr - tr],
            [pi + qi, mi + ti, pi - qi, mi - ti],
        )

    er, ei = four(re[0::2], im[0::2])
    orr, oi = four(re[1::2], im[1::2])
    h = np.float32(np.sqrt(0.5))
    if sign > 0:
        w1 = ((orr[1] - oi[1]) * h, (orr[1] + oi[1]) * h)
        w2 = (-oi[2], orr[2])
        w3 = (-(orr[3] + oi[3]) * h, (orr[3] - oi[3]) * h)
    else:
        w1 = ((orr[1] + oi[1]) * h, (oi[1] - orr[1]) * h)
        w2 = (oi[2], -orr[2])
        w3 = ((oi[3] - orr[3]) * h, -(orr[3] + oi[3]) * h)
    tr = [orr[0], w1[0], w2[0], w3[0]]
    ti = [oi[0], w1[1], w2[1], w3[1]]
    out_r = [er[k] + tr[k] for k in range(4)] + [er[k] - tr[k] for k in range(4)]
    out_i = [ei[k] + ti[k] for k in range(4)] + [ei[k] - ti[k] for k in range(4)]
    return out_r, out_i


def outer_forward(load, rows, tw_ref, dest):
    for r0 in range(0, rows, 8):
        re = [load(0, r0, a) for a in range(NK)]
        im = [load(1, r0, a) for a in range(NK)]
        re, im = fourier8(re, im, -1)
        for k in range(NK):
            if k:
                c, s = tw_ref[0, k : k + 1, :], tw_ref[1, k : k + 1, :]
                re[k], im[k] = re[k] * c + im[k] * s, im[k] * c - re[k] * s
            dest[k * rows + r0 : k * rows + r0 + 8, 0:NB] = re[k]
            dest[k * rows + r0 : k * rows + r0 + 8, NB : 2 * NB] = im[k]


def outer_backward(src, rows, tw_ref, store):
    for r0 in range(0, rows, 8):
        re, im = [], []
        for k in range(NK):
            a = src[k * rows + r0 : k * rows + r0 + 8, 0:NB]
            b = src[k * rows + r0 : k * rows + r0 + 8, NB : 2 * NB]
            if k:
                c, s = tw_ref[0, k : k + 1, :], tw_ref[1, k : k + 1, :]
                a, b = a * c - b * s, a * s + b * c
            re.append(a)
            im.append(b)
        re, im = fourier8(re, im, 1)
        for a in range(NK):
            store(r0, a, re[a], im[a])


def filter_spectrum(spec, rows, factor_re, factor_im):
    for k in range(NK):
        fr, fi = factor_re[k : k + 1, :], factor_im[k : k + 1, :]
        lo, hi = k * rows, (k + 1) * rows
        a, b = spec[lo:hi, 0:NB], spec[lo:hi, NB : 2 * NB]
        spec[lo:hi, 0:NB] = a * fr - b * fi
        spec[lo:hi, NB : 2 * NB] = a * fi + b * fr


def whole_sum(value):
    return jnp.sum(jnp.sum(value, axis=0, keepdims=True), axis=1, keepdims=True)


def ymode_kernel(
    seed_ref, mat_ref, lam_ref, kind_ref, disp_ref, gain_ref, sat_ref, kerr_ref, out_ref
):
    total = jnp.zeros((8, 128), F32)
    for c0 in range(0, NK, WIDE):
        block = seed_ref[:, c0 * 128 : (c0 + WIDE) * 128]
        square = block * block
        modes = mm_wide(mat_ref[...], block)
        for c in range(WIDE):
            lanes = slice(c * 128, c * 128 + 128)
            for r in range(16):
                total = total + square[8 * r : 8 * r + 8, lanes]
            place = 8 * (c0 + c)
            for d in range(NS):
                out_ref[d, place : place + 8, 0, :] = modes[8 * d : 8 * d + 8, lanes]
    lane = lax.broadcasted_iota(jnp.int32, (NS, 128), 1)
    chosen = lax.broadcasted_iota(jnp.int32, (1, 32), 1) == kind_ref[...]
    side = jnp.where(lane < 64, lam_ref[...], whole_sum(total))
    for place, ref in ((65, disp_ref), (66, gain_ref), (67, sat_ref), (68, kerr_ref)):
        value = jnp.sum(jnp.where(chosen, ref[...], 0.0), axis=1, keepdims=True)
        side = jnp.where(lane == place, value, side)
    out_ref[:, 64, 0, :] = side


def xmode_kernel(in_ref, mat_ref, modes_ref, side_ref, tile_ref):
    square = jnp.zeros((128, 128), F32)
    for c0 in range(0, NK, WIDE):
        block = jnp.concatenate(
            [
                jnp.concatenate([in_ref[d, 8 * c : 8 * c + 8, 0, :] for d in range(NS)], axis=0)
                for c in range(c0, c0 + WIDE)
            ],
            axis=1,
        )
        modes = mm_wide(mat_ref[...], block)
        modes_ref[0:128, c0 * 128 : (c0 + WIDE) * 128] = modes
        for c in range(WIDE):
            square = square + modes[:, c * 128 : c * 128 + 128] ** 2
    both = square[0:64, :] + square[64:128, :]
    both = jnp.concatenate([both, both], axis=0)
    tile = jnp.sum(both.T, axis=0, keepdims=True)
    lane = lax.broadcasted_iota(jnp.int32, (1, 128), 1)
    sides = in_ref[:, 64, 0, :]
    side = jnp.where(lane == 64, jnp.sum(sides, axis=0, keepdims=True), sides[0:1, :])
    side_ref[...] = jnp.broadcast_to(side, (8, 128))
    modes_ref[128:136, 0:128] = jnp.broadcast_to(side, (8, 128))
    modes_ref[128:136, 128:NT] = jnp.zeros((8, NT - 128), F32)
    for d in range(NS):
        tile_ref[d] = tile


def turn(angle):
    count = jnp.floor(angle * np.float32(2.0 / np.pi) + 0.5)
    x = angle - count * 1.5703125
    x = x - count * 4.837512969970703e-4
    x = x - count * 7.549789948768648e-8
    x = jnp.clip(x, -0.8, 0.8)
    z = x * x
    sine = ((-1.9515295891e-4 * z + 8.3321608736e-3) * z - 1.6666654611e-1) * z * x + x
    cosine = ((2.443315711809948e-5 * z - 1.388731625493765e-3) * z + 4.166664568298827e-2) * z
    cosine = cosine * z - 0.5 * z + 1.0
    quarter = count.astype(jnp.int32)
    odd = (quarter & 1) == 1
    c, s = jnp.where(odd, sine, cosine), jnp.where(odd, cosine, sine)
    c = jnp.where(((quarter + 1) & 2) == 2, -c, c)
    s = jnp.where((quarter & 2) == 2, -s, s)
    return c, s


def disperse_kernel(
    modes_ref, tw_ref, fwd_ref, bwd_ref, out_ref, one, two
):

    def load(part, r0, a):
        return modes_ref[64 * part + r0 : 64 * part + r0 + 8, a * NB : (a + 1) * NB]

    outer_forward(load, 64, tw_ref, one)
    two[...] = mm_split(one[...], fwd_ref)

    energy = modes_ref[128:129, 64:65]
    dispersion, gain_peak = modes_ref[128:129, 65:66], modes_ref[128:129, 66:67]
    gain = gain_peak / (1.0 + energy / (NG * NG * NT) / modes_ref[128:129, 67:68])
    w = tw_ref[2]
    relative = w / gain_width
    amplitude = jnp.exp(0.5 * gain / (1.0 + relative * relative) - loss_rate) * (1.0 / NT)
    angle = disp_scale * dispersion * w * w
    filter_spectrum(two, 64, amplitude * jnp.cos(angle), amplitude * jnp.sin(angle))

    one[...] = mm_split(two[...], bwd_ref)

    def store(r0, a, re, im):
        out_ref[r0 : r0 + 8, a * NB : (a + 1) * NB] = re
        out_ref[64 + r0 : 64 + r0 + 8, a * NB : (a + 1) * NB] = im

    outer_backward(one, 64, tw_ref, store)


def small_product(a, b):
    total = a[:, 0:1] * b[0:1, :]
    for k in range(1, KRYLOV):
        total = total + a[:, k : k + 1] * b[k : k + 1, :]
    return total


def expanded_ratios():
    series = np.array([1.0 / math.factorial(k) for k in range(taylor_terms + 1)])
    series = series / 2.0 ** (EXPANDED * np.arange(taylor_terms + 1))
    for _ in range(EXPANDED):
        series = np.convolve(series, series)
    series = series[series >= np.finfo(np.float32).tiny]
    return [float(ratio) for ratio in series[1:] / series[:-1]]


def krylov_exp(diagonals, couplings):
    row = lax.broadcasted_iota(jnp.int32, (8, 128), 0)
    lane = lax.broadcasted_iota(jnp.int32, (8, 128), 1)
    zero = jnp.zeros((8, 128), F32)
    scale = step_length / 2.0 ** (squarings - EXPANDED)
    mid, low, high = zero, zero, zero
    for j in range(KRYLOV):
        mid = jnp.where(row == j, diagonals[j] * scale, mid)
        if j + 1 < KRYLOV:
            high = jnp.where(row == j, couplings[j] * scale, high)
            low = jnp.where(row == j + 1, couplings[j] * scale, low)
    term = jnp.where(row == lane, 1.0, 0.0).astype(F32)
    real, imag = term, zero
    for order, ratio in enumerate(expanded_ratios(), 1):
        term = mid * term + low * pltpu.roll(term, 1, 0) + high * pltpu.roll(term, 7, 0)
        term = term * ratio
        signed = -term if order % 4 in (2, 3) else term
        if order % 2:
            imag = imag + signed
        else:
            real = real + signed
    for _ in range(squarings - EXPANDED):
        real, imag = (
            small_product(real, real) - small_product(imag, imag),
            2.0 * small_product(real, imag),
        )
    return real, imag


def mode_gains(weight, lam, own):
    rest = jnp.sqrt(weight)
    grown = jnp.ones((8, 128), F32)
    diagonals, couplings, polys = [], [], []
    for step in range(KRYLOV):
        spread = lam * rest
        square = whole_sum(rest * rest) + epsilon
        diagonal = whole_sum(spread * rest)
        if step:
            overlap = whole_sum(rest * vector)
        inverse = lax.rsqrt(square)
        coupling = square * inverse
        diagonal = diagonal * inverse * inverse
        if step:
            diagonal = diagonal - overlap
        diagonals.append(diagonal)
        couplings.append(coupling)
        poly = grown * inverse
        polys.append(poly)
        if step + 1 < KRYLOV:
            rest = rest * inverse
            image = spread * inverse
            grown = own * poly
            if step:
                image = image - coupling * vector
                grown = grown - coupling * before
            vector, before = rest, poly
            rest = image - diagonal * vector
            grown = grown - diagonal * before
    scale_zero = couplings[0]
    real, imag = krylov_exp(diagonals, couplings[1:])
    gains = []
    for part in (real, imag):
        gain = part[0:1, 0:1] * polys[0]
        for j in range(1, KRYLOV):
            gain = gain + part[j : j + 1, 0:1] * polys[j]
        gains.append(gain * scale_zero)
    return gains


def lanczos_kernel(side_ref, weight_ref, lam_ref, factor_ref):
    lane = lax.broadcasted_iota(jnp.int32, (NS, 128), 1)
    own = jnp.where(lane[0:8, :] < 64, side_ref[...], pltpu.roll(side_ref[...], 64, 1))
    weight = jnp.where(lane < 64, weight_ref[:, 0, :], 0.0)
    gain_re, gain_im = mode_gains(weight, lam_ref[...], own)
    row = lax.broadcasted_iota(jnp.int32, (8, 128), 0)
    factor_ref[...] = jnp.where(row == 0, gain_re, gain_im)


def propagate_kernel(factor_ref, modes_ref, mat_ref, out_ref, scaled):
    gain_re, gain_im = (
        jnp.broadcast_to(factor_ref[row : row + 1, :], (128, 128)).T[0:64, :]
        for row in range(2)
    )
    for c0 in range(0, NK, WIDE):
        for c in range(c0, c0 + WIDE):
            lanes = slice(c * 128, c * 128 + 128)
            a, b = modes_ref[0:64, lanes], modes_ref[64:128, lanes]
            scaled[0:64, lanes] = gain_re * a - gain_im * b
            scaled[64:128, lanes] = gain_im * a + gain_re * b
        lanes = slice(c0 * 128, (c0 + WIDE) * 128)
        back = mm_wide(mat_ref[...], scaled[:, lanes])
        out_ref[:, :, lanes] = back.reshape(NS, 8, WIDE * 128)


def kerr_kernel(
    modes_ref, in_ref, mat_ref, tw_ref, fwd_ref, bwd_ref,
    out_ref, field, delayed, one, two, done, sems
):
    kerr = modes_ref[128:129, 68:69]
    field[...] = mm_wide(mat_ref[...], in_ref[...].reshape(128, NT))

    copies = []
    for half in range(2):
        base = 16 * half
        mine, other = one.at[half], two.at[half]

        def load(side, r0, a):
            lanes = slice(a * NB, (a + 1) * NB)
            lo = 32 * side + base + r0
            re, im = field[lo : lo + 8, lanes], field[64 + lo : 64 + lo + 8, lanes]
            return re * re + im * im

        outer_forward(load, 16, tw_ref, mine)
        other[...] = mm_split(mine[...], fwd_ref)
        filter_spectrum(other, 16, tw_ref[3], tw_ref[4])
        mine[...] = mm_split(other[...], bwd_ref)

        def store(r0, a, re, im):
            lanes = slice(a * NB, (a + 1) * NB)
            delayed[base + r0 : base + r0 + 8, lanes] = re
            delayed[32 + base + r0 : 32 + base + r0 + 8, lanes] = im

        outer_backward(mine, 16, tw_ref, store)

        for side in range(2):
            first = 32 * side + base
            for r0 in (first, first + 8):
                re, im = field[r0 : r0 + 8, :], field[64 + r0 : 64 + r0 + 8, :]
                late = delayed[r0 : r0 + 8, :]
                rotation = kerr * ((1.0 - raman_share) * (re * re + im * im) + raman_share * late)
                c, s = turn(rotation)
                done[r0 : r0 + 8, :] = re * c - im * s
                done[64 + r0 : 64 + r0 + 8, :] = re * s + im * c
            for lo in (first, 64 + first):
                rows = pl.ds(lo, 16)
                copy = pltpu.make_async_copy(done.at[rows], out_ref.at[rows], sems.at[lo // 16])
                copy.start()
                copies.append(copy)
    for copy in copies:
        copy.wait()


VMEM = pl.BlockSpec(memory_space=pltpu.VMEM)
HBM = pl.BlockSpec(memory_space=pltpu.HBM)


def near(*shape):
    return pltpu.VMEM(shape, F32)


def hold(value):
    return pltpu.with_memory_space_constraint(value, pltpu.VMEM)


def cost(flops, moved):
    return pl.CostEstimate(flops=flops, bytes_accessed=moved, transcendentals=0)


def exchange(value):
    return lax.all_to_all(value, "shard", split_axis=0, concat_axis=0, tiled=True)


def pass_on(value):
    count = lax.axis_size("blk")
    return lax.ppermute(value, "blk", [(b, (b + 1) % count) for b in range(count)])


def per_device(seed_field, segment_order, seg_disp, seg_kerr, seg_gain, seg_sat):
    t = tables()
    near_tables = {name: hold(jnp.asarray(value)) for name, value in t.items()}
    seed = seed_field.reshape(128, NT)

    ymodes = pl.pallas_call(
        ymode_kernel,
        out_shape=near(NS, 65, 1, 128),
        in_specs=[VMEM] * 8,
        out_specs=VMEM,
        name="ymode",
    )(
        seed, t["to_ymode"], t["lam_all"], segment_order.reshape(1, 1),
        *(each.reshape(1, 32) for each in (seg_disp, seg_gain, seg_sat, seg_kerr)),
    )
    gathered = exchange(ymodes)
    modes, side, tile = pl.pallas_call(
        xmode_kernel,
        out_shape=(near(136, NT), near(8, 128), near(NS, 1, 128)),
        in_specs=[VMEM] * 2,
        out_specs=(VMEM,) * 3,
        name="xmode",
    )(hold(gathered), near_tables["to_xmode"])
    shifted = pass_on(modes)
    weights = exchange(tile)
    factor = pl.pallas_call(
        lanczos_kernel,
        out_shape=near(8, 128),
        in_specs=[VMEM] * 3,
        out_specs=VMEM,
        cost_estimate=cost(6 * 2 * 512 * 256 * 256, 2**20),
        name="lanczos",
    )(hold(side), hold(weights), near_tables["lam_all"])
    factor = pass_on(factor)
    dispersed = pl.pallas_call(
        disperse_kernel,
        out_shape=near(128, NT),
        in_specs=[VMEM] * 4,
        out_specs=VMEM,
        scratch_shapes=[pltpu.VMEM((512, 256), F32)] * 2,
        cost_estimate=cost(6 * 4 * 512 * 256 * 256, 2**20),
        name="disperse",
    )(hold(shifted), *(near_tables[name] for name in ("lines", "forward_split", "backward_split")))
    xback = pl.pallas_call(
        propagate_kernel,
        out_shape=near(NS, 8, NT),
        in_specs=[VMEM] * 3,
        out_specs=VMEM,
        scratch_shapes=[pltpu.VMEM((128, NT), F32)],
        name="propagate",
    )(hold(factor), hold(dispersed), near_tables["from_xmode"])
    rows = exchange(xback)
    result = pl.pallas_call(
        kerr_kernel,
        out_shape=jax.ShapeDtypeStruct((128, NT), F32),
        in_specs=[VMEM] * 6,
        out_specs=HBM,
        scratch_shapes=[pltpu.VMEM((128, NT), F32), pltpu.VMEM((64, NT), F32)]
        + [pltpu.VMEM((2, 128, 256), F32)] * 2
        + [pltpu.VMEM((128, NT), F32), pltpu.SemaphoreType.DMA((8,))],
        name="kerr",
    )(
        hold(shifted), hold(rows),
        *(
            near_tables[name]
            for name in ("from_ymode", "lines", "forward_split", "backward_split")
        ),
    )
    return result.reshape(seed_field.shape)


def solution(mesh):
    in_specs = (P("blk", None, "shard", None, None), P("blk"), P(), P(), P(), P())
    out_specs = P("blk", None, "shard", None, None)
    return jax.shard_map(
        per_device, mesh=mesh, in_specs=in_specs, out_specs=out_specs, check_vma=False
    )
```

```python
import functools
import math

import jax
import jax.numpy as jnp
import numpy as np
from jax import lax
from jax.experimental import pallas as pl
from jax.experimental.pallas import tpu as pltpu
from jax.sharding import PartitionSpec as P

KRYLOV = 8
EXPANDED = 6
NS = 16
NG = 32
NT = 1024
NK = 8
WIDE = 2
NB = 128

epsilon = 1e-06
step_length = 2.5
grin_depth = 1.5
squarings = 8
taylor_terms = 10
gain_width = 0.25
loss_rate = 0.5
disp_scale = 60.0
raman_share = 0.18
raman_freq = 0.05
raman_damp = 0.035

F32 = jnp.float32
HIGHEST = lax.Precision.HIGHEST


@functools.cache
def tables():
    cell = (np.arange(NG) - (NG - 1) / 2.0) / (NG / 2.0)
    line = np.diag(-grin_depth * cell * cell)
    line = line + 0.5 * (np.eye(NG, k=1) + np.eye(NG, k=-1))
    values, q = np.linalg.eigh(line)

    to_ymode = np.zeros((NS, 2, 2, 2, 2, 2, NG))
    to_xmode = np.zeros((2, 2, NG, NS, 2, 2, 2))
    for part in range(2):
        for side in range(2):
            for jj in range(2):
                to_ymode[:, part, jj, side, part, side, :] = q[:, jj::2].T
                to_xmode[part, jj, :, :, part, jj, side] = q[side::2, :].T
    to_ymode = to_ymode.reshape(128, 128)
    to_xmode = to_xmode.reshape(128, 128)

    pair = values.reshape(NS, 2)
    lam = pair[:, None, :, None] + values[None, None, None, :] + np.zeros((1, 2, 1, 1))
    lam_all = lam.reshape(NS, 128)

    inner = np.arange(NB)
    angle = 2.0 * np.pi * ((inner[:, None] * inner[None, :]) % NB) / NB
    c, s = np.cos(angle), np.sin(angle)
    forward = np.block([[c, -s], [s, c]])
    backward = np.block([[c, s], [-s, c]])
    turn = 2.0 * np.pi * (np.arange(NK)[:, None] * inner[None, :]) / NT
    tw_cos, tw_sin = np.cos(turn), np.sin(turn)

    freq = np.arange(NK)[:, None] + NK * inner[None, :]
    signed = np.where(freq >= NT // 2, freq - NT, freq)
    w = signed / (NT / 2.0)
    resonance = raman_freq * raman_freq
    raman = resonance / (resonance - w * w - 1j * raman_damp * w)
    ram_re = raman.real / NT
    ram_im = np.where(signed == -(NT // 2), 0.0, raman.imag) / NT

    f32 = lambda a: np.ascontiguousarray(a, dtype=np.float32)
    return dict(
        to_ymode=widen(f32(to_ymode)),
        from_ymode=widen(f32(to_ymode.T)),
        to_xmode=widen(f32(to_xmode)),
        from_xmode=widen(f32(to_xmode.T)),
        lam_all=f32(lam_all),
        forward_split=split(f32(forward)),
        backward_split=split(f32(backward)),
        forward=f32(forward),
        backward=f32(backward),
        lines=f32(np.stack([tw_cos, tw_sin, w, ram_re, ram_im])),
    )


def split(table):
    high = table.astype(jnp.bfloat16)
    return np.stack([high, (table - high.astype(np.float32)).astype(jnp.bfloat16)])


def parts_of(value):
    high = value.astype(jnp.bfloat16)
    rest = value - high.astype(F32)
    middle = rest.astype(jnp.bfloat16)
    low = (rest - middle.astype(F32)).astype(jnp.bfloat16)
    return high, middle, low


def widen(table):
    high = table.astype(jnp.bfloat16)
    rest = table - high.astype(np.float32)
    middle = rest.astype(jnp.bfloat16)
    low = (rest - middle.astype(np.float32)).astype(jnp.bfloat16)
    return np.concatenate([high, middle, high], axis=1)


def mm_wide(table, b):
    high, middle, low = parts_of(b)
    stacked = jnp.concatenate([high, high, middle], axis=0)
    return jnp.dot(table, stacked, preferred_element_type=F32)


def mm_split(a, b_ref):
    high = a.astype(jnp.bfloat16)
    low = (a - high.astype(F32)).astype(jnp.bfloat16)
    dot = functools.partial(jnp.dot, preferred_element_type=F32)
    return dot(high, b_ref[0]) + (dot(high, b_ref[1]) + dot(low, b_ref[0]))


def mm(a, b):
    return jnp.dot(a, b, precision=HIGHEST, preferred_element_type=F32)


def fourier8(re, im, sign):
    def four(r, i):
        pr, pi = r[0] + r[2], i[0] + i[2]
        mr, mi = r[0] - r[2], i[0] - i[2]
        qr, qi = r[1] + r[3], i[1] + i[3]
        nr, ni = r[1] - r[3], i[1] - i[3]
        tr, ti = (-ni, nr) if sign > 0 else (ni, -nr)
        return (
            [pr + qr, mr + tr, pr - qr, mr - tr],
            [pi + qi, mi + ti, pi - qi, mi - ti],
        )

    er, ei = four(re[0::2], im[0::2])
    orr, oi = four(re[1::2], im[1::2])
    h = np.float32(np.sqrt(0.5))
    if sign > 0:
        w1 = ((orr[1] - oi[1]) * h, (orr[1] + oi[1]) * h)
        w2 = (-oi[2], orr[2])
        w3 = (-(orr[3] + oi[3]) * h, (orr[3] - oi[3]) * h)
    else:
        w1 = ((orr[1] + oi[1]) * h, (oi[1] - orr[1]) * h)
        w2 = (oi[2], -orr[2])
        w3 = ((oi[3] - orr[3]) * h, -(orr[3] + oi[3]) * h)
    tr = [orr[0], w1[0], w2[0], w3[0]]
    ti = [oi[0], w1[1], w2[1], w3[1]]
    out_r = [er[k] + tr[k] for k in range(4)] + [er[k] - tr[k] for k in range(4)]
    out_i = [ei[k] + ti[k] for k in range(4)] + [ei[k] - ti[k] for k in range(4)]
    return out_r, out_i


def outer_forward(load, rows, tw_ref, dest):
    for r0 in range(0, rows, 8):
        re = [load(0, r0, a) for a in range(NK)]
        im = [load(1, r0, a) for a in range(NK)]
        re, im = fourier8(re, im, -1)
        for k in range(NK):
            if k:
                c, s = tw_ref[0, k : k + 1, :], tw_ref[1, k : k + 1, :]
                re[k], im[k] = re[k] * c + im[k] * s, im[k] * c - re[k] * s
            dest[k * rows + r0 : k * rows + r0 + 8, 0:NB] = re[k]
            dest[k * rows + r0 : k * rows + r0 + 8, NB : 2 * NB] = im[k]


def outer_backward(src, rows, tw_ref, store):
    for r0 in range(0, rows, 8):
        re, im = [], []
        for k in range(NK):
            a = src[k * rows + r0 : k * rows + r0 + 8, 0:NB]
            b = src[k * rows + r0 : k * rows + r0 + 8, NB : 2 * NB]
            if k:
                c, s = tw_ref[0, k : k + 1, :], tw_ref[1, k : k + 1, :]
                a, b = a * c - b * s, a * s + b * c
            re.append(a)
            im.append(b)
        re, im = fourier8(re, im, 1)
        for a in range(NK):
            store(r0, a, re[a], im[a])


def filter_spectrum(spec, rows, factor_re, factor_im):
    for k in range(NK):
        fr, fi = factor_re[k : k + 1, :], factor_im[k : k + 1, :]
        lo, hi = k * rows, (k + 1) * rows
        a, b = spec[lo:hi, 0:NB], spec[lo:hi, NB : 2 * NB]
        spec[lo:hi, 0:NB] = a * fr - b * fi
        spec[lo:hi, NB : 2 * NB] = a * fi + b * fr


def whole_sum(value):
    return jnp.sum(jnp.sum(value, axis=0, keepdims=True), axis=1, keepdims=True)


def ymode_kernel(
    upper_ref, lower_ref, mat_ref, lam_ref, kind_ref, disp_ref, gain_ref, sat_ref, kerr_ref, out_ref
):
    total = jnp.zeros((8, 128), F32)
    for c0 in range(0, NK, WIDE):
        lanes = slice(c0 * 128, (c0 + WIDE) * 128)
        block = jnp.concatenate([upper_ref[:, lanes], lower_ref[:, lanes]], axis=0)
        square = block * block
        modes = mm_wide(mat_ref[...], block)
        for c in range(WIDE):
            lanes = slice(c * 128, c * 128 + 128)
            for r in range(16):
                total = total + square[8 * r : 8 * r + 8, lanes]
            place = 8 * (c0 + c)
            for d in range(NS):
                out_ref[d, place : place + 8, 0, :] = modes[8 * d : 8 * d + 8, lanes]
    lane = lax.broadcasted_iota(jnp.int32, (NS, 128), 1)
    chosen = lax.broadcasted_iota(jnp.int32, (1, 32), 1) == kind_ref[...]
    side = jnp.where(lane < 64, lam_ref[...], whole_sum(total))
    for place, ref in ((65, disp_ref), (66, gain_ref), (67, sat_ref), (68, kerr_ref)):
        value = jnp.sum(jnp.where(chosen, ref[...], 0.0), axis=1, keepdims=True)
        side = jnp.where(lane == place, value, side)
    out_ref[:, 64, 0, :] = side


def xmode_kernel(in_ref, mat_ref, modes_ref, side_ref, tile_ref):
    square = jnp.zeros((128, 128), F32)
    for c0 in range(0, NK, WIDE):
        block = jnp.concatenate(
            [
                jnp.concatenate([in_ref[d, 8 * c : 8 * c + 8, 0, :] for d in range(NS)], axis=0)
                for c in range(c0, c0 + WIDE)
            ],
            axis=1,
        )
        modes = mm_wide(mat_ref[...], block)
        modes_ref[0:128, c0 * 128 : (c0 + WIDE) * 128] = modes
        for c in range(WIDE):
            square = square + modes[:, c * 128 : c * 128 + 128] ** 2
    both = square[0:64, :] + square[64:128, :]
    both = jnp.concatenate([both, both], axis=0)
    tile = jnp.sum(both.T, axis=0, keepdims=True)
    lane = lax.broadcasted_iota(jnp.int32, (1, 128), 1)
    sides = in_ref[:, 64, 0, :]
    side = jnp.where(lane == 64, jnp.sum(sides, axis=0, keepdims=True), sides[0:1, :])
    side_ref[...] = jnp.broadcast_to(side, (8, 128))
    modes_ref[128:136, 0:128] = jnp.broadcast_to(side, (8, 128))
    modes_ref[128:136, 128:NT] = jnp.zeros((8, NT - 128), F32)
    for d in range(NS):
        tile_ref[d] = tile


def turn(angle):
    count = jnp.floor(angle * np.float32(2.0 / np.pi) + 0.5)
    x = angle - count * 1.5703125
    x = x - count * 4.837512969970703e-4
    x = x - count * 7.549789948768648e-8
    x = jnp.clip(x, -0.8, 0.8)
    z = x * x
    sine = ((-1.9515295891e-4 * z + 8.3321608736e-3) * z - 1.6666654611e-1) * z * x + x
    cosine = ((2.443315711809948e-5 * z - 1.388731625493765e-3) * z + 4.166664568298827e-2) * z
    cosine = cosine * z - 0.5 * z + 1.0
    quarter = count.astype(jnp.int32)
    odd = (quarter & 1) == 1
    c, s = jnp.where(odd, sine, cosine), jnp.where(odd, cosine, sine)
    c = jnp.where(((quarter + 1) & 2) == 2, -c, c)
    s = jnp.where((quarter & 2) == 2, -s, s)
    return c, s


def disperse_kernel(
    modes_ref, tw_ref, fwd_ref, bwd_ref, out_ref, one, two
):

    def load(part, r0, a):
        return modes_ref[64 * part + r0 : 64 * part + r0 + 8, a * NB : (a + 1) * NB]

    outer_forward(load, 64, tw_ref, one)
    two[...] = mm_split(one[...], fwd_ref)

    energy = modes_ref[128:129, 64:65]
    dispersion, gain_peak = modes_ref[128:129, 65:66], modes_ref[128:129, 66:67]
    gain = gain_peak / (1.0 + energy / (NG * NG * NT) / modes_ref[128:129, 67:68])
    w = tw_ref[2]
    relative = w / gain_width
    amplitude = jnp.exp(0.5 * gain / (1.0 + relative * relative) - loss_rate) * (1.0 / NT)
    angle = disp_scale * dispersion * w * w
    filter_spectrum(two, 64, amplitude * jnp.cos(angle), amplitude * jnp.sin(angle))

    one[...] = mm_split(two[...], bwd_ref)

    def store(r0, a, re, im):
        out_ref[r0 : r0 + 8, a * NB : (a + 1) * NB] = re
        out_ref[64 + r0 : 64 + r0 + 8, a * NB : (a + 1) * NB] = im

    outer_backward(one, 64, tw_ref, store)


def small_product(a, b):
    total = a[:, 0:1] * b[0:1, :]
    for k in range(1, KRYLOV):
        total = total + a[:, k : k + 1] * b[k : k + 1, :]
    return total


def expanded_ratios():
    series = np.array([1.0 / math.factorial(k) for k in range(taylor_terms + 1)])
    series = series / 2.0 ** (EXPANDED * np.arange(taylor_terms + 1))
    for _ in range(EXPANDED):
        series = np.convolve(series, series)
    series = series[series >= np.finfo(np.float32).tiny]
    return [float(ratio) for ratio in series[1:] / series[:-1]]


def krylov_exp(diagonals, couplings):
    row = lax.broadcasted_iota(jnp.int32, (8, 128), 0)
    lane = lax.broadcasted_iota(jnp.int32, (8, 128), 1)
    zero = jnp.zeros((8, 128), F32)
    scale = step_length / 2.0 ** (squarings - EXPANDED)
    mid, low, high = zero, zero, zero
    for j in range(KRYLOV):
        mid = jnp.where(row == j, diagonals[j] * scale, mid)
        if j + 1 < KRYLOV:
            high = jnp.where(row == j, couplings[j] * scale, high)
            low = jnp.where(row == j + 1, couplings[j] * scale, low)
    term = jnp.where(row == lane, 1.0, 0.0).astype(F32)
    real, imag = term, zero
    for order, ratio in enumerate(expanded_ratios(), 1):
        term = mid * term + low * pltpu.roll(term, 1, 0) + high * pltpu.roll(term, 7, 0)
        term = term * ratio
        signed = -term if order % 4 in (2, 3) else term
        if order % 2:
            imag = imag + signed
        else:
            real = real + signed
    for _ in range(squarings - EXPANDED):
        real, imag = (
            small_product(real, real) - small_product(imag, imag),
            2.0 * small_product(real, imag),
        )
    return real, imag


def mode_gains(weight, lam, own):
    rest = jnp.sqrt(weight)
    grown = jnp.ones((8, 128), F32)
    diagonals, couplings, polys = [], [], []
    for step in range(KRYLOV):
        spread = lam * rest
        square = whole_sum(rest * rest) + epsilon
        diagonal = whole_sum(spread * rest)
        if step:
            overlap = whole_sum(rest * vector)
        inverse = lax.rsqrt(square)
        coupling = square * inverse
        diagonal = diagonal * inverse * inverse
        if step:
            diagonal = diagonal - overlap
        diagonals.append(diagonal)
        couplings.append(coupling)
        poly = grown * inverse
        polys.append(poly)
        if step + 1 < KRYLOV:
            rest = rest * inverse
            image = spread * inverse
            grown = own * poly
            if step:
                image = image - coupling * vector
                grown = grown - coupling * before
            vector, before = rest, poly
            rest = image - diagonal * vector
            grown = grown - diagonal * before
    scale_zero = couplings[0]
    real, imag = krylov_exp(diagonals, couplings[1:])
    gains = []
    for part in (real, imag):
        gain = part[0:1, 0:1] * polys[0]
        for j in range(1, KRYLOV):
            gain = gain + part[j : j + 1, 0:1] * polys[j]
        gains.append(gain * scale_zero)
    return gains


def lanczos_kernel(side_ref, weight_ref, lam_ref, factor_ref):
    lane = lax.broadcasted_iota(jnp.int32, (NS, 128), 1)
    own = jnp.where(lane[0:8, :] < 64, side_ref[...], pltpu.roll(side_ref[...], 64, 1))
    weight = jnp.where(lane < 64, weight_ref[:, 0, :], 0.0)
    gain_re, gain_im = mode_gains(weight, lam_ref[...], own)
    row = lax.broadcasted_iota(jnp.int32, (8, 128), 0)
    factor_ref[...] = jnp.where(row == 0, gain_re, gain_im)


def propagate_kernel(factor_ref, modes_ref, mat_ref, out_ref, scaled):
    gain_re, gain_im = (
        jnp.broadcast_to(factor_ref[row : row + 1, :], (128, 128)).T[0:64, :]
        for row in range(2)
    )
    for c0 in range(0, NK, WIDE):
        for c in range(c0, c0 + WIDE):
            lanes = slice(c * 128, c * 128 + 128)
            a, b = modes_ref[0:64, lanes], modes_ref[64:128, lanes]
            scaled[0:64, lanes] = gain_re * a - gain_im * b
            scaled[64:128, lanes] = gain_im * a + gain_re * b
        lanes = slice(c0 * 128, (c0 + WIDE) * 128)
        back = mm_wide(mat_ref[...], scaled[:, lanes])
        out_ref[:, :, lanes] = back.reshape(NS, 8, WIDE * 128)


def kerr_kernel(
    modes_ref, in_ref, mat_ref, tw_ref, fwd_ref, bwd_ref,
    out_ref, field, delayed, one, two, done, sems
):
    kerr = modes_ref[128:129, 68:69]
    field[...] = mm_wide(mat_ref[...], in_ref[...].reshape(128, NT))

    copies = []
    for half in range(2):
        base = 16 * half
        mine, other = one.at[half], two.at[half]

        def load(side, r0, a):
            lanes = slice(a * NB, (a + 1) * NB)
            lo = 32 * side + base + r0
            re, im = field[lo : lo + 8, lanes], field[64 + lo : 64 + lo + 8, lanes]
            return re * re + im * im

        outer_forward(load, 16, tw_ref, mine)
        other[...] = mm_split(mine[...], fwd_ref)
        filter_spectrum(other, 16, tw_ref[3], tw_ref[4])
        mine[...] = mm_split(other[...], bwd_ref)

        def store(r0, a, re, im):
            lanes = slice(a * NB, (a + 1) * NB)
            delayed[base + r0 : base + r0 + 8, lanes] = re
            delayed[32 + base + r0 : 32 + base + r0 + 8, lanes] = im

        outer_backward(mine, 16, tw_ref, store)

        for side in range(2):
            first = 32 * side + base
            for r0 in (first, first + 8):
                re, im = field[r0 : r0 + 8, :], field[64 + r0 : 64 + r0 + 8, :]
                late = delayed[r0 : r0 + 8, :]
                rotation = kerr * ((1.0 - raman_share) * (re * re + im * im) + raman_share * late)
                c, s = turn(rotation)
                done[r0 : r0 + 8, :] = re * c - im * s
                done[64 + r0 : 64 + r0 + 8, :] = re * s + im * c
            for lo in (first, 64 + first):
                rows = pl.ds(lo, 16)
                copy = pltpu.make_async_copy(done.at[rows], out_ref.at[rows], sems.at[lo // 16])
                copy.start()
                copies.append(copy)
    for copy in copies:
        copy.wait()


VMEM = pl.BlockSpec(memory_space=pltpu.VMEM)
HBM = pl.BlockSpec(memory_space=pltpu.HBM)


def near(*shape):
    return pltpu.VMEM(shape, F32)


def hold(value):
    return pltpu.with_memory_space_constraint(value, pltpu.VMEM)


def cost(flops, moved):
    return pl.CostEstimate(flops=flops, bytes_accessed=moved, transcendentals=0)


def exchange(value):
    return lax.all_to_all(value, "shard", split_axis=0, concat_axis=0, tiled=True)


def pass_on(value):
    count = lax.axis_size("blk")
    return lax.ppermute(value, "blk", [(b, (b + 1) % count) for b in range(count)])


def per_device(seed_field, segment_order, seg_disp, seg_kerr, seg_gain, seg_sat):
    t = tables()
    near_tables = {name: hold(jnp.asarray(value)) for name, value in t.items()}
    seed = seed_field.reshape(128, NT)

    ymodes = pl.pallas_call(
        ymode_kernel,
        out_shape=near(NS, 65, 1, 128),
        grid=(1,),
        in_specs=[pl.BlockSpec((64, NT), lambda i: (0, 0)), pl.BlockSpec((64, NT), lambda i: (1, 0))]
        + [VMEM] * 7,
        out_specs=VMEM,
        name="ymode",
    )(
        seed, seed, t["to_ymode"], t["lam_all"], segment_order.reshape(1, 1),
        *(each.reshape(1, 32) for each in (seg_disp, seg_gain, seg_sat, seg_kerr)),
    )
    gathered = exchange(ymodes)
    modes, side, tile = pl.pallas_call(
        xmode_kernel,
        out_shape=(near(136, NT), near(8, 128), near(NS, 1, 128)),
        in_specs=[VMEM] * 2,
        out_specs=(VMEM,) * 3,
        name="xmode",
    )(hold(gathered), near_tables["to_xmode"])
    shifted = pass_on(modes)
    weights = exchange(tile)
    factor = pl.pallas_call(
        lanczos_kernel,
        out_shape=near(8, 128),
        in_specs=[VMEM] * 3,
        out_specs=VMEM,
        cost_estimate=cost(6 * 2 * 512 * 256 * 256, 2**20),
        name="lanczos",
    )(hold(side), hold(weights), near_tables["lam_all"])
    factor = pass_on(factor)
    dispersed = pl.pallas_call(
        disperse_kernel,
        out_shape=near(128, NT),
        in_specs=[VMEM] * 4,
        out_specs=VMEM,
        scratch_shapes=[pltpu.VMEM((512, 256), F32)] * 2,
        cost_estimate=cost(6 * 4 * 512 * 256 * 256, 2**20),
        name="disperse",
    )(hold(shifted), *(near_tables[name] for name in ("lines", "forward_split", "backward_split")))
    xback = pl.pallas_call(
        propagate_kernel,
        out_shape=near(NS, 8, NT),
        in_specs=[VMEM] * 3,
        out_specs=VMEM,
        scratch_shapes=[pltpu.VMEM((128, NT), F32)],
        name="propagate",
    )(hold(factor), hold(dispersed), near_tables["from_xmode"])
    rows = exchange(xback)
    result = pl.pallas_call(
        kerr_kernel,
        out_shape=jax.ShapeDtypeStruct((128, NT), F32),
        in_specs=[VMEM] * 6,
        out_specs=HBM,
        scratch_shapes=[pltpu.VMEM((128, NT), F32), pltpu.VMEM((64, NT), F32)]
        + [pltpu.VMEM((2, 128, 256), F32)] * 2
        + [pltpu.VMEM((128, NT), F32), pltpu.SemaphoreType.DMA((8,))],
        name="kerr",
    )(
        hold(shifted), hold(rows),
        *(
            near_tables[name]
            for name in ("from_ymode", "lines", "forward_split", "backward_split")
        ),
    )
    return result.reshape(seed_field.shape)


def solution(mesh):
    in_specs = (P("blk", None, "shard", None, None), P("blk"), P(), P(), P(), P())
    out_specs = P("blk", None, "shard", None, None)
    return jax.shard_map(
        per_device, mesh=mesh, in_specs=in_specs, out_specs=out_specs, check_vma=False
    )
```
